32 devices in a mesh: gx: 4 (over z), gy: 4 (over y, x), gz: 2 (over core).
Axes of the slice: x: 2, y: 2, z: 4, core: 2. Of those that a mesh axis runs over, the one named last changes fastest.
Arguments:
- features: bfloat16 [8, 16, 2, 128, 256], P('gx', 'gy', 'gz'), may hold values from -6 to 6
- fractions: bfloat16 [8, 16, 2, 3, 128], P('gx', 'gy', 'gz'), may hold values from 0 to 0.98828125
- occupied: int32 [8, 16, 2, 128], P('gx', 'gy', 'gz'), may hold values 0 or 1
- wave_index: int32 [3, 512], replicated, may hold values from -14 to 14, as said below
- radial_weight: float32 [8, 4], replicated, may hold values from -4 to 4
- ewald_mix: float32 [256, 256], replicated, may hold values from -0.375 to 0.375
- msg_weight: bfloat16 [256, 256], replicated, may hold values from -0.375 to 0.375
- ewald_weight: bfloat16 [256, 256], replicated, may hold values from -0.375 to 0.375
- out_weight: bfloat16 [256, 256], replicated, may hold values from -0.375 to 0.375
Outputs:
- updated: bfloat16 [8, 16, 2, 128, 256], P('gx', 'gy', 'gz')
The draws below stay inside these ranges and needn't reach their ends.
Inputs may be any that keep to these rules, and one draw needn't show every extreme that they name: `wave_index`: no wavevector is zero, and no two wavevectors are equal or opposite.
All inputs are finite; a program needn't handle non-finite values. No bound on the sum of `occupied` on one device may be relied on, other than what follows from the above.
Results may differ from the reference program's by a relative error of at most 0.007.
Values may be sent and summed in bfloat16 or wider, within the bound.
A program may use at most 64 MiB of HBM per device.

```python
import math
import jax
import jax.numpy as jnp
from jax import lax

FEAT = 256
WAVES = 512
SLOTS = 128
HEADS = 4
BASIS = 8
NXC = 8
NYC = 16
NZC = 2
ATOMS = 32768


def draw_wave_index(key, part):
    reach_x = NXC // 2 + 6
    reach_y = NYC // 2 + 6
    reach_z = NZC // 2 + 6
    longest = max(NXC, NYC, NZC)
    factor_x = (longest // NXC) ** 2
    factor_y = (longest // NYC) ** 2
    factor_z = (longest // NZC) ** 2
    comp_x, comp_y, comp_z = jnp.meshgrid(jnp.arange(-reach_x, reach_x + 1, dtype=jnp.int32), jnp.arange(-reach_y, reach_y + 1, dtype=jnp.int32), jnp.arange(-reach_z, reach_z + 1, dtype=jnp.int32), indexing='ij')
    comp_x = comp_x.reshape(-1)
    comp_y = comp_y.reshape(-1)
    comp_z = comp_z.reshape(-1)
    upper = (comp_x > 0) | (comp_x == 0) & (comp_y > 0) | (comp_x == 0) & (comp_y == 0) & (comp_z > 0)
    norm_int = comp_x * comp_x * factor_x + comp_y * comp_y * factor_y + comp_z * comp_z * factor_z
    score = jnp.where(upper, norm_int, jnp.int32(2 ** 30))
    pool_count = score.shape[0]
    shuffled = jax.random.permutation(jax.random.fold_in(key, 31), pool_count).astype(jnp.int32)
    ranked = jnp.argsort(score[shuffled], stable=True)
    lowest = shuffled[ranked[:2 * WAVES]]
    picks = jax.random.permutation(jax.random.fold_in(key, 37), 2 * WAVES)[:WAVES]
    chosen = lowest[picks]
    signs = 2 * jax.random.randint(jax.random.fold_in(key, 41), (WAVES,), 0, 2) - 1
    values = jnp.stack([comp_x[chosen], comp_y[chosen], comp_z[chosen]], axis=0) * signs[None, :]
    return values.astype(jnp.int32)


def place_ends(entries, key, least, high):
    index_at = [jax.random.randint(jax.random.fold_in(key, axis), (), 0, length) for axis, length in enumerate(entries.shape)]
    widest = entries.shape.index(max(entries.shape))
    next_to = index_at[:widest] + [(index_at[widest] + 1) % entries.shape[widest]] + index_at[widest + 1:]
    return entries.at[tuple(index_at)].set(least).at[tuple(next_to)].set(high)


def steps_of(stream_key, shape, shards, least, high):
    loudness, own = 1.0, jax.random.fold_in(stream_key, 6)
    for position, blocks in shards:
        steps = jnp.exp(jax.random.uniform(jax.random.fold_in(own, position), (blocks,), jnp.float32, least / len(shards), high / len(shards)))
        loudness = loudness * jnp.repeat(steps, shape[position] // blocks).reshape([-1 if axis == position else 1 for axis in range(len(shape))])
    return loudness


def noise(rng, dims, scale, bound, cuts=(), kind=jnp.bfloat16):
    values = jax.random.normal(rng, dims, jnp.float32) * scale
    if len(cuts) > 0:
        values = steps_of(rng, dims, cuts, -0.22, 0.18) * values
    return jnp.clip(values, min=-bound, max=bound).astype(kind)


def setup_inputs(seed: int = 0) -> dict:
    key_of = jax.random.split(jax.random.key(seed), 10)
    return {
        "features": noise(key_of[0], (NXC, NYC, NZC, SLOTS, FEAT), 1.0, 6.0, ((0, 4), (1, 4), (2, 2))),
        "fractions": jnp.clip(0.98828125 * jax.random.uniform(key_of[1], (NXC, NYC, NZC, 3, SLOTS), jnp.float32) ** steps_of(key_of[1], (NXC, NYC, NZC, 3, SLOTS), ((0, 4), (1, 4), (2, 2)), -0.2, 0.2), 0.0, 0.98828125).astype(jnp.bfloat16),
        "occupied": place_ends((jax.random.randint(key_of[2], (NXC, NYC, NZC, SLOTS), 0, 8) < 7).astype(jnp.int32), jax.random.fold_in(key_of[2], 1), 0, 1),
        "wave_index": draw_wave_index(jax.random.fold_in(key_of[9], 71), 0),
        "radial_weight": noise(key_of[4], (BASIS, HEADS), 1.0, 4.0, (), jnp.float32),
        "ewald_mix": noise(key_of[5], (FEAT, FEAT), FEAT ** -0.5, 0.375, (), jnp.float32),
        "msg_weight": noise(key_of[6], (FEAT, FEAT), FEAT ** -0.5, 0.375),
        "ewald_weight": noise(key_of[7], (FEAT, FEAT), FEAT ** -0.5, 0.375),
        "out_weight": noise(key_of[8], (FEAT, FEAT), FEAT ** -0.5, 0.375),
    }


sharpness = 16.0
smearing = 0.04
screening = 4.0
strength = 24.0

def pair_weights(home_geom, near_geom, shift_vec, radial_weight, self_pair):
    slot_count = home_geom.shape[2]
    dist_sq = jnp.zeros((home_geom.shape[0], slot_count, slot_count), jnp.float32)
    for axis_id in range(3):
        axis_gap = near_geom[:, axis_id, None, :] + shift_vec[axis_id] - home_geom[:, axis_id, :, None]
        dist_sq = dist_sq + axis_gap * axis_gap
    distance = jnp.sqrt(dist_sq)
    envelope = jnp.square(jnp.maximum(1.0 - dist_sq, 0.0)) * near_geom[:, 3, None, :]
    envelope = envelope * (1.0 - self_pair * jnp.eye(slot_count, dtype=jnp.float32))
    level_count = radial_weight.shape[0]
    radial_sum = jnp.zeros((home_geom.shape[0], radial_weight.shape[1], slot_count, slot_count), jnp.float32)
    for level_id in range(level_count):
        radial_bump = jnp.exp(-sharpness * jnp.square(distance - level_id / (level_count - 1)))
        radial_sum = radial_sum + radial_bump[:, None] * radial_weight[level_id][None, :, None, None]
    return (radial_sum * envelope[:, None]).astype(jnp.bfloat16)

def reference(features, fractions, occupied, wave_index, radial_weight, ewald_mix, msg_weight, ewald_weight, out_weight):
    head_count = radial_weight.shape[1]
    head_width = FEAT // head_count
    plane_cells = NYC * NZC
    geometry = jnp.concatenate([fractions.astype(jnp.float32), occupied[:, :, :, None, :].astype(jnp.float32)], axis=3)
    padding = ((1, 1), (1, 1), (1, 1), (0, 0), (0, 0))
    wide_feat = jnp.pad(features, padding, mode='wrap')
    wide_geom = jnp.pad(geometry, padding, mode='wrap')
    msg_scale = 1.0 / math.sqrt(4.0 * SLOTS)
    planes = jnp.arange(NXC, dtype=jnp.int32)

    def neighbour_plane(plane_id):
        feat_slab = lax.dynamic_slice_in_dim(wide_feat, plane_id, 3, 0)
        geom_slab = lax.dynamic_slice_in_dim(wide_geom, plane_id, 3, 0)
        home_geom = lax.dynamic_index_in_dim(geometry, plane_id, 0, keepdims=False).reshape(plane_cells, 4, SLOTS)
        msg_sum = jnp.zeros((plane_cells, SLOTS, head_count, head_width), jnp.float32)
        for offset_id in range(27):
            step_x = offset_id // 9 - 1
            step_y = offset_id // 3 % 3 - 1
            step_z = offset_id % 3 - 1
            near_feat = feat_slab[step_x + 1, step_y + 1:step_y + 1 + NYC, step_z + 1:step_z + 1 + NZC]
            near_feat = near_feat.reshape(plane_cells, SLOTS, head_count, head_width)
            near_geom = geom_slab[step_x + 1, step_y + 1:step_y + 1 + NYC, step_z + 1:step_z + 1 + NZC]
            near_geom = near_geom.reshape(plane_cells, 4, SLOTS)
            shift_vec = jnp.array([step_x, step_y, step_z], jnp.float32)
            self_pair = 1.0 if offset_id == 13 else 0.0
            weights = pair_weights(home_geom, near_geom, shift_vec, radial_weight, self_pair)
            msg_sum = msg_sum + jnp.einsum('nhpq,nqhc->nphc', weights.astype(jnp.float32), near_feat.astype(jnp.float32))
        scaled = msg_sum.reshape(plane_cells, SLOTS, FEAT) * msg_scale
        return scaled.astype(jnp.bfloat16).reshape(NYC, NZC, SLOTS, FEAT)
    messages = lax.map(neighbour_plane, planes)
    lengths = jnp.array([NXC, NYC, NZC], jnp.float32)
    wave_vec = 2.0 * math.pi * wave_index.astype(jnp.float32) / lengths[:, None]
    wave_sq = lax.optimization_barrier(jnp.sum(wave_vec * wave_vec, axis=0))
    damping = strength * jnp.exp(-0.5 * smearing * wave_sq) / (wave_sq + screening) * (1.0 / math.sqrt(ATOMS * WAVES))
    y_cells = jnp.arange(NYC, dtype=jnp.int32).astype(jnp.float32)[:, None, None]
    z_cells = jnp.arange(NZC, dtype=jnp.int32).astype(jnp.float32)[None, :, None]

    def plane_basis(plane_id):
        slab = lax.dynamic_index_in_dim(fractions, plane_id, 0, keepdims=False).astype(jnp.float32)
        pos_x = plane_id.astype(jnp.float32) + slab[:, :, 0]
        pos_y = y_cells + slab[:, :, 1]
        pos_z = z_cells + slab[:, :, 2]
        phase_rows = pos_x[..., None] * wave_vec[0] + pos_y[..., None] * wave_vec[1] + pos_z[..., None] * wave_vec[2]
        phase_rows = phase_rows.reshape(plane_cells * SLOTS, WAVES)
        return jnp.concatenate([jnp.cos(phase_rows), jnp.sin(phase_rows)], axis=1).astype(jnp.bfloat16)

    def project(carry, plane_id):
        wave_basis = plane_basis(plane_id)
        plane_feat = lax.dynamic_index_in_dim(features, plane_id, 0, keepdims=False)
        plane_mask = lax.dynamic_index_in_dim(occupied, plane_id, 0, keepdims=False)
        masked = (plane_feat * plane_mask[..., None].astype(jnp.bfloat16)).reshape(plane_cells * SLOTS, FEAT)
        term = lax.dot_general(wave_basis, masked, (((0,), (0,)), ((), ())), preferred_element_type=jnp.float32)
        return (carry + term, None)
    structure, unused = lax.scan(project, jnp.zeros((2 * WAVES, FEAT), jnp.float32), planes)
    mixed_rows = jnp.dot(structure, ewald_mix, precision=lax.Precision.HIGHEST).reshape(2, WAVES, FEAT)
    filtered = (mixed_rows * damping[None, :, None]).astype(jnp.bfloat16).reshape(2 * WAVES, FEAT)

    def decode(plane_id):
        values = jnp.dot(plane_basis(plane_id), filtered, preferred_element_type=jnp.float32)
        return values.astype(jnp.bfloat16).reshape(NYC, NZC, SLOTS, FEAT)
    ewald_out = lax.map(decode, planes)
    msg_rows = messages.reshape(-1, FEAT)
    ewald_rows = ewald_out.reshape(-1, FEAT)
    joined = jnp.dot(msg_rows, msg_weight, preferred_element_type=jnp.float32) + jnp.dot(ewald_rows, ewald_weight, preferred_element_type=jnp.float32)
    hidden = jax.nn.silu(joined).astype(jnp.bfloat16)
    result = features.reshape(-1, FEAT).astype(jnp.float32) + jnp.dot(hidden, out_weight, preferred_element_type=jnp.float32)
    result = result * occupied.reshape(-1, 1).astype(jnp.float32)
    return result.astype(jnp.bfloat16).reshape(features.shape)
```

```python
import functools
import math

import jax
import jax.numpy as jnp
from jax import lax
from jax.experimental import pallas as pl
from jax.experimental.pallas import tpu as pltpu
from jax.sharding import PartitionSpec as P

sharpness = 16.0
smearing = 0.04
screening = 4.0
strength = 24.0

SIN_C = [(-1.0) ** k * math.pi ** (2 * k + 1) / math.factorial(2 * k + 1) for k in range(7)]
COS_C = [(-1.0) ** k * math.pi ** (2 * k) / math.factorial(2 * k) for k in range(7)]


def poly(z, coefs):
    acc = jnp.full_like(z, coefs[-1])
    for c in coefs[-2::-1]:
        acc = acc * z + c
    return acc


def shifted(x, axis, dim, width):
    count, length = lax.axis_size(axis), x.shape[dim]
    up = [(i, (i + 1) % count) for i in range(count)]
    down = [(j, i) for i, j in up]
    last = lax.slice_in_dim(x, length - width, length, axis=dim)
    first = lax.slice_in_dim(x, 0, width, axis=dim)
    return lax.ppermute(last, axis, up), lax.ppermute(first, axis, down)


def widen(x, axis, dim):
    before, after = shifted(x, axis, dim, 1)
    return jnp.concatenate([before, x, after], axis=dim)


def message_kernel(cells_y, cells_z, fold_z, levels, home_ref, feat_ref, geom_ref, wb_ref, out_ref, hb, phi, acc):
    cell = pl.program_id(0)
    x = cell // (cells_y * cells_z)
    y = (cell // cells_z) % cells_y
    z = cell % cells_z
    slots = out_ref.shape[1]
    feat = out_ref.shape[2]
    near_z = feat_ref.shape[3]
    chunk = 32
    for a in range(3):
        hb[a] = jnp.broadcast_to(home_ref[0, :, a : a + 1], (slots, slots))
    for ox in range(3):
        for oy in range(3):
            for oz in range(near_z):
                g = geom_ref[x + ox, z, y + oy, oz]
                nx = g[0:1] + (ox - 1.0)
                ny = g[1:2] + (oy - 1.0)
                if fold_z:
                    nz = g[2:3]
                else:
                    nz = g[2:3] + (oz - 1.0)
                col = (oy * near_z + oz) * slots
                center = ox == 1 and oy == 1 and oz == (0 if fold_z else 1)
                for p0 in range(0, slots, chunk):
                    dx = nx - hb[0, p0 : p0 + chunk]
                    dy = ny - hb[1, p0 : p0 + chunk]
                    dz = nz - hb[2, p0 : p0 + chunk]
                    if fold_z and oz == 1:
                        dz = 1.0 - jnp.abs(dz)
                    radial_terms(dx, dy, dz, levels, center, p0, phi.at[ox], col, slots)
        rows = feat_ref[x + ox, z, pl.ds(y, 3)].reshape(3 * near_z * slots, feat)
        part = jnp.dot(phi[ox], rows, preferred_element_type=jnp.float32)
        if ox == 0:
            acc[...] = part
        elif ox == 1:
            acc[...] += part
    total = jnp.zeros((slots, feat), jnp.float32)
    for b in range(levels):
        both = acc[b * slots : (b + 1) * slots] + part[b * slots : (b + 1) * slots]
        total = total + both * wb_ref[b : b + 1]
    out_ref[0] = total.astype(jnp.bfloat16)


def basis_kernel(pos_ref, wave_ref, feat_ref, basis_ref, struct_ref):
    cell = pl.program_id(0)
    waves = wave_ref.shape[0]
    pos = pos_ref[0]
    chunk = 64
    for w0 in range(0, waves, chunk):
        wv = wave_ref[w0 : w0 + chunk]
        turns = wv[:, 0:1] * pos[0:1] + wv[:, 1:2] * pos[1:2] + wv[:, 2:3] * pos[2:3]
        u = turns - jnp.floor(turns + 0.5)
        q = u * u
        s = u * poly(q, SIN_C)
        c = poly(q, COS_C)
        basis_ref[0, w0 : w0 + chunk] = (1.0 - 2.0 * s * s).astype(jnp.bfloat16)
        basis_ref[0, waves + w0 : waves + w0 + chunk] = (2.0 * s * c).astype(jnp.bfloat16)
    part = jnp.dot(basis_ref[0], feat_ref[0], preferred_element_type=jnp.float32)

    @pl.when(cell == 0)
    def _():
        struct_ref[...] = part

    @pl.when(cell > 0)
    def _():
        struct_ref[...] += part


def final_kernel(basis_ref, grid_ref, msg_ref, feat_ref, home_ref, wm_ref, wo_ref, out_ref):
    far = lax.dot_general(
        basis_ref[0], grid_ref[...], (((0,), (0,)), ((), ())), preferred_element_type=jnp.float32
    )
    joined = far + jnp.dot(msg_ref[0], wm_ref[...], preferred_element_type=jnp.float32)
    hidden = (joined / (1.0 + jnp.exp(-joined))).astype(jnp.bfloat16)
    result = feat_ref[0].astype(jnp.float32) + jnp.dot(hidden, wo_ref[...], preferred_element_type=jnp.float32)
    out_ref[0] = (result * home_ref[0, :, 3:4]).astype(jnp.bfloat16)


def coords(index, counts):
    return (index // (counts[1] * counts[2]), (index // counts[2]) % counts[1], index % counts[2])


def layer_kernel(
    counts,
    levels,
    feat_ref,
    frac_ref,
    occ_ref,
    index_ref,
    radial_ref,
    mix_ref,
    we_ref,
    wm_ref,
    wo_ref,
    out_ref,
    wide,
    rows_sc,
    out_mask,
    turn_cols,
    wb,
    hb,
    phi,
    msg,
    basis,
    struct,
    pair,
    chip_sum,
    parts,
    share,
    field,
    halo_send,
    halo_recv,
    side_send,
    side_recv,
    pair_send,
    pair_recv,
    part_send,
    part_recv,
    share_send,
    share_recv,
):
    cx, cy, slots, feat = feat_ref.shape
    cells = cx * cy
    waves = index_ref.shape[1]
    heads = radial_ref.shape[0]
    devices = counts[0] * counts[1] * counts[2]
    grid = (counts[0] * cx, counts[1] * cy, counts[2])
    rows = waves // devices
    at = (lax.axis_index("gx"), lax.axis_index("gy"), lax.axis_index("gz"))
    chips = counts[0] * counts[1]
    chip = at[0] * counts[1] + at[1]
    core = at[2]
    mesh_id = pl.DeviceIdType.MESH
    pad = wide.shape[3] - slots

    partner = (at[0], at[1], 1 - core)

    def same_core(k):
        peer = (chip + k) % chips
        return (peer // counts[1], peer % counts[1], core)

    def to_partner(src, dst, send, recv):
        return pltpu.make_async_remote_copy(
            src_ref=src, dst_ref=dst, send_sem=send, recv_sem=recv, device_id=partner, device_id_type=mesh_id
        )

    barrier = pltpu.get_barrier_semaphore()

    @pl.loop(1, chips)
    def _(k):
        pl.semaphore_signal(barrier, inc=1, device_id=same_core(k), device_id_type=mesh_id)

    pl.semaphore_signal(barrier, inc=1, device_id=partner, device_id_type=mesh_id)

    rows_sc[...] = jnp.zeros_like(rows_sc)
    for x in range(cx):
        for a in range(3):
            k = (x * 3 + a) * cy
            rows_sc[k : k + cy] = frac_ref[x, a].astype(jnp.float32)
    rows_sc[3 * cells : 4 * cells] = occ_ref[...].astype(jnp.float32)
    turned = rows_sc[...].T
    for x in range(cx):
        for y in range(cy):
            cell = x * cy + y
            ks = [(x * 3 + a) * cy + y for a in range(3)]
            there = jnp.broadcast_to(turned[:, 3 * cells + cell : 3 * cells + cell + 1], (slots, feat))
            wide[1 + x, 1 + y, 0, 0:slots] = feat_ref[x, y] * there.astype(jnp.bfloat16)
            own = jnp.concatenate([rows_sc[k : k + 1] for k in ks] + [jnp.zeros((pad - 3, slots), jnp.float32)])
            own = jnp.concatenate([own, jnp.zeros((pad, feat - slots), jnp.float32)], axis=1)
            wide[1 + x, 1 + y, 0, slots:] = own.astype(jnp.bfloat16)

    pl.semaphore_wait(barrier, chips)

    def span(step, length):
        if step == 0:
            return 1, 1, length
        if step == 1:
            return length, 0, 1
        return 1, length + 1, 1

    halo, side = {}, {}
    for n, (dx, dy) in enumerate([(0, 1), (0, -1), (1, 0), (-1, 0), (1, 1), (1, -1), (-1, 1), (-1, -1), (0, 0)]):
        sx, tx, lx = span(dx, cx)
        sy, ty, ly = span(dy, cy)
        region = (pl.ds(tx, lx), pl.ds(ty, ly))
        side[dx, dy] = to_partner(wide.at[(*region, 0)], wide.at[(*region, 1)], side_send.at[n], side_recv.at[n])
        if (dx, dy) == (0, 0):
            continue
        target = ((at[0] + dx + counts[0]) % counts[0], (at[1] + dy + counts[1]) % counts[1], core)
        halo[dx, dy] = pltpu.make_async_remote_copy(
            src_ref=wide.at[pl.ds(sx, lx), pl.ds(sy, ly), 0],
            dst_ref=wide.at[(*region, 0)],
            send_sem=halo_send.at[n],
            recv_sem=halo_recv.at[n],
            device_id=target,
            device_id_type=mesh_id,
        )
    side[0, 0].start()
    for copy in halo.values():
        copy.start()

    for x in range(cx):
        for y in range(cy):
            for a in range(3):
                k = (x * 3 + a) * cy + y
                hb[x * cy + y, a] = jnp.broadcast_to(turned[:, k : k + 1], (slots, slots))
            k = 3 * cells + x * cy + y
            out_mask[x * cy + y] = jnp.broadcast_to(turned[:, k : k + 1], (slots, feat))
    for w0 in range(0, waves, 128):
        part = [index_ref[a : a + 1, w0 : w0 + 128].astype(jnp.float32) * (1.0 / grid[a]) for a in range(3)]
        part = jnp.concatenate(part + [jnp.zeros((5, 128), jnp.float32)])
        turn_cols[w0 : w0 + 128] = part.T
    owner = lax.broadcasted_iota(jnp.int32, (heads, feat), 1) // (feat // heads)
    mine = owner == lax.broadcasted_iota(jnp.int32, (heads, feat), 0)
    for b in range(levels):
        level = b / (levels - 1)
        scale = math.exp(-sharpness * level * level) / math.sqrt(4.0 * slots)
        column = jnp.broadcast_to(radial_ref[:, b : b + 1], (heads, feat)) * scale
        wb[b : b + 1] = jnp.sum(jnp.where(mine, column, 0.0), axis=0, keepdims=True)

    @pl.loop(0, cells)
    def _(cell):
        x = cell // cy
        y = cell % cy
        first = (x * 3) * cy + y
        start = [(at[0] * cx + x).astype(jnp.float32), (at[1] * cy + y).astype(jnp.float32), core.astype(jnp.float32)]
        pos = [rows_sc[pl.ds(first + a * cy, 1)] + start[a] for a in range(3)]
        lanes = pl.ds(pl.multiple_of(cell * slots, slots), slots)
        chunk = 64
        for w0 in range(0, waves, chunk):
            wv = turn_cols[w0 : w0 + chunk]
            turns = wv[:, 0:1] * pos[0] + wv[:, 1:2] * pos[1] + wv[:, 2:3] * pos[2]
            u = turns - jnp.floor(turns + 0.5)
            q = u * u
            s = u * poly(q, SIN_C)
            c = poly(q, COS_C)
            basis[w0 : w0 + chunk, lanes] = (1.0 - 2.0 * s * s).astype(jnp.bfloat16)
            basis[waves + w0 : waves + w0 + chunk, lanes] = (2.0 * s * c).astype(jnp.bfloat16)

    atoms = wide[1 : 1 + cx, 1 : 1 + cy, 0, 0:slots].reshape(cells * slots, feat)
    struct[...] = (
        jnp.dot(basis[...], atoms, preferred_element_type=jnp.float32)
        .astype(jnp.bfloat16)
        .reshape(2, chips, 2, rows, feat)
    )
    swap = to_partner(struct.at[:, :, 1 - core], pair, pair_send.at[0], pair_recv.at[0])
    swap.start()
    msg[...] = jnp.zeros_like(msg)

    def part_copy(k):
        return pltpu.make_async_remote_copy(
            src_ref=chip_sum.at[:, (chip + k) % chips],
            dst_ref=parts.at[k],
            send_sem=part_send.at[k],
            recv_sem=part_recv.at[k],
            device_id=same_core(k),
            device_id_type=mesh_id,
        )

    def share_copy(k, slot):
        return pltpu.make_async_remote_copy(
            src_ref=share,
            dst_ref=field.at[:, slot, core],
            send_sem=share_send.at[k],
            recv_sem=share_recv.at[k],
            device_id=same_core(k),
            device_id_type=mesh_id,
        )

    def field_copy(half):
        mine = field.at[:, :, half]
        return to_partner(mine, mine, pair_send.at[1], pair_recv.at[1])

    def sum_pair():
        swap.wait()
        both = struct[:, :, core].astype(jnp.float32) + pair[...].astype(jnp.float32)
        chip_sum[...] = both.astype(jnp.bfloat16)

        @pl.loop(1, chips)
        def _(k):
            part_copy(k).start()

    def filter_share():
        @pl.loop(1, chips)
        def _(k):
            part_copy(k).wait()

        parts[0] = chip_sum[:, chip]
        total = jnp.sum(parts[...].astype(jnp.float32), axis=0).reshape(2 * rows, feat)
        mixed = jnp.dot(total, mix_ref[...], precision=lax.Precision.HIGHEST, preferred_element_type=jnp.float32)
        vec = turn_cols[pl.ds((chip * 2 + core) * rows, rows)] * (2.0 * math.pi)
        square = jnp.sum(vec * vec, axis=1, keepdims=True)
        damp = strength * jnp.exp(-0.5 * smearing * square) / (square + screening)
        damp = damp * (1.0 / math.sqrt(cells * slots * devices * waves))
        filtered = (mixed * jnp.concatenate([damp, damp])).astype(jnp.bfloat16)
        projected = jnp.dot(filtered, we_ref[...], preferred_element_type=jnp.float32)
        projected = projected.astype(jnp.bfloat16).reshape(2, rows, feat)
        share[...] = projected
        field[:, chip, core] = projected

        @pl.loop(1, chips)
        def _(k):
            share_copy(k, chip).start()

    def join_field():
        @pl.loop(1, chips)
        def _(k):
            share_copy(k, (chip - k + chips) % chips).wait()

        field_copy(core).start()

    def place(x, j):
        late = j // (2 * cy)
        xi = (1 - late) * (1 + j % 2) + late * (x * (cx + 1))
        y = ((1 - late) * (j // 2) + late * (j - 2 * cy) + 1) % cy
        return xi, y

    def weigh(x, j):
        xi, y = place(x, j)
        cell = x * cy + y
        step = xi - (x + 1)
        chunk = 32
        for oy in range(3):
            for oz in range(2):
                g = wide[xi, y + oy, oz, slots : slots + pad, 0:slots].astype(jnp.float32)
                nx = g[0:1] + step.astype(jnp.float32)
                ny = g[1:2] + (oy - 1.0)
                nz = g[2:3]
                col = oy * 2 + oz
                for p0 in range(0, slots, chunk):
                    gx = nx - hb[cell, 0, p0 : p0 + chunk]
                    gy = ny - hb[cell, 1, p0 : p0 + chunk]
                    gz = nz - hb[cell, 2, p0 : p0 + chunk]
                    if oz == 1:
                        gz = 1.0 - jnp.abs(gz)
                    diagonal = p0 + step * slots if (oy, oz) == (1, 0) else None
                    radial_chain(gx, gy, gz, levels, diagonal, p0, phi.at[x, col], slots)

    def gather(x, j):
        xi, y = place(x, j)
        cell = x * cy + y
        near = wide[xi, pl.ds(y, 3), :, 0:slots].reshape(6 * slots, feat)
        left = jnp.concatenate([phi[x, col] for col in range(6)], axis=1)
        part = jnp.dot(left, near, preferred_element_type=jnp.float32)
        total = msg[cell]
        for b in range(levels):
            total = total + part[b * slots : (b + 1) * slots] * wb[b : b + 1]
        msg[cell] = total

    def halo_in(keys):
        for key in keys:
            halo[key].wait()
            side[key].start()

    def side_in(keys):
        for key in keys:
            side[key].wait()

    side_in([(0, 0)])
    weigh(0, jnp.int32(0))

    ends = 2 * cy - 4
    events = [
        (0, sum_pair),
        (ends - 2, lambda: halo_in([(0, -1)])),
        (ends - 1, lambda: side_in([(0, -1)])),
        (ends, lambda: halo_in([(0, 1)])),
        (ends + 1, lambda: side_in([(0, 1)])),
        (ends + 2, lambda: halo_in([(1, 0), (-1, 0)])),
        (ends + 2, filter_share),
        (ends + 3, lambda: side_in([(1, 0), (-1, 0)])),
        (3 * cy - 4, lambda: halo_in([(1, -1), (-1, -1)])),
        (3 * cy - 3, lambda: side_in([(1, -1), (-1, -1)])),
        (3 * cy - 3, lambda: halo_in([(1, 1), (-1, 1)])),
        (3 * cy - 2, lambda: side_in([(1, 1), (-1, 1)])),
        (3 * cy - 1, join_field),
    ]

    @pl.loop(0, 3 * cy)
    def _(j):
        for when, what in events:
            pl.when(j == when)(what)
        weigh(1, j)
        gather(0, j)
        weigh(0, j + 1)
        gather(1, j)

    field_copy(core).wait_send()
    field_copy(1 - core).wait_recv()

    waves_field = field[...].reshape(2 * waves, feat)

    @pl.loop(0, cells)
    def _(cell):
        lanes = pl.ds(pl.multiple_of(cell * slots, slots), slots)
        far = lax.dot_general(
            basis[:, lanes], waves_field, (((0,), (0,)), ((), ())), preferred_element_type=jnp.float32
        )
        near = msg[cell].astype(jnp.bfloat16)
        joined = far + jnp.dot(near, wm_ref[...], preferred_element_type=jnp.float32)
        hidden = (joined / (1.0 + jnp.exp(-joined))).astype(jnp.bfloat16)
        atom = wide[1 + cell // cy, 1 + cell % cy, 0, 0:slots].astype(jnp.float32)
        result = jnp.dot(hidden, wo_ref[...], preferred_element_type=jnp.float32)
        there = out_mask[cell]
        out_ref[cell] = (atom + result * there).astype(jnp.bfloat16)


def radial_chain(gx, gy, gz, levels, diagonal, p0, phi, slots):
    rows = gx.shape[0]
    sq = jnp.minimum(gx * gx + gy * gy + gz * gz, 1.0)
    dist = sq * lax.rsqrt(jnp.maximum(sq, 1e-30))
    ratio = jnp.exp2(dist * (2.0 * sharpness / (levels - 1) * math.log2(math.e)))
    edge = 1.0 - sq
    val = edge * edge * jnp.exp2(sq * (-sharpness * math.log2(math.e)))
    if diagonal is not None:
        row = lax.broadcasted_iota(jnp.int32, val.shape, 0) + diagonal
        lane = lax.broadcasted_iota(jnp.int32, val.shape, 1)
        val = jnp.where(row == lane, 0.0, val)
    second = ratio * ratio
    steps = [val.astype(jnp.bfloat16), (val * ratio).astype(jnp.bfloat16)]
    fourth = (second * second).astype(jnp.bfloat16)
    second = second.astype(jnp.bfloat16)
    for b in range(2, levels):
        steps.append(steps[b - 2] * second if b < 4 else steps[b - 4] * fourth)
    for b in range(levels):
        phi[b * slots + p0 : b * slots + p0 + rows] = steps[b]


def radial_terms(gx, gy, gz, levels, center, p0, phi, col, slots):
    rows = gx.shape[0]
    sq = jnp.minimum(gx * gx + gy * gy + gz * gz, 1.0)
    dist = sq * lax.rsqrt(jnp.maximum(sq, 1e-30))
    ratio = jnp.exp2(dist * (2.0 * sharpness / (levels - 1) * math.log2(math.e)))
    edge = 1.0 - sq
    val = edge * edge * jnp.exp2(sq * (-sharpness * math.log2(math.e)))
    if center:
        row = lax.broadcasted_iota(jnp.int32, val.shape, 0) + p0
        lane = lax.broadcasted_iota(jnp.int32, val.shape, 1)
        val = jnp.where(row == lane, 0.0, val)
    for b in range(levels):
        phi[b * slots + p0 : b * slots + p0 + rows, col : col + slots] = val.astype(jnp.bfloat16)
        if b + 1 < levels:
            val = val * ratio


def body(
    features,
    fractions,
    occupied,
    wave_index,
    radial_weight,
    ewald_mix,
    msg_weight,
    ewald_weight,
    out_weight,
):
    cx, cy, cz, slots, feat = features.shape
    levels, heads = radial_weight.shape
    cells = cx * cy * cz
    grid = [lax.axis_size("gx") * cx, lax.axis_size("gy") * cy, lax.axis_size("gz") * cz]
    devices = lax.axis_size("gx") * lax.axis_size("gy") * lax.axis_size("gz")
    waves = wave_index.shape[1]
    axes = ("gx", "gy", "gz")
    full = lambda shape: pl.BlockSpec(shape, lambda i: (0,) * len(shape))
    params = pltpu.CompilerParams(dimension_semantics=("arbitrary",), vmem_limit_bytes=56 * 2**20)

    fold_z = grid[2] == 2 and cz == 1
    counts = tuple(lax.axis_size(n) for n in axes)
    rows = waves // devices
    chips = counts[0] * counts[1]
    if fold_z and rows % 16 == 0 and min(counts) > 1 and cx == 2 and cy > 2 and 4 * cells <= slots == 128:
        vmem = pl.BlockSpec(memory_space=pltpu.VMEM)
        dma = pltpu.SemaphoreType.DMA
        out = pl.pallas_call(
            functools.partial(layer_kernel, counts, levels),
            in_specs=[vmem] * 9,
            out_specs=vmem,
            out_shape=jax.ShapeDtypeStruct((cells, slots, feat), jnp.bfloat16),
            scratch_shapes=[
                pltpu.VMEM((cx + 2, cy + 2, 2, slots + 8, feat), jnp.bfloat16),
                pltpu.VMEM((slots, slots), jnp.float32),
                pltpu.VMEM((cells, slots, feat), jnp.float32),
                pltpu.VMEM((waves, 8), jnp.float32),
                pltpu.VMEM((levels, feat), jnp.float32),
                pltpu.VMEM((cells, 3, slots, slots), jnp.float32),
                pltpu.VMEM((2, 6, levels * slots, slots), jnp.bfloat16),
                pltpu.VMEM((cells, slots, feat), jnp.float32),
                pltpu.VMEM((2 * waves, cells * slots), jnp.bfloat16),
                pltpu.VMEM((2, chips, 2, rows, feat), jnp.bfloat16),
                pltpu.VMEM((2, chips, rows, feat), jnp.bfloat16),
                pltpu.VMEM((2, chips, rows, feat), jnp.bfloat16),
                pltpu.VMEM((chips, 2, rows, feat), jnp.bfloat16),
                pltpu.VMEM((2, rows, feat), jnp.bfloat16),
                pltpu.VMEM((2, chips, 2, rows, feat), jnp.bfloat16),
                dma((8,)),
                dma((8,)),
                dma((9,)),
                dma((9,)),
                dma((2,)),
                dma((2,)),
                dma((chips,)),
                dma((chips,)),
                dma((chips,)),
                dma((chips,)),
            ],
            compiler_params=pltpu.CompilerParams(
                collective_id=0, has_side_effects=True, vmem_limit_bytes=56 * 2**20
            ),
            name="layer",
        )(
            features.reshape(cx, cy, slots, feat),
            fractions.transpose(0, 2, 3, 1, 4).reshape(cx, 3, cy, slots),
            occupied.reshape(cells, slots),
            wave_index,
            radial_weight.T,
            ewald_mix,
            ewald_weight,
            msg_weight,
            out_weight,
        )
        return out.reshape(features.shape)

    masked = features * occupied[..., None].astype(jnp.bfloat16)
    frac = fractions.astype(jnp.float32)
    cell_feat = masked.reshape(cells, slots, feat)
    home = jnp.concatenate([frac, occupied[:, :, :, None, :].astype(jnp.float32)], axis=3)
    home = jnp.swapaxes(home.reshape(cells, 4, slots), 1, 2)

    start = [
        (lax.axis_index(n) * c + jnp.arange(c, dtype=jnp.int32)).astype(jnp.float32)
        for n, c in zip(axes, (cx, cy, cz))
    ]
    origin = jnp.stack(jnp.meshgrid(*start, indexing="ij"), axis=-1)[..., None]
    pos = (origin + frac).reshape(cells, 3, slots)
    lengths = jnp.array(grid, jnp.float32)
    index = wave_index.astype(jnp.float32)
    wave_vec = 2.0 * math.pi * index / lengths[:, None]
    wave_sq = jnp.sum(wave_vec * wave_vec, axis=0)
    damping = (
        strength
        * jnp.exp(-0.5 * smearing * wave_sq)
        / (wave_sq + screening)
        * (1.0 / math.sqrt(cells * slots * devices * waves))
    )
    wave_turn = (index / lengths[:, None]).T

    level = jnp.arange(levels, dtype=jnp.float32) / (levels - 1)
    wb = radial_weight * (jnp.exp(-sharpness * level * level) / math.sqrt(4.0 * slots))[:, None]
    wb = jnp.repeat(wb, feat // heads, axis=1)
    basis, struct = pl.pallas_call(
        basis_kernel,
        grid=(cells,),
        in_specs=[
            pl.BlockSpec((1, 3, slots), lambda i: (i, 0, 0)),
            full((waves, 3)),
            pl.BlockSpec((1, slots, feat), lambda i: (i, 0, 0)),
        ],
        out_specs=[pl.BlockSpec((1, 2 * waves, slots), lambda i: (i, 0, 0)), full((2 * waves, feat))],
        out_shape=[
            jax.ShapeDtypeStruct((cells, 2 * waves, slots), jnp.bfloat16),
            jax.ShapeDtypeStruct((2 * waves, feat), jnp.float32),
        ],
        compiler_params=params,
        name="basis",
    )(pos, wave_turn, cell_feat)

    wave_share = lax.psum_scatter(struct.reshape(2, waves, feat), axes, scatter_dimension=1, tiled=True)
    share_rows = wave_share.shape[1]
    share_damp = lax.dynamic_slice_in_dim(damping, lax.axis_index(axes) * share_rows, share_rows, 0)
    mixed = jnp.dot(wave_share.reshape(2 * share_rows, feat), ewald_mix, precision=lax.Precision.HIGHEST)
    filtered = (mixed.reshape(2, share_rows, feat) * share_damp[None, :, None]).astype(jnp.bfloat16)
    projected = jnp.dot(filtered, ewald_weight, preferred_element_type=jnp.float32).astype(jnp.bfloat16)
    field = lax.all_gather(projected, axes, axis=1, tiled=True).reshape(2 * waves, feat)

    wide_feat = widen(widen(masked, "gx", 0), "gy", 1)
    wide_geom = widen(widen(fractions, "gx", 0), "gy", 1)
    if fold_z:
        swap = [(0, 1), (1, 0)]
        wide_feat = jnp.concatenate([wide_feat, lax.ppermute(wide_feat, "gz", swap)], axis=2)
        wide_geom = jnp.concatenate([wide_geom, lax.ppermute(wide_geom, "gz", swap)], axis=2)
        near_z = 2
    else:
        wide_feat = widen(wide_feat, "gz", 2)
        wide_geom = widen(wide_geom, "gz", 2)
        near_z = 3
    wide_feat = jnp.stack([wide_feat[:, :, z : z + near_z] for z in range(cz)], axis=1)
    wide_geom = jnp.stack([wide_geom[:, :, z : z + near_z] for z in range(cz)], axis=1).astype(jnp.float32)
    messages = pl.pallas_call(
        functools.partial(message_kernel, cy, cz, fold_z, levels),
        grid=(cells,),
        in_specs=[
            pl.BlockSpec((1, slots, 4), lambda i: (i, 0, 0)),
            full(wide_feat.shape),
            full(wide_geom.shape),
            full(wb.shape),
        ],
        out_specs=pl.BlockSpec((1, slots, feat), lambda i: (i, 0, 0)),
        out_shape=jax.ShapeDtypeStruct((cells, slots, feat), jnp.bfloat16),
        scratch_shapes=[
            pltpu.VMEM((3, slots, slots), jnp.float32),
            pltpu.VMEM((3, levels * slots, 3 * near_z * slots), jnp.bfloat16),
            pltpu.VMEM((levels * slots, feat), jnp.float32),
        ],
        compiler_params=params,
        cost_estimate=pl.CostEstimate(
            flops=2 * cells * levels * slots * 9 * near_z * slots * feat, bytes_accessed=2**22, transcendentals=0
        ),
        name="messages",
    )(home, wide_feat, wide_geom, wb)

    out = pl.pallas_call(
        final_kernel,
        grid=(cells,),
        in_specs=[
            pl.BlockSpec((1, 2 * waves, slots), lambda i: (i, 0, 0)),
            full((2 * waves, feat)),
            pl.BlockSpec((1, slots, feat), lambda i: (i, 0, 0)),
            pl.BlockSpec((1, slots, feat), lambda i: (i, 0, 0)),
            pl.BlockSpec((1, slots, 4), lambda i: (i, 0, 0)),
            full((feat, feat)),
            full((feat, feat)),
        ],
        out_specs=pl.BlockSpec((1, slots, feat), lambda i: (i, 0, 0)),
        out_shape=jax.ShapeDtypeStruct((cells, slots, feat), jnp.bfloat16),
        compiler_params=params,
        name="final",
    )(basis, field, messages, cell_feat, home, msg_weight, out_weight)
    return out.reshape(features.shape)


def solution(mesh):
    cell = P("gx", "gy", "gz", None, None)
    in_specs = (cell, cell, P("gx", "gy", "gz", None), P(), P(), P(), P(), P(), P())
    return jax.shard_map(body, mesh=mesh, in_specs=in_specs, out_specs=cell, check_vma=False)
```

```python
import functools
import math

import jax
import jax.numpy as jnp
from jax import lax
from jax.experimental import pallas as pl
from jax.experimental.pallas import tpu as pltpu
from jax.sharding import PartitionSpec as P

sharpness = 16.0
smearing = 0.04
screening = 4.0
strength = 24.0

SIN_C = [(-1.0) ** k * math.pi ** (2 * k + 1) / math.factorial(2 * k + 1) for k in range(7)]
COS_C = [(-1.0) ** k * math.pi ** (2 * k) / math.factorial(2 * k) for k in range(7)]


def poly(z, coefs):
    acc = jnp.full_like(z, coefs[-1])
    for c in coefs[-2::-1]:
        acc = acc * z + c
    return acc


def shifted(x, axis, dim, width):
    count, length = lax.axis_size(axis), x.shape[dim]
    up = [(i, (i + 1) % count) for i in range(count)]
    down = [(j, i) for i, j in up]
    last = lax.slice_in_dim(x, length - width, length, axis=dim)
    first = lax.slice_in_dim(x, 0, width, axis=dim)
    return lax.ppermute(last, axis, up), lax.ppermute(first, axis, down)


def widen(x, axis, dim):
    before, after = shifted(x, axis, dim, 1)
    return jnp.concatenate([before, x, after], axis=dim)


def message_kernel(cells_y, cells_z, fold_z, levels, home_ref, feat_ref, geom_ref, wb_ref, out_ref, hb, phi, acc):
    cell = pl.program_id(0)
    x = cell // (cells_y * cells_z)
    y = (cell // cells_z) % cells_y
    z = cell % cells_z
    slots = out_ref.shape[1]
    feat = out_ref.shape[2]
    near_z = feat_ref.shape[3]
    chunk = 32
    for a in range(3):
        hb[a] = jnp.broadcast_to(home_ref[0, :, a : a + 1], (slots, slots))
    for ox in range(3):
        for oy in range(3):
            for oz in range(near_z):
                g = geom_ref[x + ox, z, y + oy, oz]
                nx = g[0:1] + (ox - 1.0)
                ny = g[1:2] + (oy - 1.0)
                if fold_z:
                    nz = g[2:3]
                else:
                    nz = g[2:3] + (oz - 1.0)
                col = (oy * near_z + oz) * slots
                center = ox == 1 and oy == 1 and oz == (0 if fold_z else 1)
                for p0 in range(0, slots, chunk):
                    dx = nx - hb[0, p0 : p0 + chunk]
                    dy = ny - hb[1, p0 : p0 + chunk]
                    dz = nz - hb[2, p0 : p0 + chunk]
                    if fold_z and oz == 1:
                        dz = 1.0 - jnp.abs(dz)
                    radial_terms(dx, dy, dz, levels, center, p0, phi.at[ox], col, slots)
        rows = feat_ref[x + ox, z, pl.ds(y, 3)].reshape(3 * near_z * slots, feat)
        part = jnp.dot(phi[ox], rows, preferred_element_type=jnp.float32)
        if ox == 0:
            acc[...] = part
        elif ox == 1:
            acc[...] += part
    total = jnp.zeros((slots, feat), jnp.float32)
    for b in range(levels):
        both = acc[b * slots : (b + 1) * slots] + part[b * slots : (b + 1) * slots]
        total = total + both * wb_ref[b : b + 1]
    out_ref[0] = total.astype(jnp.bfloat16)


def basis_kernel(pos_ref, wave_ref, feat_ref, basis_ref, struct_ref):
    cell = pl.program_id(0)
    waves = wave_ref.shape[0]
    pos = pos_ref[0]
    chunk = 64
    for w0 in range(0, waves, chunk):
        wv = wave_ref[w0 : w0 + chunk]
        turns = wv[:, 0:1] * pos[0:1] + wv[:, 1:2] * pos[1:2] + wv[:, 2:3] * pos[2:3]
        u = turns - jnp.floor(turns + 0.5)
        q = u * u
        s = u * poly(q, SIN_C)
        c = poly(q, COS_C)
        basis_ref[0, w0 : w0 + chunk] = (1.0 - 2.0 * s * s).astype(jnp.bfloat16)
        basis_ref[0, waves + w0 : waves + w0 + chunk] = (2.0 * s * c).astype(jnp.bfloat16)
    part = jnp.dot(basis_ref[0], feat_ref[0], preferred_element_type=jnp.float32)

    @pl.when(cell == 0)
    def _():
        struct_ref[...] = part

    @pl.when(cell > 0)
    def _():
        struct_ref[...] += part


def final_kernel(basis_ref, grid_ref, msg_ref, feat_ref, home_ref, wm_ref, wo_ref, out_ref):
    far = lax.dot_general(
        basis_ref[0], grid_ref[...], (((0,), (0,)), ((), ())), preferred_element_type=jnp.float32
    )
    joined = far + jnp.dot(msg_ref[0], wm_ref[...], preferred_element_type=jnp.float32)
    hidden = (joined / (1.0 + jnp.exp(-joined))).astype(jnp.bfloat16)
    result = feat_ref[0].astype(jnp.float32) + jnp.dot(hidden, wo_ref[...], preferred_element_type=jnp.float32)
    out_ref[0] = (result * home_ref[0, :, 3:4]).astype(jnp.bfloat16)


def coords(index, counts):
    return (index // (counts[1] * counts[2]), (index // counts[2]) % counts[1], index % counts[2])


def layer_kernel(
    counts,
    levels,
    feat_in,
    frac_in,
    occ_in,
    index_in,
    radial_in,
    mix_in,
    we_in,
    wm_in,
    wo_in,
    out_ref,
    feat_ref,
    frac_ref,
    occ_ref,
    index_ref,
    radial_ref,
    mix_ref,
    we_ref,
    wm_ref,
    wo_ref,
    in_sem,
    wide,
    rows_sc,
    out_mask,
    turn_cols,
    wb,
    hb,
    phi,
    msg,
    basis,
    struct,
    pair,
    chip_sum,
    parts,
    share,
    field,
    halo_send,
    halo_recv,
    side_send,
    side_recv,
    pair_send,
    pair_recv,
    part_send,
    part_recv,
    share_send,
    share_recv,
):
    cx, cy, slots, feat = feat_ref.shape
    cells = cx * cy
    waves = index_ref.shape[1]
    heads = radial_ref.shape[0]
    devices = counts[0] * counts[1] * counts[2]
    grid = (counts[0] * cx, counts[1] * cy, counts[2])
    rows = waves // devices
    at = (lax.axis_index("gx"), lax.axis_index("gy"), lax.axis_index("gz"))
    chips = counts[0] * counts[1]
    chip = at[0] * counts[1] + at[1]
    core = at[2]
    mesh_id = pl.DeviceIdType.MESH
    pad = wide.shape[3] - slots

    reach = 2.0 * sharpness / (levels - 1) * math.log2(math.e)
    partner = (at[0], at[1], 1 - core)

    def same_core(k):
        peer = (chip + k) % chips
        return (peer // counts[1], peer % counts[1], core)

    def to_partner(src, dst, send, recv):
        return pltpu.make_async_remote_copy(
            src_ref=src, dst_ref=dst, send_sem=send, recv_sem=recv, device_id=partner, device_id_type=mesh_id
        )

    sources = [frac_in, occ_in, index_in, radial_in, feat_in, mix_in, we_in, wm_in, wo_in]
    places = [frac_ref, occ_ref, index_ref, radial_ref, feat_ref, mix_ref, we_ref, wm_ref, wo_ref]
    loads = [pltpu.make_async_copy(src, dst, in_sem.at[n]) for n, (src, dst) in enumerate(zip(sources, places))]
    for load in loads:
        load.start()

    barrier = pltpu.get_barrier_semaphore()

    @pl.loop(1, chips)
    def _(k):
        pl.semaphore_signal(barrier, inc=1, device_id=same_core(k), device_id_type=mesh_id)

    pl.semaphore_signal(barrier, inc=1, device_id=partner, device_id_type=mesh_id)

    for load in loads[:4]:
        load.wait()
    rows_sc[...] = jnp.zeros_like(rows_sc)
    for x in range(cx):
        for a in range(3):
            k = (x * 3 + a) * cy
            rows_sc[k : k + cy] = frac_ref[x, a].astype(jnp.float32)
    rows_sc[3 * cells : 4 * cells] = occ_ref[...].astype(jnp.float32)
    turned = rows_sc[...].T
    for x in range(cx):
        for y in range(cy):
            for a in range(3):
                k = (x * 3 + a) * cy + y
                hb[x * cy + y, a] = jnp.broadcast_to(turned[:, k : k + 1] * reach, (slots, slots))
            k = 3 * cells + x * cy + y
            out_mask[x * cy + y] = jnp.broadcast_to(turned[:, k : k + 1], (slots, feat))
    for w0 in range(0, waves, 128):
        part = [index_ref[a : a + 1, w0 : w0 + 128].astype(jnp.float32) * (1.0 / grid[a]) for a in range(3)]
        part = jnp.concatenate(part + [jnp.zeros((5, 128), jnp.float32)])
        turn_cols[w0 : w0 + 128] = part.T
    owner = lax.broadcasted_iota(jnp.int32, (heads, feat), 1) // (feat // heads)
    mine = owner == lax.broadcasted_iota(jnp.int32, (heads, feat), 0)
    for b in range(levels):
        level = b / (levels - 1)
        scale = math.exp(-sharpness * level * level) / math.sqrt(4.0 * slots) / reach**4
        column = jnp.broadcast_to(radial_ref[:, b : b + 1], (heads, feat)) * scale
        wb[b : b + 1] = jnp.sum(jnp.where(mine, column, 0.0), axis=0, keepdims=True)

    loads[4].wait()
    for x in range(cx):
        for y in range(cy):
            cell = x * cy + y
            ks = [(x * 3 + a) * cy + y for a in range(3)]
            wide[1 + x, 1 + y, 0, 0:slots] = feat_ref[x, y] * out_mask[cell].astype(jnp.bfloat16)
            own = jnp.concatenate([rows_sc[k : k + 1] for k in ks] + [jnp.zeros((pad - 3, slots), jnp.float32)])
            own = jnp.concatenate([own, jnp.zeros((pad, feat - slots), jnp.float32)], axis=1)
            wide[1 + x, 1 + y, 0, slots:] = own.astype(jnp.bfloat16)

    @pl.loop(0, cells)
    def _(cell):
        x = cell // cy
        y = cell % cy
        first = (x * 3) * cy + y
        start = [(at[0] * cx + x).astype(jnp.float32), (at[1] * cy + y).astype(jnp.float32), core.astype(jnp.float32)]
        pos = [rows_sc[pl.ds(first + a * cy, 1)] + start[a] for a in range(3)]
        lanes = pl.ds(pl.multiple_of(cell * slots, slots), slots)
        chunk = 64
        for w0 in range(0, waves, chunk):
            wv = turn_cols[w0 : w0 + chunk]
            turns = wv[:, 0:1] * pos[0] + wv[:, 1:2] * pos[1] + wv[:, 2:3] * pos[2]
            u = turns - jnp.floor(turns + 0.5)
            q = u * u
            s = u * poly(q, SIN_C)
            c = poly(q, COS_C)
            basis[w0 : w0 + chunk, lanes] = (1.0 - 2.0 * s * s).astype(jnp.bfloat16)
            basis[waves + w0 : waves + w0 + chunk, lanes] = (2.0 * s * c).astype(jnp.bfloat16)

    atoms = wide[1 : 1 + cx, 1 : 1 + cy, 0, 0:slots].reshape(cells * slots, feat)
    struct[...] = (
        jnp.dot(basis[...], atoms, preferred_element_type=jnp.float32)
        .astype(jnp.bfloat16)
        .reshape(2, chips, 2, rows, feat)
    )
    pl.semaphore_wait(barrier, chips)

    def span(step, length):
        if step == 0:
            return 1, 1, length
        if step == 1:
            return length, 0, 1
        return 1, length + 1, 1

    halo, side = {}, {}
    for n, (dx, dy) in enumerate([(0, 1), (0, -1), (1, 0), (-1, 0), (1, 1), (1, -1), (-1, 1), (-1, -1), (0, 0)]):
        sx, tx, lx = span(dx, cx)
        sy, ty, ly = span(dy, cy)
        region = (pl.ds(tx, lx), pl.ds(ty, ly))
        side[dx, dy] = to_partner(wide.at[(*region, 0)], wide.at[(*region, 1)], side_send.at[n], side_recv.at[n])
        if (dx, dy) == (0, 0):
            continue
        target = ((at[0] + dx + counts[0]) % counts[0], (at[1] + dy + counts[1]) % counts[1], core)
        halo[dx, dy] = pltpu.make_async_remote_copy(
            src_ref=wide.at[pl.ds(sx, lx), pl.ds(sy, ly), 0],
            dst_ref=wide.at[(*region, 0)],
            send_sem=halo_send.at[n],
            recv_sem=halo_recv.at[n],
            device_id=target,
            device_id_type=mesh_id,
        )

    swap = to_partner(struct.at[:, :, 1 - core], pair, pair_send.at[0], pair_recv.at[0])
    swap.start()
    side[0, 0].start()
    for copy in halo.values():
        copy.start()
    for load in loads[5:]:
        load.wait()
    msg[...] = jnp.zeros_like(msg)

    def part_copy(k):
        return pltpu.make_async_remote_copy(
            src_ref=chip_sum.at[:, (chip + k) % chips],
            dst_ref=parts.at[k],
            send_sem=part_send.at[k],
            recv_sem=part_recv.at[k],
            device_id=same_core(k),
            device_id_type=mesh_id,
        )

    def share_copy(k, slot):
        return pltpu.make_async_remote_copy(
            src_ref=share,
            dst_ref=field.at[:, slot, core],
            send_sem=share_send.at[k],
            recv_sem=share_recv.at[k],
            device_id=same_core(k),
            device_id_type=mesh_id,
        )

    def field_copy(half):
        mine = field.at[:, :, half]
        return to_partner(mine, mine, pair_send.at[1], pair_recv.at[1])

    def sum_pair():
        swap.wait()
        both = struct[:, :, core].astype(jnp.float32) + pair[...].astype(jnp.float32)
        chip_sum[...] = both.astype(jnp.bfloat16)

        @pl.loop(1, chips)
        def _(k):
            part_copy(k).start()

    def filter_share():
        @pl.loop(1, chips)
        def _(k):
            part_copy(k).wait()

        parts[0] = chip_sum[:, chip]
        total = jnp.sum(parts[...].astype(jnp.float32), axis=0).reshape(2 * rows, feat)
        mixed = jnp.dot(total, mix_ref[...], precision=lax.Precision.HIGHEST, preferred_element_type=jnp.float32)
        vec = turn_cols[pl.ds((chip * 2 + core) * rows, rows)] * (2.0 * math.pi)
        square = jnp.sum(vec * vec, axis=1, keepdims=True)
        damp = strength * jnp.exp(-0.5 * smearing * square) / (square + screening)
        damp = damp * (1.0 / math.sqrt(cells * slots * devices * waves))
        filtered = (mixed * jnp.concatenate([damp, damp])).astype(jnp.bfloat16)
        projected = jnp.dot(filtered, we_ref[...], preferred_element_type=jnp.float32)
        projected = projected.astype(jnp.bfloat16).reshape(2, rows, feat)
        share[...] = projected
        field[:, chip, core] = projected

        @pl.loop(1, chips)
        def _(k):
            share_copy(k, chip).start()

    def join_field():
        @pl.loop(1, chips)
        def _(k):
            share_copy(k, (chip - k + chips) % chips).wait()

        field_copy(core).start()

    def place(x, j):
        late = j // (2 * cy)
        xi = (1 - late) * (1 + j % 2) + late * (x * (cx + 1))
        y = ((1 - late) * (j // 2) + late * (j - 2 * cy) + 1) % cy
        return xi, y

    def weigh(x, j):
        xi, y = place(x, j)
        cell = x * cy + y
        step = xi - (x + 1)
        chunk = 16
        for oy in range(3):
            near = [
                wide[xi, y + oy, oz, slots : slots + pad, 0:slots].astype(jnp.float32) * reach for oz in range(2)
            ]
            near = jnp.concatenate(near, axis=1)
            nx = near[0:1] + step.astype(jnp.float32) * reach
            ny = near[1:2] + (oy - 1.0) * reach
            nz = near[2:3]
            for p0 in range(0, slots, chunk):
                gx, gy, gz = (
                    n - jnp.concatenate([hb[cell, a, p0 : p0 + chunk]] * 2, axis=1) for a, n in enumerate((nx, ny, nz))
                )
                gz = jnp.concatenate([gz[:, :slots], reach - jnp.abs(gz[:, slots:])], axis=1)
                diagonal = p0 + step * slots if oy == 1 else None
                radial_chain(gx, gy, gz, levels, reach, diagonal, p0, phi.at[x, oy], slots)

    def gather(x, j):
        xi, y = place(x, j)
        cell = x * cy + y
        near = wide[xi, pl.ds(y, 3), :, 0:slots].reshape(6 * slots, feat)
        left = jnp.concatenate([phi[x, oy] for oy in range(3)], axis=1)
        part = jnp.dot(left, near, preferred_element_type=jnp.float32)
        total = msg[cell]
        for b in range(levels):
            total = total + part[b * slots : (b + 1) * slots] * wb[b : b + 1]
        msg[cell] = total

    def halo_in(keys):
        for key in keys:
            halo[key].wait()
            side[key].start()

    def side_in(keys):
        for key in keys:
            side[key].wait()

    side_in([(0, 0)])
    weigh(0, jnp.int32(0))

    ends = 2 * cy - 4
    events = [
        (0, sum_pair),
        (ends - 2, lambda: halo_in([(0, -1)])),
        (ends - 1, lambda: side_in([(0, -1)])),
        (ends, lambda: halo_in([(0, 1)])),
        (ends + 1, lambda: side_in([(0, 1)])),
        (ends + 2, lambda: halo_in([(1, 0), (-1, 0)])),
        (ends + 2, filter_share),
        (ends + 3, lambda: side_in([(1, 0), (-1, 0)])),
        (3 * cy - 4, lambda: halo_in([(1, -1), (-1, -1)])),
        (3 * cy - 3, lambda: side_in([(1, -1), (-1, -1)])),
        (3 * cy - 3, lambda: halo_in([(1, 1), (-1, 1)])),
        (3 * cy - 2, lambda: side_in([(1, 1), (-1, 1)])),
        (3 * cy - 1, join_field),
    ]

    @pl.loop(0, 3 * cy)
    def _(j):
        for when, what in events:
            pl.when(j == when)(what)
        weigh(1, j)
        gather(0, j)
        weigh(0, j + 1)
        gather(1, j)

    field_copy(core).wait_send()
    field_copy(1 - core).wait_recv()

    waves_field = field[...].reshape(2 * waves, feat)

    @pl.loop(0, cells)
    def _(cell):
        lanes = pl.ds(pl.multiple_of(cell * slots, slots), slots)
        far = lax.dot_general(
            basis[:, lanes], waves_field, (((0,), (0,)), ((), ())), preferred_element_type=jnp.float32
        )
        near = msg[cell].astype(jnp.bfloat16)
        joined = far + jnp.dot(near, wm_ref[...], preferred_element_type=jnp.float32)
        hidden = (joined / (1.0 + jnp.exp(-joined))).astype(jnp.bfloat16)
        atom = wide[1 + cell // cy, 1 + cell % cy, 0, 0:slots].astype(jnp.float32)
        result = jnp.dot(hidden, wo_ref[...], preferred_element_type=jnp.float32)
        there = out_mask[cell]
        out_ref[cell] = (atom + result * there).astype(jnp.bfloat16)


def radial_chain(gx, gy, gz, levels, reach, diagonal, p0, phi, slots):
    rows = gx.shape[0]
    sq = jnp.minimum(gx * gx + gy * gy + gz * gz, reach * reach)
    ratio = jnp.exp2(sq * lax.rsqrt(jnp.maximum(sq, 1e-30)))
    edge = reach * reach - sq
    val = edge * edge * jnp.exp2(sq * (-sharpness * math.log2(math.e) / reach**2))
    if diagonal is not None:
        row = lax.broadcasted_iota(jnp.int32, (rows, slots), 0) + diagonal
        lane = lax.broadcasted_iota(jnp.int32, (rows, slots), 1)
        val = jnp.concatenate([jnp.where(row == lane, 0.0, val[:, :slots]), val[:, slots:]], axis=1)
    second = ratio * ratio
    steps = [val.astype(jnp.bfloat16), (val * ratio).astype(jnp.bfloat16)]
    fourth = (second * second).astype(jnp.bfloat16)
    second = second.astype(jnp.bfloat16)
    for b in range(2, levels):
        steps.append(steps[b - 2] * second if b < 4 else steps[b - 4] * fourth)
    for b in range(levels):
        phi[b * slots + p0 : b * slots + p0 + rows] = steps[b]


def radial_terms(gx, gy, gz, levels, center, p0, phi, col, slots):
    rows = gx.shape[0]
    sq = jnp.minimum(gx * gx + gy * gy + gz * gz, 1.0)
    dist = sq * lax.rsqrt(jnp.maximum(sq, 1e-30))
    ratio = jnp.exp2(dist * (2.0 * sharpness / (levels - 1) * math.log2(math.e)))
    edge = 1.0 - sq
    val = edge * edge * jnp.exp2(sq * (-sharpness * math.log2(math.e)))
    if center:
        row = lax.broadcasted_iota(jnp.int32, val.shape, 0) + p0
        lane = lax.broadcasted_iota(jnp.int32, val.shape, 1)
        val = jnp.where(row == lane, 0.0, val)
    for b in range(levels):
        phi[b * slots + p0 : b * slots + p0 + rows, col : col + slots] = val.astype(jnp.bfloat16)
        if b + 1 < levels:
            val = val * ratio


def body(
    features,
    fractions,
    occupied,
    wave_index,
    radial_weight,
    ewald_mix,
    msg_weight,
    ewald_weight,
    out_weight,
):
    cx, cy, cz, slots, feat = features.shape
    levels, heads = radial_weight.shape
    cells = cx * cy * cz
    grid = [lax.axis_size("gx") * cx, lax.axis_size("gy") * cy, lax.axis_size("gz") * cz]
    devices = lax.axis_size("gx") * lax.axis_size("gy") * lax.axis_size("gz")
    waves = wave_index.shape[1]
    axes = ("gx", "gy", "gz")
    full = lambda shape: pl.BlockSpec(shape, lambda i: (0,) * len(shape))
    params = pltpu.CompilerParams(dimension_semantics=("arbitrary",), vmem_limit_bytes=56 * 2**20)

    fold_z = grid[2] == 2 and cz == 1
    counts = tuple(lax.axis_size(n) for n in axes)
    rows = waves // devices
    chips = counts[0] * counts[1]
    if fold_z and rows % 16 == 0 and min(counts) > 1 and cx == 2 and cy > 2 and 4 * cells <= slots == 128:
        vmem = pl.BlockSpec(memory_space=pltpu.VMEM)
        dma = pltpu.SemaphoreType.DMA
        out = pl.pallas_call(
            functools.partial(layer_kernel, counts, levels),
            in_specs=[pl.BlockSpec(memory_space=pl.ANY)] * 9,
            out_specs=vmem,
            out_shape=pltpu.VMEM((cells, slots, feat), jnp.bfloat16),
            scratch_shapes=[
                pltpu.VMEM((cx, cy, slots, feat), jnp.bfloat16),
                pltpu.VMEM((cx, 3, cy, slots), jnp.bfloat16),
                pltpu.VMEM((cells, slots), jnp.int32),
                pltpu.VMEM(wave_index.shape, jnp.int32),
                pltpu.VMEM((heads, levels), jnp.float32),
                pltpu.VMEM(ewald_mix.shape, jnp.float32),
                pltpu.VMEM(ewald_weight.shape, jnp.bfloat16),
                pltpu.VMEM(msg_weight.shape, jnp.bfloat16),
                pltpu.VMEM(out_weight.shape, jnp.bfloat16),
                dma((9,)),
                pltpu.VMEM((cx + 2, cy + 2, 2, slots + 8, feat), jnp.bfloat16),
                pltpu.VMEM((slots, slots), jnp.float32),
                pltpu.VMEM((cells, slots, feat), jnp.float32),
                pltpu.VMEM((waves, 8), jnp.float32),
                pltpu.VMEM((levels, feat), jnp.float32),
                pltpu.VMEM((cells, 3, slots, slots), jnp.float32),
                pltpu.VMEM((2, 3, levels * slots, 2 * slots), jnp.bfloat16),
                pltpu.VMEM((cells, slots, feat), jnp.float32),
                pltpu.VMEM((2 * waves, cells * slots), jnp.bfloat16),
                pltpu.VMEM((2, chips, 2, rows, feat), jnp.bfloat16),
                pltpu.VMEM((2, chips, rows, feat), jnp.bfloat16),
                pltpu.VMEM((2, chips, rows, feat), jnp.bfloat16),
                pltpu.VMEM((chips, 2, rows, feat), jnp.bfloat16),
                pltpu.VMEM((2, rows, feat), jnp.bfloat16),
                pltpu.VMEM((2, chips, 2, rows, feat), jnp.bfloat16),
                dma((8,)),
                dma((8,)),
                dma((9,)),
                dma((9,)),
                dma((2,)),
                dma((2,)),
                dma((chips,)),
                dma((chips,)),
                dma((chips,)),
                dma((chips,)),
            ],
            compiler_params=pltpu.CompilerParams(
                collective_id=0, has_side_effects=True, vmem_limit_bytes=56 * 2**20
            ),
            name="layer",
        )(
            features.reshape(cx, cy, slots, feat),
            fractions.transpose(0, 2, 3, 1, 4).reshape(cx, 3, cy, slots),
            occupied.reshape(cells, slots),
            wave_index,
            radial_weight.T,
            ewald_mix,
            ewald_weight,
            msg_weight,
            out_weight,
        )
        return out.reshape(features.shape)

    masked = features * occupied[..., None].astype(jnp.bfloat16)
    frac = fractions.astype(jnp.float32)
    cell_feat = masked.reshape(cells, slots, feat)
    home = jnp.concatenate([frac, occupied[:, :, :, None, :].astype(jnp.float32)], axis=3)
    home = jnp.swapaxes(home.reshape(cells, 4, slots), 1, 2)

    start = [
        (lax.axis_index(n) * c + jnp.arange(c, dtype=jnp.int32)).astype(jnp.float32)
        for n, c in zip(axes, (cx, cy, cz))
    ]
    origin = jnp.stack(jnp.meshgrid(*start, indexing="ij"), axis=-1)[..., None]
    pos = (origin + frac).reshape(cells, 3, slots)
    lengths = jnp.array(grid, jnp.float32)
    index = wave_index.astype(jnp.float32)
    wave_vec = 2.0 * math.pi * index / lengths[:, None]
    wave_sq = jnp.sum(wave_vec * wave_vec, axis=0)
    damping = (
        strength
        * jnp.exp(-0.5 * smearing * wave_sq)
        / (wave_sq + screening)
        * (1.0 / math.sqrt(cells * slots * devices * waves))
    )
    wave_turn = (index / lengths[:, None]).T

    level = jnp.arange(levels, dtype=jnp.float32) / (levels - 1)
    wb = radial_weight * (jnp.exp(-sharpness * level * level) / math.sqrt(4.0 * slots))[:, None]
    wb = jnp.repeat(wb, feat // heads, axis=1)
    basis, struct = pl.pallas_call(
        basis_kernel,
        grid=(cells,),
        in_specs=[
            pl.BlockSpec((1, 3, slots), lambda i: (i, 0, 0)),
            full((waves, 3)),
            pl.BlockSpec((1, slots, feat), lambda i: (i, 0, 0)),
        ],
        out_specs=[pl.BlockSpec((1, 2 * waves, slots), lambda i: (i, 0, 0)), full((2 * waves, feat))],
        out_shape=[
            jax.ShapeDtypeStruct((cells, 2 * waves, slots), jnp.bfloat16),
            jax.ShapeDtypeStruct((2 * waves, feat), jnp.float32),
        ],
        compiler_params=params,
        name="basis",
    )(pos, wave_turn, cell_feat)

    wave_share = lax.psum_scatter(struct.reshape(2, waves, feat), axes, scatter_dimension=1, tiled=True)
    share_rows = wave_share.shape[1]
    share_damp = lax.dynamic_slice_in_dim(damping, lax.axis_index(axes) * share_rows, share_rows, 0)
    mixed = jnp.dot(wave_share.reshape(2 * share_rows, feat), ewald_mix, precision=lax.Precision.HIGHEST)
    filtered = (mixed.reshape(2, share_rows, feat) * share_damp[None, :, None]).astype(jnp.bfloat16)
    projected = jnp.dot(filtered, ewald_weight, preferred_element_type=jnp.float32).astype(jnp.bfloat16)
    field = lax.all_gather(projected, axes, axis=1, tiled=True).reshape(2 * waves, feat)

    wide_feat = widen(widen(masked, "gx", 0), "gy", 1)
    wide_geom = widen(widen(fractions, "gx", 0), "gy", 1)
    if fold_z:
        swap = [(0, 1), (1, 0)]
        wide_feat = jnp.concatenate([wide_feat, lax.ppermute(wide_feat, "gz", swap)], axis=2)
        wide_geom = jnp.concatenate([wide_geom, lax.ppermute(wide_geom, "gz", swap)], axis=2)
        near_z = 2
    else:
        wide_feat = widen(wide_feat, "gz", 2)
        wide_geom = widen(wide_geom, "gz", 2)
        near_z = 3
    wide_feat = jnp.stack([wide_feat[:, :, z : z + near_z] for z in range(cz)], axis=1)
    wide_geom = jnp.stack([wide_geom[:, :, z : z + near_z] for z in range(cz)], axis=1).astype(jnp.float32)
    messages = pl.pallas_call(
        functools.partial(message_kernel, cy, cz, fold_z, levels),
        grid=(cells,),
        in_specs=[
            pl.BlockSpec((1, slots, 4), lambda i: (i, 0, 0)),
            full(wide_feat.shape),
            full(wide_geom.shape),
            full(wb.shape),
        ],
        out_specs=pl.BlockSpec((1, slots, feat), lambda i: (i, 0, 0)),
        out_shape=jax.ShapeDtypeStruct((cells, slots, feat), jnp.bfloat16),
        scratch_shapes=[
            pltpu.VMEM((3, slots, slots), jnp.float32),
            pltpu.VMEM((3, levels * slots, 3 * near_z * slots), jnp.bfloat16),
            pltpu.VMEM((levels * slots, feat), jnp.float32),
        ],
        compiler_params=params,
        cost_estimate=pl.CostEstimate(
            flops=2 * cells * levels * slots * 9 * near_z * slots * feat, bytes_accessed=2**22, transcendentals=0
        ),
        name="messages",
    )(home, wide_feat, wide_geom, wb)

    out = pl.pallas_call(
        final_kernel,
        grid=(cells,),
        in_specs=[
            pl.BlockSpec((1, 2 * waves, slots), lambda i: (i, 0, 0)),
            full((2 * waves, feat)),
            pl.BlockSpec((1, slots, feat), lambda i: (i, 0, 0)),
            pl.BlockSpec((1, slots, feat), lambda i: (i, 0, 0)),
            pl.BlockSpec((1, slots, 4), lambda i: (i, 0, 0)),
            full((feat, feat)),
            full((feat, feat)),
        ],
        out_specs=pl.BlockSpec((1, slots, feat), lambda i: (i, 0, 0)),
        out_shape=jax.ShapeDtypeStruct((cells, slots, feat), jnp.bfloat16),
        compiler_params=params,
        name="final",
    )(basis, field, messages, cell_feat, home, msg_weight, out_weight)
    return out.reshape(features.shape)


def solution(mesh):
    cell = P("gx", "gy", "gz", None, None)
    in_specs = (cell, cell, P("gx", "gy", "gz", None), P(), P(), P(), P(), P(), P())
    return jax.shard_map(body, mesh=mesh, in_specs=in_specs, out_specs=cell, check_vma=False)
```

```python
import functools
import math

import jax
import jax.numpy as jnp
from jax import lax
from jax.experimental import pallas as pl
from jax.experimental.pallas import tpu as pltpu
from jax.sharding import PartitionSpec as P

sharpness = 16.0
smearing = 0.04
screening = 4.0
strength = 24.0

SIN_C = [(-1.0) ** k * math.pi ** (2 * k + 1) / math.factorial(2 * k + 1) for k in range(7)]
COS_C = [(-1.0) ** k * math.pi ** (2 * k) / math.factorial(2 * k) for k in range(7)]


def poly(z, coefs):
    acc = jnp.full_like(z, coefs[-1])
    for c in coefs[-2::-1]:
        acc = acc * z + c
    return acc


def shifted(x, axis, dim, width):
    count, length = lax.axis_size(axis), x.shape[dim]
    up = [(i, (i + 1) % count) for i in range(count)]
    down = [(j, i) for i, j in up]
    last = lax.slice_in_dim(x, length - width, length, axis=dim)
    first = lax.slice_in_dim(x, 0, width, axis=dim)
    return lax.ppermute(last, axis, up), lax.ppermute(first, axis, down)


def widen(x, axis, dim):
    before, after = shifted(x, axis, dim, 1)
    return jnp.concatenate([before, x, after], axis=dim)


def message_kernel(cells_y, cells_z, fold_z, levels, home_ref, feat_ref, geom_ref, wb_ref, out_ref, hb, phi, acc):
    cell = pl.program_id(0)
    x = cell // (cells_y * cells_z)
    y = (cell // cells_z) % cells_y
    z = cell % cells_z
    slots = out_ref.shape[1]
    feat = out_ref.shape[2]
    near_z = feat_ref.shape[3]
    chunk = 32
    for a in range(3):
        hb[a] = jnp.broadcast_to(home_ref[0, :, a : a + 1], (slots, slots))
    for ox in range(3):
        for oy in range(3):
            for oz in range(near_z):
                g = geom_ref[x + ox, z, y + oy, oz]
                nx = g[0:1] + (ox - 1.0)
                ny = g[1:2] + (oy - 1.0)
                if fold_z:
                    nz = g[2:3]
                else:
                    nz = g[2:3] + (oz - 1.0)
                col = (oy * near_z + oz) * slots
                center = ox == 1 and oy == 1 and oz == (0 if fold_z else 1)
                for p0 in range(0, slots, chunk):
                    dx = nx - hb[0, p0 : p0 + chunk]
                    dy = ny - hb[1, p0 : p0 + chunk]
                    dz = nz - hb[2, p0 : p0 + chunk]
                    if fold_z and oz == 1:
                        dz = 1.0 - jnp.abs(dz)
                    radial_terms(dx, dy, dz, levels, center, p0, phi.at[ox], col, slots)
        rows = feat_ref[x + ox, z, pl.ds(y, 3)].reshape(3 * near_z * slots, feat)
        part = jnp.dot(phi[ox], rows, preferred_element_type=jnp.float32)
        if ox == 0:
            acc[...] = part
        elif ox == 1:
            acc[...] += part
    total = jnp.zeros((slots, feat), jnp.float32)
    for b in range(levels):
        both = acc[b * slots : (b + 1) * slots] + part[b * slots : (b + 1) * slots]
        total = total + both * wb_ref[b : b + 1]
    out_ref[0] = total.astype(jnp.bfloat16)


def basis_kernel(pos_ref, wave_ref, feat_ref, basis_ref, struct_ref):
    cell = pl.program_id(0)
    waves = wave_ref.shape[0]
    pos = pos_ref[0]
    chunk = 64
    for w0 in range(0, waves, chunk):
        wv = wave_ref[w0 : w0 + chunk]
        turns = wv[:, 0:1] * pos[0:1] + wv[:, 1:2] * pos[1:2] + wv[:, 2:3] * pos[2:3]
        u = turns - jnp.floor(turns + 0.5)
        q = u * u
        s = u * poly(q, SIN_C)
        c = poly(q, COS_C)
        basis_ref[0, w0 : w0 + chunk] = (1.0 - 2.0 * s * s).astype(jnp.bfloat16)
        basis_ref[0, waves + w0 : waves + w0 + chunk] = (2.0 * s * c).astype(jnp.bfloat16)
    part = jnp.dot(basis_ref[0], feat_ref[0], preferred_element_type=jnp.float32)

    @pl.when(cell == 0)
    def _():
        struct_ref[...] = part

    @pl.when(cell > 0)
    def _():
        struct_ref[...] += part


def final_kernel(basis_ref, grid_ref, msg_ref, feat_ref, home_ref, wm_ref, wo_ref, out_ref):
    far = lax.dot_general(
        basis_ref[0], grid_ref[...], (((0,), (0,)), ((), ())), preferred_element_type=jnp.float32
    )
    joined = far + jnp.dot(msg_ref[0], wm_ref[...], preferred_element_type=jnp.float32)
    hidden = (joined / (1.0 + jnp.exp(-joined))).astype(jnp.bfloat16)
    result = feat_ref[0].astype(jnp.float32) + jnp.dot(hidden, wo_ref[...], preferred_element_type=jnp.float32)
    out_ref[0] = (result * home_ref[0, :, 3:4]).astype(jnp.bfloat16)


def coords(index, counts):
    return (index // (counts[1] * counts[2]), (index // counts[2]) % counts[1], index % counts[2])


def layer_kernel(
    counts,
    levels,
    feat_in,
    frac_in,
    occ_in,
    index_in,
    radial_in,
    mix_in,
    we_in,
    wm_in,
    wo_in,
    out_ref,
    feat_ref,
    frac_ref,
    occ_ref,
    index_ref,
    radial_ref,
    mix_ref,
    we_ref,
    wm_ref,
    wo_ref,
    in_sem,
    wide,
    rows_sc,
    out_mask,
    turn_cols,
    wb,
    hb,
    phi,
    msg,
    basis,
    struct,
    pair,
    chip_sum,
    parts,
    lines,
    field,
    token,
    halo_send,
    halo_recv,
    side_send,
    side_recv,
    pair_send,
    pair_recv,
    part_send,
    part_recv,
    line_send,
    line_recv,
    share_send,
    share_recv,
):
    cx, cy, slots, feat = feat_ref.shape
    cells = cx * cy
    waves = index_ref.shape[1]
    heads = radial_ref.shape[0]
    devices = counts[0] * counts[1] * counts[2]
    grid = (counts[0] * cx, counts[1] * cy, counts[2])
    rows = waves // devices
    at = (lax.axis_index("gx"), lax.axis_index("gy"), lax.axis_index("gz"))
    core = at[2]
    nx, ny = counts[0], counts[1]
    mesh_id = pl.DeviceIdType.MESH
    pad = wide.shape[3] - slots
    reach = 2.0 * sharpness / (levels - 1) * math.log2(math.e)
    partner = (at[0], at[1], 1 - core)
    lower = (at[0] + nx - 1) // nx
    upper = (2 * nx - 2 - at[0]) // nx

    def over_x(k):
        return ((at[0] + k + nx) % nx, at[1], core)

    def over_y(k):
        return (at[0], (at[1] + k + ny) % ny, core)

    def to_partner(src, dst, send, recv):
        return pltpu.make_async_remote_copy(
            src_ref=src, dst_ref=dst, send_sem=send, recv_sem=recv, device_id=partner, device_id_type=mesh_id
        )

    sources = [frac_in, occ_in, index_in, radial_in, feat_in, mix_in, we_in, wm_in, wo_in]
    places = [frac_ref, occ_ref, index_ref, radial_ref, feat_ref, mix_ref, we_ref, wm_ref, wo_ref]
    loads = [pltpu.make_async_copy(src, dst, in_sem.at[n]) for n, (src, dst) in enumerate(zip(sources, places))]
    for load in loads:
        load.start()

    barrier = pltpu.get_barrier_semaphore()

    def greet_line(sem):
        @pl.when(at[0] > 0)
        def _():
            pl.semaphore_signal(sem, inc=1, device_id=over_x(-1), device_id_type=mesh_id)

        @pl.when(at[0] < nx - 1)
        def _():
            pl.semaphore_signal(sem, inc=1, device_id=over_x(1), device_id_type=mesh_id)

    pl.semaphore_signal(barrier, inc=1, device_id=partner, device_id_type=mesh_id)
    greet_line(barrier)
    for k in range(1, ny):
        pl.semaphore_signal(barrier, inc=1, device_id=over_y(k), device_id_type=mesh_id)

    for load in loads[:4]:
        load.wait()
    rows_sc[...] = jnp.zeros_like(rows_sc)
    for x in range(cx):
        for a in range(3):
            k = (x * 3 + a) * cy
            rows_sc[k : k + cy] = frac_ref[x, a].astype(jnp.float32)
    rows_sc[3 * cells : 4 * cells] = occ_ref[...].astype(jnp.float32)
    turned = rows_sc[...].T
    for x in range(cx):
        for y in range(cy):
            k = 3 * cells + x * cy + y
            out_mask[x * cy + y] = jnp.broadcast_to(turned[:, k : k + 1], (slots, feat))
    loads[4].wait()
    for x in range(cx):
        for y in range(cy):
            cell = x * cy + y
            ks = [(x * 3 + a) * cy + y for a in range(3)]
            wide[1 + x, 1 + y, 0, 0:slots] = feat_ref[x, y] * out_mask[cell].astype(jnp.bfloat16)
            own = jnp.concatenate([rows_sc[k : k + 1] for k in ks] + [jnp.zeros((pad - 3, slots), jnp.float32)])
            own = jnp.concatenate([own, jnp.zeros((pad, feat - slots), jnp.float32)], axis=1)
            wide[1 + x, 1 + y, 0, slots:] = own.astype(jnp.bfloat16)

    def span(step, length):
        if step == 0:
            return 1, 1, length
        if step == 1:
            return length, 0, 1
        return 1, length + 1, 1

    halo, side = {}, {}
    for n, (dx, dy) in enumerate([(0, 1), (0, -1), (1, 0), (-1, 0), (1, 1), (1, -1), (-1, 1), (-1, -1), (0, 0)]):
        sx, tx, lx = span(dx, cx)
        sy, ty, ly = span(dy, cy)
        region = (pl.ds(tx, lx), pl.ds(ty, ly))
        side[dx, dy] = to_partner(wide.at[(*region, 0)], wide.at[(*region, 1)], side_send.at[n], side_recv.at[n])
        if (dx, dy) == (0, 0):
            continue
        halo[dx, dy] = pltpu.make_async_remote_copy(
            src_ref=wide.at[pl.ds(tx if dx and dy else sx, lx), pl.ds(sy, ly), 0],
            dst_ref=wide.at[(*region, 0)],
            send_sem=halo_send.at[n],
            recv_sem=halo_recv.at[n],
            device_id=over_y(dy) if dy else over_x(dx),
            device_id_type=mesh_id,
        )

    def send_faces(direct):
        for step, inside in ((1, at[0] < nx - 1), (-1, at[0] > 0)):
            pl.when(inside if direct else jnp.logical_not(inside))(halo[step, 0].start)

    def open_links():
        pl.semaphore_wait(barrier, 1 + lower + upper + ny - 1)
        greet_line(token.at[0])
        side[0, 0].start()
        halo[0, 1].start()
        halo[0, -1].start()
        send_faces(True)

    def pass_token():
        pl.semaphore_wait(token.at[0], lower + upper)
        greet_line(token.at[1])

    def open_wrap():
        pl.semaphore_wait(token.at[1], lower + upper)
        send_faces(False)

    for x in range(cx):
        for y in range(cy):
            for a in range(3):
                k = (x * 3 + a) * cy + y
                hb[x * cy + y, a] = jnp.broadcast_to(turned[:, k : k + 1] * reach, (slots, slots))
    for w0 in range(0, waves, 128):
        part = [index_ref[a : a + 1, w0 : w0 + 128].astype(jnp.float32) * (1.0 / grid[a]) for a in range(3)]
        part = jnp.concatenate(part + [jnp.zeros((5, 128), jnp.float32)])
        turn_cols[w0 : w0 + 128] = part.T
    owner = lax.broadcasted_iota(jnp.int32, (heads, feat), 1) // (feat // heads)
    mine = owner == lax.broadcasted_iota(jnp.int32, (heads, feat), 0)
    for b in range(levels):
        level = b / (levels - 1)
        scale = math.exp(-sharpness * level * level) / math.sqrt(4.0 * slots) / reach**4
        column = jnp.broadcast_to(radial_ref[:, b : b + 1], (heads, feat)) * scale
        wb[b : b + 1] = jnp.sum(jnp.where(mine, column, 0.0), axis=0, keepdims=True)

    @pl.loop(0, cells)
    def _(cell):
        x = cell // cy
        y = cell % cy
        first = (x * 3) * cy + y
        start = [(at[0] * cx + x).astype(jnp.float32), (at[1] * cy + y).astype(jnp.float32), core.astype(jnp.float32)]
        pos = [rows_sc[pl.ds(first + a * cy, 1)] + start[a] for a in range(3)]
        lanes = pl.ds(pl.multiple_of(cell * slots, slots), slots)
        pl.when(cell == 0)(open_links)
        pl.when(cell == cells // 4)(pass_token)
        pl.when(cell == cells // 2 + 1)(open_wrap)
        chunk = 64
        for w0 in range(0, waves, chunk):
            wv = turn_cols[w0 : w0 + chunk]
            turns = wv[:, 0:1] * pos[0] + wv[:, 1:2] * pos[1] + wv[:, 2:3] * pos[2]
            u = turns - jnp.floor(turns + 0.5)
            q = u * u
            s = u * poly(q, SIN_C)
            c = poly(q, COS_C)
            basis[w0 : w0 + chunk, lanes] = (1.0 - 2.0 * s * s).astype(jnp.bfloat16)
            basis[waves + w0 : waves + w0 + chunk, lanes] = (2.0 * s * c).astype(jnp.bfloat16)

    atoms = wide[1 : 1 + cx, 1 : 1 + cy, 0, 0:slots].reshape(cells * slots, feat)
    struct[...] = (
        jnp.dot(basis[...], atoms, preferred_element_type=jnp.float32)
        .astype(jnp.bfloat16)
        .reshape(struct.shape)
    )
    swap = to_partner(struct.at[:, :, :, 1 - core], pair, pair_send.at[0], pair_recv.at[0])
    swap.start()
    for load in loads[5:]:
        load.wait()
    msg[...] = jnp.zeros_like(msg)

    def part_copy(k):
        return pltpu.make_async_remote_copy(
            src_ref=chip_sum.at[:, :, (at[1] + k) % ny],
            dst_ref=parts.at[k],
            send_sem=part_send.at[k],
            recv_sem=part_recv.at[k],
            device_id=over_y(k),
            device_id_type=mesh_id,
        )

    def line_copy(k, slot):
        return pltpu.make_async_remote_copy(
            src_ref=lines.at[at[0]],
            dst_ref=lines.at[slot],
            send_sem=line_send.at[k],
            recv_sem=line_recv.at[k],
            device_id=over_x(k),
            device_id_type=mesh_id,
        )

    def share_copy(k, slot):
        return pltpu.make_async_remote_copy(
            src_ref=field.at[:, :, at[1], core],
            dst_ref=field.at[:, :, slot, core],
            send_sem=share_send.at[k],
            recv_sem=share_recv.at[k],
            device_id=over_y(k),
            device_id_type=mesh_id,
        )

    def field_copy(half):
        mine = field.at[:, :, :, half]
        return to_partner(mine, mine, pair_send.at[1], pair_recv.at[1])

    def sum_pair():
        swap.wait()
        both = struct[:, :, :, core].astype(jnp.float32) + pair[...].astype(jnp.float32)
        chip_sum[...] = both.astype(jnp.bfloat16)
        for k in range(1, ny):
            part_copy(k).start()

    def sum_parts():
        for k in range(1, ny):
            part_copy(k).wait()
        parts[0] = chip_sum[:, :, at[1]]
        lines[at[0]] = jnp.sum(parts[...].astype(jnp.float32), axis=0).astype(jnp.bfloat16)
        for k in range(1, nx):
            line_copy(k, at[0]).start()

    def filter_share():
        for k in range(1, nx):
            line_copy(k, (at[0] - k + nx) % nx).wait()
        total = jnp.sum(lines[...].astype(jnp.float32), axis=0).reshape(2 * nx * rows, feat)
        mixed = jnp.dot(total, mix_ref[...], precision=lax.Precision.HIGHEST, preferred_element_type=jnp.float32)
        vec = [turn_cols[pl.ds(((x * ny + at[1]) * 2 + core) * rows, rows)] for x in range(nx)]
        vec = jnp.concatenate(vec) * (2.0 * math.pi)
        square = jnp.sum(vec * vec, axis=1, keepdims=True)
        damp = strength * jnp.exp(-0.5 * smearing * square) / (square + screening)
        damp = damp * (1.0 / math.sqrt(cells * slots * devices * waves))
        filtered = (mixed * jnp.concatenate([damp, damp])).astype(jnp.bfloat16)
        projected = jnp.dot(filtered, we_ref[...], preferred_element_type=jnp.float32)
        field[:, :, at[1], core] = projected.astype(jnp.bfloat16).reshape(2, nx, rows, feat)
        for k in range(1, ny):
            share_copy(k, at[1]).start()

    def join_field():
        for k in range(1, ny):
            share_copy(k, (at[1] - k + ny) % ny).wait()
        field_copy(core).start()

    def place(x, j):
        late = j // (2 * cy)
        xi = (1 - late) * (1 + j % 2) + late * (x * (cx + 1))
        y = ((1 - late) * (j // 2) + late * (j - 2 * cy) + 1) % cy
        return xi, y

    def weigh(x, j):
        xi, y = place(x, j)
        cell = x * cy + y
        step = xi - (x + 1)
        chunk = 16
        for oy in range(3):
            near = [
                wide[xi, y + oy, oz, slots : slots + pad, 0:slots].astype(jnp.float32) * reach for oz in range(2)
            ]
            near = jnp.concatenate(near, axis=1)
            nx = near[0:1] + step.astype(jnp.float32) * reach
            ny = near[1:2] + (oy - 1.0) * reach
            nz = near[2:3]
            for p0 in range(0, slots, chunk):
                gx, gy, gz = (
                    n - jnp.concatenate([hb[cell, a, p0 : p0 + chunk]] * 2, axis=1) for a, n in enumerate((nx, ny, nz))
                )
                gz = jnp.concatenate([gz[:, :slots], reach - jnp.abs(gz[:, slots:])], axis=1)
                diagonal = p0 + step * slots if oy == 1 else None
                radial_chain(gx, gy, gz, levels, reach, diagonal, p0, phi.at[x, oy], slots)

    def gather(x, j):
        xi, y = place(x, j)
        cell = x * cy + y
        near = wide[xi, pl.ds(y, 3), :, 0:slots].reshape(6 * slots, feat)
        left = jnp.concatenate([phi[x, oy] for oy in range(3)], axis=1)
        part = jnp.dot(left, near, preferred_element_type=jnp.float32)
        total = msg[cell]
        for b in range(levels):
            total = total + part[b * slots : (b + 1) * slots] * wb[b : b + 1]
        msg[cell] = total

    def halo_in(keys):
        for key in keys:
            halo[key].wait_recv()
            side[key].start()

    def face_in(step):
        halo_in([(step, 0)])
        halo[step, 1].start()
        halo[step, -1].start()

    def faces_in(direct):
        for step, inside in ((1, at[0] > 0), (-1, at[0] < nx - 1)):
            pl.when(inside if direct else jnp.logical_not(inside))(functools.partial(face_in, step))

    def side_in(keys):
        for key in keys:
            side[key].wait()

    side_in([(0, 0)])
    weigh(0, jnp.int32(0))

    ends = 2 * cy - 4
    last = 3 * cy
    events = [
        (1, sum_pair),
        (ends - 2, lambda: halo_in([(0, -1)])),
        (ends - 1, lambda: side_in([(0, -1)])),
        (ends, lambda: halo_in([(0, 1)])),
        (ends, sum_parts),
        (ends + 1, lambda: side_in([(0, 1)])),
        (ends + 1, lambda: faces_in(True)),
        (ends + 2, lambda: faces_in(False)),
        (ends + 3, lambda: side_in([(1, 0), (-1, 0)])),
        (last - 4, filter_share),
        (last - 3, lambda: halo_in([(1, -1), (-1, -1)])),
        (last - 3, lambda: side_in([(1, -1), (-1, -1)])),
        (last - 2, lambda: halo_in([(1, 1), (-1, 1)])),
        (last - 2, lambda: side_in([(1, 1), (-1, 1)])),
        (last - 1, join_field),
    ]

    @pl.loop(0, 3 * cy)
    def _(j):
        for when, what in events:
            pl.when(j == when)(what)
        weigh(1, j)
        gather(0, j)
        weigh(0, j + 1)
        gather(1, j)

    for copy in halo.values():
        copy.wait_send()
    field_copy(core).wait_send()
    field_copy(1 - core).wait_recv()

    waves_field = field[...].reshape(2 * waves, feat)

    @pl.loop(0, cells)
    def _(cell):
        lanes = pl.ds(pl.multiple_of(cell * slots, slots), slots)
        far = lax.dot_general(
            basis[:, lanes], waves_field, (((0,), (0,)), ((), ())), preferred_element_type=jnp.float32
        )
        near = msg[cell].astype(jnp.bfloat16)
        joined = far + jnp.dot(near, wm_ref[...], preferred_element_type=jnp.float32)
        hidden = (joined / (1.0 + jnp.exp(-joined))).astype(jnp.bfloat16)
        atom = wide[1 + cell // cy, 1 + cell % cy, 0, 0:slots].astype(jnp.float32)
        result = jnp.dot(hidden, wo_ref[...], preferred_element_type=jnp.float32)
        there = out_mask[cell]
        out_ref[cell] = (atom + result * there).astype(jnp.bfloat16)


def radial_chain(gx, gy, gz, levels, reach, diagonal, p0, phi, slots):
    rows = gx.shape[0]
    sq = jnp.minimum(gx * gx + gy * gy + gz * gz, reach * reach)
    ratio = jnp.exp2(sq * lax.rsqrt(jnp.maximum(sq, 1e-30)))
    edge = reach * reach - sq
    val = edge * edge * jnp.exp2(sq * (-sharpness * math.log2(math.e) / reach**2))
    if diagonal is not None:
        row = lax.broadcasted_iota(jnp.int32, (rows, slots), 0) + diagonal
        lane = lax.broadcasted_iota(jnp.int32, (rows, slots), 1)
        val = jnp.concatenate([jnp.where(row == lane, 0.0, val[:, :slots]), val[:, slots:]], axis=1)
    second = ratio * ratio
    steps = [val.astype(jnp.bfloat16), (val * ratio).astype(jnp.bfloat16)]
    fourth = (second * second).astype(jnp.bfloat16)
    second = second.astype(jnp.bfloat16)
    for b in range(2, levels):
        steps.append(steps[b - 2] * second if b < 4 else steps[b - 4] * fourth)
    for b in range(levels):
        phi[b * slots + p0 : b * slots + p0 + rows] = steps[b]


def radial_terms(gx, gy, gz, levels, center, p0, phi, col, slots):
    rows = gx.shape[0]
    sq = jnp.minimum(gx * gx + gy * gy + gz * gz, 1.0)
    dist = sq * lax.rsqrt(jnp.maximum(sq, 1e-30))
    ratio = jnp.exp2(dist * (2.0 * sharpness / (levels - 1) * math.log2(math.e)))
    edge = 1.0 - sq
    val = edge * edge * jnp.exp2(sq * (-sharpness * math.log2(math.e)))
    if center:
        row = lax.broadcasted_iota(jnp.int32, val.shape, 0) + p0
        lane = lax.broadcasted_iota(jnp.int32, val.shape, 1)
        val = jnp.where(row == lane, 0.0, val)
    for b in range(levels):
        phi[b * slots + p0 : b * slots + p0 + rows, col : col + slots] = val.astype(jnp.bfloat16)
        if b + 1 < levels:
            val = val * ratio


def body(
    features,
    fractions,
    occupied,
    wave_index,
    radial_weight,
    ewald_mix,
    msg_weight,
    ewald_weight,
    out_weight,
):
    cx, cy, cz, slots, feat = features.shape
    levels, heads = radial_weight.shape
    cells = cx * cy * cz
    grid = [lax.axis_size("gx") * cx, lax.axis_size("gy") * cy, lax.axis_size("gz") * cz]
    devices = lax.axis_size("gx") * lax.axis_size("gy") * lax.axis_size("gz")
    waves = wave_index.shape[1]
    axes = ("gx", "gy", "gz")
    full = lambda shape: pl.BlockSpec(shape, lambda i: (0,) * len(shape))
    params = pltpu.CompilerParams(dimension_semantics=("arbitrary",), vmem_limit_bytes=56 * 2**20)

    fold_z = grid[2] == 2 and cz == 1
    counts = tuple(lax.axis_size(n) for n in axes)
    rows = waves // devices
    nx, ny = counts[:2]
    known = 2 < nx < 5
    if fold_z and known and rows % 16 == 0 and ny > 2 and cx == 2 and cy > 2 and 4 * cells <= slots == 128:
        vmem = pl.BlockSpec(memory_space=pltpu.VMEM)
        dma = pltpu.SemaphoreType.DMA
        out = pl.pallas_call(
            functools.partial(layer_kernel, counts, levels),
            in_specs=[pl.BlockSpec(memory_space=pl.ANY)] * 9,
            out_specs=vmem,
            out_shape=pltpu.VMEM((cells, slots, feat), jnp.bfloat16),
            scratch_shapes=[
                pltpu.VMEM((cx, cy, slots, feat), jnp.bfloat16),
                pltpu.VMEM((cx, 3, cy, slots), jnp.bfloat16),
                pltpu.VMEM((cells, slots), jnp.int32),
                pltpu.VMEM(wave_index.shape, jnp.int32),
                pltpu.VMEM((heads, levels), jnp.float32),
                pltpu.VMEM(ewald_mix.shape, jnp.float32),
                pltpu.VMEM(ewald_weight.shape, jnp.bfloat16),
                pltpu.VMEM(msg_weight.shape, jnp.bfloat16),
                pltpu.VMEM(out_weight.shape, jnp.bfloat16),
                dma((9,)),
                pltpu.VMEM((cx + 2, cy + 2, 2, slots + 8, feat), jnp.bfloat16),
                pltpu.VMEM((slots, slots), jnp.float32),
                pltpu.VMEM((cells, slots, feat), jnp.float32),
                pltpu.VMEM((waves, 8), jnp.float32),
                pltpu.VMEM((levels, feat), jnp.float32),
                pltpu.VMEM((cells, 3, slots, slots), jnp.float32),
                pltpu.VMEM((2, 3, levels * slots, 2 * slots), jnp.bfloat16),
                pltpu.VMEM((cells, slots, feat), jnp.float32),
                pltpu.VMEM((2 * waves, cells * slots), jnp.bfloat16),
                pltpu.VMEM((2, nx, ny, 2, rows, feat), jnp.bfloat16),
                pltpu.VMEM((2, nx, ny, rows, feat), jnp.bfloat16),
                pltpu.VMEM((2, nx, ny, rows, feat), jnp.bfloat16),
                pltpu.VMEM((ny, 2, nx, rows, feat), jnp.bfloat16),
                pltpu.VMEM((nx, 2, nx, rows, feat), jnp.bfloat16),
                pltpu.VMEM((2, nx, ny, 2, rows, feat), jnp.bfloat16),
                pltpu.SemaphoreType.REGULAR((2,)),
                dma((8,)),
                dma((8,)),
                dma((9,)),
                dma((9,)),
                dma((2,)),
                dma((2,)),
                dma((ny,)),
                dma((ny,)),
                dma((nx,)),
                dma((nx,)),
                dma((ny,)),
                dma((ny,)),
            ],
            compiler_params=pltpu.CompilerParams(
                collective_id=0, has_side_effects=True, vmem_limit_bytes=56 * 2**20
            ),
            name="layer",
        )(
            features.reshape(cx, cy, slots, feat),
            fractions.transpose(0, 2, 3, 1, 4).reshape(cx, 3, cy, slots),
            occupied.reshape(cells, slots),
            wave_index,
            radial_weight.T,
            ewald_mix,
            ewald_weight,
            msg_weight,
            out_weight,
        )
        return out.reshape(features.shape)

    masked = features * occupied[..., None].astype(jnp.bfloat16)
    frac = fractions.astype(jnp.float32)
    cell_feat = masked.reshape(cells, slots, feat)
    home = jnp.concatenate([frac, occupied[:, :, :, None, :].astype(jnp.float32)], axis=3)
    home = jnp.swapaxes(home.reshape(cells, 4, slots), 1, 2)

    start = [
        (lax.axis_index(n) * c + jnp.arange(c, dtype=jnp.int32)).astype(jnp.float32)
        for n, c in zip(axes, (cx, cy, cz))
    ]
    origin = jnp.stack(jnp.meshgrid(*start, indexing="ij"), axis=-1)[..., None]
    pos = (origin + frac).reshape(cells, 3, slots)
    lengths = jnp.array(grid, jnp.float32)
    index = wave_index.astype(jnp.float32)
    wave_vec = 2.0 * math.pi * index / lengths[:, None]
    wave_sq = jnp.sum(wave_vec * wave_vec, axis=0)
    damping = (
        strength
        * jnp.exp(-0.5 * smearing * wave_sq)
        / (wave_sq + screening)
        * (1.0 / math.sqrt(cells * slots * devices * waves))
    )
    wave_turn = (index / lengths[:, None]).T

    level = jnp.arange(levels, dtype=jnp.float32) / (levels - 1)
    wb = radial_weight * (jnp.exp(-sharpness * level * level) / math.sqrt(4.0 * slots))[:, None]
    wb = jnp.repeat(wb, feat // heads, axis=1)
    basis, struct = pl.pallas_call(
        basis_kernel,
        grid=(cells,),
        in_specs=[
            pl.BlockSpec((1, 3, slots), lambda i: (i, 0, 0)),
            full((waves, 3)),
            pl.BlockSpec((1, slots, feat), lambda i: (i, 0, 0)),
        ],
        out_specs=[pl.BlockSpec((1, 2 * waves, slots), lambda i: (i, 0, 0)), full((2 * waves, feat))],
        out_shape=[
            jax.ShapeDtypeStruct((cells, 2 * waves, slots), jnp.bfloat16),
            jax.ShapeDtypeStruct((2 * waves, feat), jnp.float32),
        ],
        compiler_params=params,
        name="basis",
    )(pos, wave_turn, cell_feat)

    wave_share = lax.psum_scatter(struct.reshape(2, waves, feat), axes, scatter_dimension=1, tiled=True)
    share_rows = wave_share.shape[1]
    share_damp = lax.dynamic_slice_in_dim(damping, lax.axis_index(axes) * share_rows, share_rows, 0)
    mixed = jnp.dot(wave_share.reshape(2 * share_rows, feat), ewald_mix, precision=lax.Precision.HIGHEST)
    filtered = (mixed.reshape(2, share_rows, feat) * share_damp[None, :, None]).astype(jnp.bfloat16)
    projected = jnp.dot(filtered, ewald_weight, preferred_element_type=jnp.float32).astype(jnp.bfloat16)
    field = lax.all_gather(projected, axes, axis=1, tiled=True).reshape(2 * waves, feat)

    wide_feat = widen(widen(masked, "gx", 0), "gy", 1)
    wide_geom = widen(widen(fractions, "gx", 0), "gy", 1)
    if fold_z:
        swap = [(0, 1), (1, 0)]
        wide_feat = jnp.concatenate([wide_feat, lax.ppermute(wide_feat, "gz", swap)], axis=2)
        wide_geom = jnp.concatenate([wide_geom, lax.ppermute(wide_geom, "gz", swap)], axis=2)
        near_z = 2
    else:
        wide_feat = widen(wide_feat, "gz", 2)
        wide_geom = widen(wide_geom, "gz", 2)
        near_z = 3
    wide_feat = jnp.stack([wide_feat[:, :, z : z + near_z] for z in range(cz)], axis=1)
    wide_geom = jnp.stack([wide_geom[:, :, z : z + near_z] for z in range(cz)], axis=1).astype(jnp.float32)
    messages = pl.pallas_call(
        functools.partial(message_kernel, cy, cz, fold_z, levels),
        grid=(cells,),
        in_specs=[
            pl.BlockSpec((1, slots, 4), lambda i: (i, 0, 0)),
            full(wide_feat.shape),
            full(wide_geom.shape),
            full(wb.shape),
        ],
        out_specs=pl.BlockSpec((1, slots, feat), lambda i: (i, 0, 0)),
        out_shape=jax.ShapeDtypeStruct((cells, slots, feat), jnp.bfloat16),
        scratch_shapes=[
            pltpu.VMEM((3, slots, slots), jnp.float32),
            pltpu.VMEM((3, levels * slots, 3 * near_z * slots), jnp.bfloat16),
            pltpu.VMEM((levels * slots, feat), jnp.float32),
        ],
        compiler_params=params,
        cost_estimate=pl.CostEstimate(
            flops=2 * cells * levels * slots * 9 * near_z * slots * feat, bytes_accessed=2**22, transcendentals=0
        ),
        name="messages",
    )(home, wide_feat, wide_geom, wb)

    out = pl.pallas_call(
        final_kernel,
        grid=(cells,),
        in_specs=[
            pl.BlockSpec((1, 2 * waves, slots), lambda i: (i, 0, 0)),
            full((2 * waves, feat)),
            pl.BlockSpec((1, slots, feat), lambda i: (i, 0, 0)),
            pl.BlockSpec((1, slots, feat), lambda i: (i, 0, 0)),
            pl.BlockSpec((1, slots, 4), lambda i: (i, 0, 0)),
            full((feat, feat)),
            full((feat, feat)),
        ],
        out_specs=pl.BlockSpec((1, slots, feat), lambda i: (i, 0, 0)),
        out_shape=jax.ShapeDtypeStruct((cells, slots, feat), jnp.bfloat16),
        compiler_params=params,
        name="final",
    )(basis, field, messages, cell_feat, home, msg_weight, out_weight)
    return out.reshape(features.shape)


def solution(mesh):
    cell = P("gx", "gy", "gz", None, None)
    in_specs = (cell, cell, P("gx", "gy", "gz", None), P(), P(), P(), P(), P(), P())
    return jax.shard_map(body, mesh=mesh, in_specs=in_specs, out_specs=cell, check_vma=False)
```

```python
import functools
import math

import jax
import jax.numpy as jnp
from jax import lax
from jax.experimental import pallas as pl
from jax.experimental.pallas import tpu as pltpu
from jax.sharding import PartitionSpec as P

sharpness = 16.0
smearing = 0.04
screening = 4.0
strength = 24.0

SIN_C = [(-1.0) ** k * math.pi ** (2 * k + 1) / math.factorial(2 * k + 1) for k in range(7)]
COS_C = [(-1.0) ** k * math.pi ** (2 * k) / math.factorial(2 * k) for k in range(7)]

SIN_P = [3.1415926401839953, -5.167710090331888, 2.550077659731212, -0.5982921594834444, 0.07765940825518475]
COS_P = [0.9999999534666585, -4.934792858674198, 4.058411914145813, -1.3318801611126891, 0.21969679833109643]


def poly(z, coefs):
    acc = jnp.full_like(z, coefs[-1])
    for c in coefs[-2::-1]:
        acc = acc * z + c
    return acc


def shifted(x, axis, dim, width):
    count, length = lax.axis_size(axis), x.shape[dim]
    up = [(i, (i + 1) % count) for i in range(count)]
    down = [(j, i) for i, j in up]
    last = lax.slice_in_dim(x, length - width, length, axis=dim)
    first = lax.slice_in_dim(x, 0, width, axis=dim)
    return lax.ppermute(last, axis, up), lax.ppermute(first, axis, down)


def widen(x, axis, dim):
    before, after = shifted(x, axis, dim, 1)
    return jnp.concatenate([before, x, after], axis=dim)


def message_kernel(cells_y, cells_z, fold_z, levels, home_ref, feat_ref, geom_ref, wb_ref, out_ref, hb, phi, acc):
    cell = pl.program_id(0)
    x = cell // (cells_y * cells_z)
    y = (cell // cells_z) % cells_y
    z = cell % cells_z
    slots = out_ref.shape[1]
    feat = out_ref.shape[2]
    near_z = feat_ref.shape[3]
    chunk = 32
    for a in range(3):
        hb[a] = jnp.broadcast_to(home_ref[0, :, a : a + 1], (slots, slots))
    for ox in range(3):
        for oy in range(3):
            for oz in range(near_z):
                g = geom_ref[x + ox, z, y + oy, oz]
                nx = g[0:1] + (ox - 1.0)
                ny = g[1:2] + (oy - 1.0)
                if fold_z:
                    nz = g[2:3]
                else:
                    nz = g[2:3] + (oz - 1.0)
                col = (oy * near_z + oz) * slots
                center = ox == 1 and oy == 1 and oz == (0 if fold_z else 1)
                for p0 in range(0, slots, chunk):
                    dx = nx - hb[0, p0 : p0 + chunk]
                    dy = ny - hb[1, p0 : p0 + chunk]
                    dz = nz - hb[2, p0 : p0 + chunk]
                    if fold_z and oz == 1:
                        dz = 1.0 - jnp.abs(dz)
                    radial_terms(dx, dy, dz, levels, center, p0, phi.at[ox], col, slots)
        rows = feat_ref[x + ox, z, pl.ds(y, 3)].reshape(3 * near_z * slots, feat)
        part = jnp.dot(phi[ox], rows, preferred_element_type=jnp.float32)
        if ox == 0:
            acc[...] = part
        elif ox == 1:
            acc[...] += part
    total = jnp.zeros((slots, feat), jnp.float32)
    for b in range(levels):
        both = acc[b * slots : (b + 1) * slots] + part[b * slots : (b + 1) * slots]
        total = total + both * wb_ref[b : b + 1]
    out_ref[0] = total.astype(jnp.bfloat16)


def basis_kernel(pos_ref, wave_ref, feat_ref, basis_ref, struct_ref):
    cell = pl.program_id(0)
    waves = wave_ref.shape[0]
    pos = pos_ref[0]
    chunk = 64
    for w0 in range(0, waves, chunk):
        wv = wave_ref[w0 : w0 + chunk]
        turns = wv[:, 0:1] * pos[0:1] + wv[:, 1:2] * pos[1:2] + wv[:, 2:3] * pos[2:3]
        u = turns - jnp.floor(turns + 0.5)
        q = u * u
        s = u * poly(q, SIN_C)
        c = poly(q, COS_C)
        basis_ref[0, w0 : w0 + chunk] = (1.0 - 2.0 * s * s).astype(jnp.bfloat16)
        basis_ref[0, waves + w0 : waves + w0 + chunk] = (2.0 * s * c).astype(jnp.bfloat16)
    part = jnp.dot(basis_ref[0], feat_ref[0], preferred_element_type=jnp.float32)

    @pl.when(cell == 0)
    def _():
        struct_ref[...] = part

    @pl.when(cell > 0)
    def _():
        struct_ref[...] += part


def final_kernel(basis_ref, grid_ref, msg_ref, feat_ref, home_ref, wm_ref, wo_ref, out_ref):
    far = lax.dot_general(
        basis_ref[0], grid_ref[...], (((0,), (0,)), ((), ())), preferred_element_type=jnp.float32
    )
    joined = far + jnp.dot(msg_ref[0], wm_ref[...], preferred_element_type=jnp.float32)
    hidden = (joined / (1.0 + jnp.exp(-joined))).astype(jnp.bfloat16)
    result = feat_ref[0].astype(jnp.float32) + jnp.dot(hidden, wo_ref[...], preferred_element_type=jnp.float32)
    out_ref[0] = (result * home_ref[0, :, 3:4]).astype(jnp.bfloat16)


def coords(index, counts):
    return (index // (counts[1] * counts[2]), (index // counts[2]) % counts[1], index % counts[2])


def layer_kernel(
    counts,
    levels,
    feat_in,
    frac_in,
    occ_in,
    index_in,
    radial_in,
    mix_in,
    we_in,
    wm_in,
    wo_in,
    out_ref,
    feat_ref,
    frac_ref,
    occ_ref,
    index_ref,
    radial_ref,
    mix_ref,
    we_ref,
    wm_ref,
    wo_ref,
    in_sem,
    wide,
    rows_sc,
    pos_sc,
    out_mask,
    turn_cols,
    wb,
    hb,
    phi,
    msg,
    basis,
    basis_t,
    joined,
    struct,
    pair,
    chip_sum,
    parts,
    lines,
    field,
    token,
    halo_send,
    halo_recv,
    side_send,
    side_recv,
    pair_send,
    pair_recv,
    part_send,
    part_recv,
    line_send,
    line_recv,
    share_send,
    share_recv,
):
    cx, cy, slots, feat = feat_ref.shape
    cells = cx * cy
    waves = index_ref.shape[1]
    heads = radial_ref.shape[0]
    devices = counts[0] * counts[1] * counts[2]
    grid = (counts[0] * cx, counts[1] * cy, counts[2])
    rows = waves // devices
    at = (lax.axis_index("gx"), lax.axis_index("gy"), lax.axis_index("gz"))
    core = at[2]
    nx, ny = counts[0], counts[1]
    mesh_id = pl.DeviceIdType.MESH
    pad = wide.shape[3] - slots
    reach = 2.0 * sharpness / (levels - 1) * math.log2(math.e)
    partner = (at[0], at[1], 1 - core)
    line_near = (at[0] + nx - 1) // nx + (2 * nx - 2 - at[0]) // nx
    bits = [1 << n for n in range(ny.bit_length() - 1)]

    def over_x(k):
        return ((at[0] + k + nx) % nx, at[1], core)

    def over_y(k):
        return (at[0], (at[1] + k + ny) % ny, core)

    def to_partner(src, dst, send, recv):
        return pltpu.make_async_remote_copy(
            src_ref=src, dst_ref=dst, send_sem=send, recv_sem=recv, device_id=partner, device_id_type=mesh_id
        )

    sources = [frac_in, occ_in, index_in, radial_in, feat_in, mix_in, we_in, wm_in, wo_in]
    places = [frac_ref, occ_ref, index_ref, radial_ref, feat_ref, mix_ref, we_ref, wm_ref, wo_ref]
    loads = [pltpu.make_async_copy(src, dst, in_sem.at[n]) for n, (src, dst) in enumerate(zip(sources, places))]
    for load in loads:
        load.start()

    barrier = pltpu.get_barrier_semaphore()

    def greet_line(sem):
        @pl.when(at[0] > 0)
        def _():
            pl.semaphore_signal(sem, inc=1, device_id=over_x(-1), device_id_type=mesh_id)

        @pl.when(at[0] < nx - 1)
        def _():
            pl.semaphore_signal(sem, inc=1, device_id=over_x(1), device_id_type=mesh_id)

    def greet_near(sem):
        greet_line(sem)
        for bit in bits:
            step = bit * (1 - 2 * (at[1] // bit % 2))
            pl.semaphore_signal(sem, inc=1, device_id=over_y(step), device_id_type=mesh_id)

    pl.semaphore_signal(barrier, inc=1, device_id=partner, device_id_type=mesh_id)
    greet_near(barrier)

    loads[0].wait()
    loads[1].wait()
    rows_sc[...] = jnp.zeros_like(rows_sc)
    for x in range(cx):
        for a in range(3):
            k = (x * 3 + a) * cy
            rows_sc[k : k + cy] = frac_ref[x, a].astype(jnp.float32)
    rows_sc[3 * cells : 4 * cells] = occ_ref[...].astype(jnp.float32)
    turned = rows_sc[...].T
    for x in range(cx):
        for y in range(cy):
            k = 3 * cells + x * cy + y
            out_mask[x * cy + y] = jnp.broadcast_to(turned[:, k : k + 1], (slots, feat))
    loads[4].wait()
    for x in range(cx):
        for y in range(cy):
            cell = x * cy + y
            ks = [(x * 3 + a) * cy + y for a in range(3)]
            wide[1 + x, 1 + y, 0, 0:slots] = feat_ref[x, y] * out_mask[cell].astype(jnp.bfloat16)
            own = jnp.concatenate([rows_sc[k : k + 1] for k in ks] + [jnp.zeros((pad - 3, slots), jnp.float32)])
            own = jnp.concatenate([own, jnp.zeros((pad, feat - slots), jnp.float32)], axis=1)
            wide[1 + x, 1 + y, 0, slots:] = own.astype(jnp.bfloat16)

    def span(step, length):
        if step == 0:
            return 1, 1, length
        if step == 1:
            return length, 0, 1
        return 1, length + 1, 1

    halo, side = {}, {}
    for n, (dx, dy) in enumerate([(0, 1), (0, -1), (1, 0), (-1, 0), (1, 1), (1, -1), (-1, 1), (-1, -1), (0, 0)]):
        sx, tx, lx = span(dx, cx)
        sy, ty, ly = span(dy, cy)
        region = (pl.ds(tx, lx), pl.ds(ty, ly))
        side[dx, dy] = to_partner(wide.at[(*region, 0)], wide.at[(*region, 1)], side_send.at[n], side_recv.at[n])
        if (dx, dy) == (0, 0):
            continue
        halo[dx, dy] = pltpu.make_async_remote_copy(
            src_ref=wide.at[pl.ds(tx if dx and dy else sx, lx), pl.ds(sy, ly), 0],
            dst_ref=wide.at[(*region, 0)],
            send_sem=halo_send.at[n],
            recv_sem=halo_recv.at[n],
            device_id=over_y(dy) if dy else over_x(dx),
            device_id_type=mesh_id,
        )

    def send_faces(direct):
        for step, inside in ((1, at[0] < nx - 1), (-1, at[0] > 0)):
            pl.when(inside if direct else jnp.logical_not(inside))(halo[step, 0].start)

    def send_rows(direct):
        for step, near in ((1, at[1] % 2 == 0), (-1, at[1] % 2 == 1)):
            pl.when(near if direct else jnp.logical_not(near))(halo[0, step].start)

    def pass_token():
        pl.semaphore_wait(token.at[0], line_near + len(bits))
        greet_line(token.at[1])
        send_rows(False)

    def open_wrap():
        pl.semaphore_wait(token.at[1], line_near)
        send_faces(False)

    pl.semaphore_wait(barrier, 1 + line_near + len(bits))
    greet_near(token.at[0])
    send_rows(True)
    send_faces(True)
    side[0, 0].start()

    loads[2].wait()
    for w0 in range(0, waves, 128):
        part = [index_ref[a : a + 1, w0 : w0 + 128].astype(jnp.float32) * (1.0 / grid[a]) for a in range(3)]
        part = jnp.concatenate(part + [jnp.zeros((5, 128), jnp.float32)])
        turn_cols[w0 : w0 + 128] = part.T
    for x in range(cx):
        for y in range(cy):
            start = [at[0] * cx + x, at[1] * cy + y, core]
            cell = x * cy + y
            for a in range(3):
                k = (x * 3 + a) * cy + y
                pos_sc[a : a + 1, cell * slots : (cell + 1) * slots] = rows_sc[k : k + 1] + start[a].astype(jnp.float32)

    @pl.loop(0, cells // 2)
    def _(two):
        pl.when(two == cells // 8)(pass_token)
        pl.when(two == cells // 4 + 1)(open_wrap)
        lanes = pl.ds(pl.multiple_of(two * 2 * slots, 2 * slots), 2 * slots)
        pos = pos_sc[:, lanes]
        chunk = 32
        for w0 in range(0, waves, chunk):
            wv = turn_cols[w0 : w0 + chunk]
            turns = wv[:, 0:1] * pos[0:1] + wv[:, 1:2] * pos[1:2] + wv[:, 2:3] * pos[2:3]
            u = turns - jnp.round(turns)
            q = u * u
            s = u * poly(q, [v * math.sqrt(2.0) for v in SIN_P])
            c = poly(q, [v * math.sqrt(2.0) for v in COS_P])
            basis[w0 : w0 + chunk, lanes] = (1.0 - s * s).astype(jnp.bfloat16)
            basis[waves + w0 : waves + w0 + chunk, lanes] = (s * c).astype(jnp.bfloat16)

    atoms = wide[1 : 1 + cx, 1 : 1 + cy, 0, 0:slots].reshape(cells * slots, feat)
    struct[...] = (
        jnp.dot(basis[...], atoms, preferred_element_type=jnp.float32)
        .astype(jnp.bfloat16)
        .reshape(struct.shape)
    )
    swap = to_partner(struct.at[:, 1 - core], pair, pair_send.at[0], pair_recv.at[0])
    swap.start()

    loads[3].wait()
    for x in range(cx):
        for y in range(cy):
            for a in range(3):
                k = (x * 3 + a) * cy + y
                hb[x * cy + y, a] = jnp.broadcast_to(turned[:, k : k + 1] * reach, (slots, slots))
    owner = lax.broadcasted_iota(jnp.int32, (heads, feat), 1) // (feat // heads)
    mine = owner == lax.broadcasted_iota(jnp.int32, (heads, feat), 0)
    for b in range(levels):
        level = b / (levels - 1)
        scale = math.exp(-sharpness * level * level) / math.sqrt(4.0 * slots) / reach**4
        column = jnp.broadcast_to(radial_ref[:, b : b + 1], (heads, feat)) * scale
        wb[b : b + 1] = jnp.sum(jnp.where(mine, column, 0.0), axis=0, keepdims=True)

    for load in loads[5:]:
        load.wait()
    msg[...] = jnp.zeros_like(msg)

    def part_copy(k):
        return pltpu.make_async_remote_copy(
            src_ref=chip_sum.at[:, :, (at[1] + k) % ny],
            dst_ref=parts.at[k],
            send_sem=part_send.at[k],
            recv_sem=part_recv.at[k],
            device_id=over_y(k),
            device_id_type=mesh_id,
        )

    def line_copy(k, slot):
        return pltpu.make_async_remote_copy(
            src_ref=lines.at[at[0]],
            dst_ref=lines.at[slot],
            send_sem=line_send.at[k],
            recv_sem=line_recv.at[k],
            device_id=over_x(k),
            device_id_type=mesh_id,
        )

    def share_copy(k, slot):
        return pltpu.make_async_remote_copy(
            src_ref=field.at[:, core, :, at[1]],
            dst_ref=field.at[:, core, :, slot],
            send_sem=share_send.at[k],
            recv_sem=share_recv.at[k],
            device_id=over_y(k),
            device_id_type=mesh_id,
        )

    def field_copy(half):
        mine = field.at[:, half]
        return to_partner(mine, mine, pair_send.at[1], pair_recv.at[1])

    def sum_pair():
        swap.wait()
        both = struct[:, core].astype(jnp.float32) + pair[...].astype(jnp.float32)
        chip_sum[...] = both.astype(jnp.bfloat16)
        for k in range(1, ny):
            part_copy(k).start()

    def sum_parts():
        for k in range(1, ny):
            part_copy(k).wait()
        parts[0] = chip_sum[:, :, at[1]]
        lines[at[0]] = jnp.sum(parts[...].astype(jnp.float32), axis=0).astype(jnp.bfloat16)
        for k in range(1, nx):
            line_copy(k, at[0]).start()

    def filter_share():
        for k in range(1, nx):
            line_copy(k, (at[0] - k + nx) % nx).wait()
        total = jnp.sum(lines[...].astype(jnp.float32), axis=0).reshape(2 * nx * rows, feat)
        mixed = jnp.dot(total, mix_ref[...], precision=lax.Precision.HIGHEST, preferred_element_type=jnp.float32)
        vec = [turn_cols[pl.ds(((core * nx + x) * ny + at[1]) * rows, rows)] for x in range(nx)]
        vec = jnp.concatenate(vec) * (2.0 * math.pi)
        square = jnp.sum(vec * vec, axis=1, keepdims=True)
        damp = strength * jnp.exp(-0.5 * smearing * square) / (square + screening)
        damp = damp * (1.0 / math.sqrt(cells * slots * devices * waves))
        filtered = (mixed * jnp.concatenate([damp, damp])).astype(jnp.bfloat16)
        projected = jnp.dot(filtered, we_ref[...], preferred_element_type=jnp.float32)
        field[:, core, :, at[1]] = projected.astype(jnp.bfloat16).reshape(2, nx, rows, feat)
        for k in range(1, ny):
            share_copy(k, at[1]).start()

    def join_field():
        for k in range(1, ny):
            share_copy(k, (at[1] - k + ny) % ny).wait()
        field_copy(core).start()

    def place(x, j):
        late = j // (2 * cy)
        xi = (1 - late) * (1 + j % 2) + late * (x * (cx + 1))
        y = ((1 - late) * (j // 2) + late * (j - 2 * cy) + 1) % cy
        return xi, y

    def weigh(x, j):
        xi, y = place(x, j)
        cell = x * cy + y
        step = xi - (x + 1)
        chunk = 16
        for oy in range(3):
            near = [
                wide[xi, y + oy, oz, slots : slots + pad, 0:slots].astype(jnp.float32) * reach for oz in range(2)
            ]
            near = jnp.concatenate(near, axis=1)
            nx = near[0:1] + step.astype(jnp.float32) * reach
            ny = near[1:2] + (oy - 1.0) * reach
            nz = near[2:3]
            for p0 in range(0, slots, chunk):
                gx, gy, gz = (
                    n - jnp.concatenate([hb[cell, a, p0 : p0 + chunk]] * 2, axis=1) for a, n in enumerate((nx, ny, nz))
                )
                gz = jnp.concatenate([gz[:, :slots], reach - jnp.abs(gz[:, slots:])], axis=1)
                diagonal = p0 + step * slots if oy == 1 else None
                radial_chain(gx, gy, gz, levels, reach, diagonal, p0, phi.at[x, oy], slots)

    def gather(x, j):
        xi, y = place(x, j)
        cell = x * cy + y
        near = wide[xi, pl.ds(y, 3), :, 0:slots].reshape(6 * slots, feat)
        left = jnp.concatenate([phi[x, oy] for oy in range(3)], axis=1)
        part = jnp.dot(left, near, preferred_element_type=jnp.float32)
        total = msg[cell]
        for b in range(levels):
            total = total + part[b * slots : (b + 1) * slots] * wb[b : b + 1]
        msg[cell] = total

    def halo_in(keys):
        for key in keys:
            halo[key].wait_recv()
            side[key].start()

    def face_in(step):
        halo_in([(step, 0)])
        halo[step, 1].start()
        halo[step, -1].start()

    def faces_in(direct):
        for step, inside in ((1, at[0] > 0), (-1, at[0] < nx - 1)):
            pl.when(inside if direct else jnp.logical_not(inside))(functools.partial(face_in, step))

    def side_in(keys):
        for key in keys:
            side[key].wait()

    side_in([(0, 0)])
    weigh(0, jnp.int32(0))

    ends = 2 * cy - 4
    last = 3 * cy
    events = [
        (1, sum_pair),
        (ends - 2, lambda: halo_in([(0, -1)])),
        (ends - 1, lambda: side_in([(0, -1)])),
        (ends, lambda: halo_in([(0, 1)])),
        (ends, sum_parts),
        (ends + 1, lambda: side_in([(0, 1)])),
        (ends + 1, lambda: faces_in(True)),
        (ends + 2, lambda: faces_in(False)),
        (ends + 3, lambda: side_in([(1, 0), (-1, 0)])),
        (last - 4, filter_share),
        (last - 3, lambda: halo_in([(1, -1), (-1, -1)])),
        (last - 3, lambda: side_in([(1, -1), (-1, -1)])),
        (last - 2, lambda: halo_in([(1, 1), (-1, 1)])),
        (last - 2, lambda: side_in([(1, 1), (-1, 1)])),
    ]

    @pl.loop(0, 3 * cy)
    def _(j):
        for when, what in events:
            pl.when(j == when)(what)
        cell = j % cells
        basis_t[cell] = basis[:, pl.ds(pl.multiple_of(cell * slots, slots), slots)].T
        weigh(1, j)
        gather(0, j)
        weigh(0, j + 1)
        gather(1, j)

    for copy in halo.values():
        copy.wait_send()

    half = waves // 2
    two = 2 * slots

    def far_of(pair_of_cells, half_of):
        c0 = pair_of_cells * 2
        first = pl.multiple_of(half_of * half, half)
        left = jnp.concatenate([basis_t[pl.ds(c0, 2), :, pl.ds(k * waves + first, half)] for k in range(2)], axis=2)
        right = field[:, half_of].reshape(waves, feat)
        return jnp.dot(left.reshape(two, waves), right, preferred_element_type=jnp.float32)

    @pl.loop(0, cells // 2)
    def _(n):
        near = msg[pl.ds(2 * n, 2)].reshape(two, feat).astype(jnp.bfloat16)
        joined[n] = jnp.dot(near, wm_ref[...], preferred_element_type=jnp.float32)

    join_field()

    @pl.loop(0, cells // 2)
    def _(n):
        joined[n] += far_of(n, core)

    field_copy(core).wait_send()
    field_copy(1 - core).wait_recv()

    @pl.loop(0, cells // 2)
    def _(n):
        total = joined[n] + far_of(n, 1 - core)
        hidden = (total / (1.0 + jnp.exp(-total))).astype(jnp.bfloat16)
        result = jnp.dot(hidden, wo_ref[...], preferred_element_type=jnp.float32).reshape(2, slots, feat)
        c0 = 2 * n
        atom = wide[1 + c0 // cy, pl.ds(1 + c0 % cy, 2), 0, 0:slots].astype(jnp.float32)
        out_ref[pl.ds(c0, 2)] = (atom + result * out_mask[pl.ds(c0, 2)]).astype(jnp.bfloat16)


def radial_chain(gx, gy, gz, levels, reach, diagonal, p0, phi, slots):
    rows = gx.shape[0]
    sq = jnp.minimum(gx * gx + gy * gy + gz * gz, reach * reach)
    ratio = jnp.exp2(sq * lax.rsqrt(jnp.maximum(sq, 1e-30)))
    edge = reach * reach - sq
    val = edge * edge * jnp.exp2(sq * (-sharpness * math.log2(math.e) / reach**2))
    if diagonal is not None:
        row = lax.broadcasted_iota(jnp.int32, (rows, slots), 0) + diagonal
        lane = lax.broadcasted_iota(jnp.int32, (rows, slots), 1)
        val = jnp.concatenate([jnp.where(row == lane, 0.0, val[:, :slots]), val[:, slots:]], axis=1)
    second = ratio * ratio
    steps = [val.astype(jnp.bfloat16), (val * ratio).astype(jnp.bfloat16)]
    fourth = (second * second).astype(jnp.bfloat16)
    second = second.astype(jnp.bfloat16)
    for b in range(2, levels):
        steps.append(steps[b - 2] * second if b < 4 else steps[b - 4] * fourth)
    for b in range(levels):
        phi[b * slots + p0 : b * slots + p0 + rows] = steps[b]


def radial_terms(gx, gy, gz, levels, center, p0, phi, col, slots):
    rows = gx.shape[0]
    sq = jnp.minimum(gx * gx + gy * gy + gz * gz, 1.0)
    dist = sq * lax.rsqrt(jnp.maximum(sq, 1e-30))
    ratio = jnp.exp2(dist * (2.0 * sharpness / (levels - 1) * math.log2(math.e)))
    edge = 1.0 - sq
    val = edge * edge * jnp.exp2(sq * (-sharpness * math.log2(math.e)))
    if center:
        row = lax.broadcasted_iota(jnp.int32, val.shape, 0) + p0
        lane = lax.broadcasted_iota(jnp.int32, val.shape, 1)
        val = jnp.where(row == lane, 0.0, val)
    for b in range(levels):
        phi[b * slots + p0 : b * slots + p0 + rows, col : col + slots] = val.astype(jnp.bfloat16)
        if b + 1 < levels:
            val = val * ratio


def body(
    features,
    fractions,
    occupied,
    wave_index,
    radial_weight,
    ewald_mix,
    msg_weight,
    ewald_weight,
    out_weight,
):
    cx, cy, cz, slots, feat = features.shape
    levels, heads = radial_weight.shape
    cells = cx * cy * cz
    grid = [lax.axis_size("gx") * cx, lax.axis_size("gy") * cy, lax.axis_size("gz") * cz]
    devices = lax.axis_size("gx") * lax.axis_size("gy") * lax.axis_size("gz")
    waves = wave_index.shape[1]
    axes = ("gx", "gy", "gz")
    full = lambda shape: pl.BlockSpec(shape, lambda i: (0,) * len(shape))
    params = pltpu.CompilerParams(dimension_semantics=("arbitrary",), vmem_limit_bytes=56 * 2**20)

    fold_z = grid[2] == 2 and cz == 1
    counts = tuple(lax.axis_size(n) for n in axes)
    rows = waves // devices
    nx, ny = counts[:2]
    known = 2 < nx < 5 and ny == 4 and waves % 512 == 0 and cy % 2 == 0
    if fold_z and known and rows % 16 == 0 and ny > 2 and cx == 2 and cy > 2 and 4 * cells <= slots == 128:
        vmem = pl.BlockSpec(memory_space=pltpu.VMEM)
        dma = pltpu.SemaphoreType.DMA
        out = pl.pallas_call(
            functools.partial(layer_kernel, counts, levels),
            in_specs=[pl.BlockSpec(memory_space=pl.ANY)] * 9,
            out_specs=vmem,
            out_shape=pltpu.VMEM((cells, slots, feat), jnp.bfloat16),
            scratch_shapes=[
                pltpu.VMEM((cx, cy, slots, feat), jnp.bfloat16),
                pltpu.VMEM((cx, 3, cy, slots), jnp.bfloat16),
                pltpu.VMEM((cells, slots), jnp.int32),
                pltpu.VMEM(wave_index.shape, jnp.int32),
                pltpu.VMEM((heads, levels), jnp.float32),
                pltpu.VMEM(ewald_mix.shape, jnp.float32),
                pltpu.VMEM(ewald_weight.shape, jnp.bfloat16),
                pltpu.VMEM(msg_weight.shape, jnp.bfloat16),
                pltpu.VMEM(out_weight.shape, jnp.bfloat16),
                dma((9,)),
                pltpu.VMEM((cx + 2, cy + 2, 2, slots + 8, feat), jnp.bfloat16),
                pltpu.VMEM((slots, slots), jnp.float32),
                pltpu.VMEM((3, cells * slots), jnp.float32),
                pltpu.VMEM((cells, slots, feat), jnp.float32),
                pltpu.VMEM((waves, 8), jnp.float32),
                pltpu.VMEM((levels, feat), jnp.float32),
                pltpu.VMEM((cells, 3, slots, slots), jnp.float32),
                pltpu.VMEM((2, 3, levels * slots, 2 * slots), jnp.bfloat16),
                pltpu.VMEM((cells, slots, feat), jnp.float32),
                pltpu.VMEM((2 * waves, cells * slots), jnp.bfloat16),
                pltpu.VMEM((cells, slots, 2 * waves), jnp.bfloat16),
                pltpu.VMEM((cells // 2, 2 * slots, feat), jnp.float32),
                pltpu.VMEM((2, 2, nx, ny, rows, feat), jnp.bfloat16),
                pltpu.VMEM((2, nx, ny, rows, feat), jnp.bfloat16),
                pltpu.VMEM((2, nx, ny, rows, feat), jnp.bfloat16),
                pltpu.VMEM((ny, 2, nx, rows, feat), jnp.bfloat16),
                pltpu.VMEM((nx, 2, nx, rows, feat), jnp.bfloat16),
                pltpu.VMEM((2, 2, nx, ny, rows, feat), jnp.bfloat16),
                pltpu.SemaphoreType.REGULAR((2,)),
                dma((8,)),
                dma((8,)),
                dma((9,)),
                dma((9,)),
                dma((2,)),
                dma((2,)),
                dma((ny,)),
                dma((ny,)),
                dma((nx,)),
                dma((nx,)),
                dma((ny,)),
                dma((ny,)),
            ],
            compiler_params=pltpu.CompilerParams(
                collective_id=0, has_side_effects=True, vmem_limit_bytes=56 * 2**20
            ),
            name="layer",
        )(
            features.reshape(cx, cy, slots, feat),
            fractions.transpose(0, 2, 3, 1, 4).reshape(cx, 3, cy, slots),
            occupied.reshape(cells, slots),
            wave_index,
            radial_weight.T,
            ewald_mix,
            ewald_weight,
            msg_weight,
            out_weight,
        )
        return out.reshape(features.shape)

    masked = features * occupied[..., None].astype(jnp.bfloat16)
    frac = fractions.astype(jnp.float32)
    cell_feat = masked.reshape(cells, slots, feat)
    home = jnp.concatenate([frac, occupied[:, :, :, None, :].astype(jnp.float32)], axis=3)
    home = jnp.swapaxes(home.reshape(cells, 4, slots), 1, 2)

    start = [
        (lax.axis_index(n) * c + jnp.arange(c, dtype=jnp.int32)).astype(jnp.float32)
        for n, c in zip(axes, (cx, cy, cz))
    ]
    origin = jnp.stack(jnp.meshgrid(*start, indexing="ij"), axis=-1)[..., None]
    pos = (origin + frac).reshape(cells, 3, slots)
    lengths = jnp.array(grid, jnp.float32)
    index = wave_index.astype(jnp.float32)
    wave_vec = 2.0 * math.pi * index / lengths[:, None]
    wave_sq = jnp.sum(wave_vec * wave_vec, axis=0)
    damping = (
        strength
        * jnp.exp(-0.5 * smearing * wave_sq)
        / (wave_sq + screening)
        * (1.0 / math.sqrt(cells * slots * devices * waves))
    )
    wave_turn = (index / lengths[:, None]).T

    level = jnp.arange(levels, dtype=jnp.float32) / (levels - 1)
    wb = radial_weight * (jnp.exp(-sharpness * level * level) / math.sqrt(4.0 * slots))[:, None]
    wb = jnp.repeat(wb, feat // heads, axis=1)
    basis, struct = pl.pallas_call(
        basis_kernel,
        grid=(cells,),
        in_specs=[
            pl.BlockSpec((1, 3, slots), lambda i: (i, 0, 0)),
            full((waves, 3)),
            pl.BlockSpec((1, slots, feat), lambda i: (i, 0, 0)),
        ],
        out_specs=[pl.BlockSpec((1, 2 * waves, slots), lambda i: (i, 0, 0)), full((2 * waves, feat))],
        out_shape=[
            jax.ShapeDtypeStruct((cells, 2 * waves, slots), jnp.bfloat16),
            jax.ShapeDtypeStruct((2 * waves, feat), jnp.float32),
        ],
        compiler_params=params,
        name="basis",
    )(pos, wave_turn, cell_feat)

    wave_share = lax.psum_scatter(struct.reshape(2, waves, feat), axes, scatter_dimension=1, tiled=True)
    share_rows = wave_share.shape[1]
    share_damp = lax.dynamic_slice_in_dim(damping, lax.axis_index(axes) * share_rows, share_rows, 0)
    mixed = jnp.dot(wave_share.reshape(2 * share_rows, feat), ewald_mix, precision=lax.Precision.HIGHEST)
    filtered = (mixed.reshape(2, share_rows, feat) * share_damp[None, :, None]).astype(jnp.bfloat16)
    projected = jnp.dot(filtered, ewald_weight, preferred_element_type=jnp.float32).astype(jnp.bfloat16)
    field = lax.all_gather(projected, axes, axis=1, tiled=True).reshape(2 * waves, feat)

    wide_feat = widen(widen(masked, "gx", 0), "gy", 1)
    wide_geom = widen(widen(fractions, "gx", 0), "gy", 1)
    if fold_z:
        swap = [(0, 1), (1, 0)]
        wide_feat = jnp.concatenate([wide_feat, lax.ppermute(wide_feat, "gz", swap)], axis=2)
        wide_geom = jnp.concatenate([wide_geom, lax.ppermute(wide_geom, "gz", swap)], axis=2)
        near_z = 2
    else:
        wide_feat = widen(wide_feat, "gz", 2)
        wide_geom = widen(wide_geom, "gz", 2)
        near_z = 3
    wide_feat = jnp.stack([wide_feat[:, :, z : z + near_z] for z in range(cz)], axis=1)
    wide_geom = jnp.stack([wide_geom[:, :, z : z + near_z] for z in range(cz)], axis=1).astype(jnp.float32)
    messages = pl.pallas_call(
        functools.partial(message_kernel, cy, cz, fold_z, levels),
        grid=(cells,),
        in_specs=[
            pl.BlockSpec((1, slots, 4), lambda i: (i, 0, 0)),
            full(wide_feat.shape),
            full(wide_geom.shape),
            full(wb.shape),
        ],
        out_specs=pl.BlockSpec((1, slots, feat), lambda i: (i, 0, 0)),
        out_shape=jax.ShapeDtypeStruct((cells, slots, feat), jnp.bfloat16),
        scratch_shapes=[
            pltpu.VMEM((3, slots, slots), jnp.float32),
            pltpu.VMEM((3, levels * slots, 3 * near_z * slots), jnp.bfloat16),
            pltpu.VMEM((levels * slots, feat), jnp.float32),
        ],
        compiler_params=params,
        cost_estimate=pl.CostEstimate(
            flops=2 * cells * levels * slots * 9 * near_z * slots * feat, bytes_accessed=2**22, transcendentals=0
        ),
        name="messages",
    )(home, wide_feat, wide_geom, wb)

    out = pl.pallas_call(
        final_kernel,
        grid=(cells,),
        in_specs=[
            pl.BlockSpec((1, 2 * waves, slots), lambda i: (i, 0, 0)),
            full((2 * waves, feat)),
            pl.BlockSpec((1, slots, feat), lambda i: (i, 0, 0)),
            pl.BlockSpec((1, slots, feat), lambda i: (i, 0, 0)),
            pl.BlockSpec((1, slots, 4), lambda i: (i, 0, 0)),
            full((feat, feat)),
            full((feat, feat)),
        ],
        out_specs=pl.BlockSpec((1, slots, feat), lambda i: (i, 0, 0)),
        out_shape=jax.ShapeDtypeStruct((cells, slots, feat), jnp.bfloat16),
        compiler_params=params,
        name="final",
    )(basis, field, messages, cell_feat, home, msg_weight, out_weight)
    return out.reshape(features.shape)


def solution(mesh):
    cell = P("gx", "gy", "gz", None, None)
    in_specs = (cell, cell, P("gx", "gy", "gz", None), P(), P(), P(), P(), P(), P())
    return jax.shard_map(body, mesh=mesh, in_specs=in_specs, out_specs=cell, check_vma=False)
```

```python
import functools
import math

import jax
import jax.numpy as jnp
from jax import lax
from jax.experimental import pallas as pl
from jax.experimental.pallas import tpu as pltpu
from jax.sharding import PartitionSpec as P

sharpness = 16.0
smearing = 0.04
screening = 4.0
strength = 24.0

SIN_C = [(-1.0) ** k * math.pi ** (2 * k + 1) / math.factorial(2 * k + 1) for k in range(7)]
COS_C = [(-1.0) ** k * math.pi ** (2 * k) / math.factorial(2 * k) for k in range(7)]

SIN_P = [3.1415926401839953, -5.167710090331888, 2.550077659731212, -0.5982921594834444, 0.07765940825518475]
COS_P = [0.9999999534666585, -4.934792858674198, 4.058411914145813, -1.3318801611126891, 0.21969679833109643]


def poly(z, coefs):
    acc = jnp.full_like(z, coefs[-1])
    for c in coefs[-2::-1]:
        acc = acc * z + c
    return acc


def shifted(x, axis, dim, width):
    count, length = lax.axis_size(axis), x.shape[dim]
    up = [(i, (i + 1) % count) for i in range(count)]
    down = [(j, i) for i, j in up]
    last = lax.slice_in_dim(x, length - width, length, axis=dim)
    first = lax.slice_in_dim(x, 0, width, axis=dim)
    return lax.ppermute(last, axis, up), lax.ppermute(first, axis, down)


def widen(x, axis, dim):
    before, after = shifted(x, axis, dim, 1)
    return jnp.concatenate([before, x, after], axis=dim)


def message_kernel(cells_y, cells_z, fold_z, levels, home_ref, feat_ref, geom_ref, wb_ref, out_ref, hb, phi, acc):
    cell = pl.program_id(0)
    x = cell // (cells_y * cells_z)
    y = (cell // cells_z) % cells_y
    z = cell % cells_z
    slots = out_ref.shape[1]
    feat = out_ref.shape[2]
    near_z = feat_ref.shape[3]
    chunk = 32
    for a in range(3):
        hb[a] = jnp.broadcast_to(home_ref[0, :, a : a + 1], (slots, slots))
    for ox in range(3):
        for oy in range(3):
            for oz in range(near_z):
                g = geom_ref[x + ox, z, y + oy, oz]
                nx = g[0:1] + (ox - 1.0)
                ny = g[1:2] + (oy - 1.0)
                if fold_z:
                    nz = g[2:3]
                else:
                    nz = g[2:3] + (oz - 1.0)
                col = (oy * near_z + oz) * slots
                center = ox == 1 and oy == 1 and oz == (0 if fold_z else 1)
                for p0 in range(0, slots, chunk):
                    dx = nx - hb[0, p0 : p0 + chunk]
                    dy = ny - hb[1, p0 : p0 + chunk]
                    dz = nz - hb[2, p0 : p0 + chunk]
                    if fold_z and oz == 1:
                        dz = 1.0 - jnp.abs(dz)
                    radial_terms(dx, dy, dz, levels, center, p0, phi.at[ox], col, slots)
        rows = feat_ref[x + ox, z, pl.ds(y, 3)].reshape(3 * near_z * slots, feat)
        part = jnp.dot(phi[ox], rows, preferred_element_type=jnp.float32)
        if ox == 0:
            acc[...] = part
        elif ox == 1:
            acc[...] += part
    total = jnp.zeros((slots, feat), jnp.float32)
    for b in range(levels):
        both = acc[b * slots : (b + 1) * slots] + part[b * slots : (b + 1) * slots]
        total = total + both * wb_ref[b : b + 1]
    out_ref[0] = total.astype(jnp.bfloat16)


def basis_kernel(pos_ref, wave_ref, feat_ref, basis_ref, struct_ref):
    cell = pl.program_id(0)
    waves = wave_ref.shape[0]
    pos = pos_ref[0]
    chunk = 64
    for w0 in range(0, waves, chunk):
        wv = wave_ref[w0 : w0 + chunk]
        turns = wv[:, 0:1] * pos[0:1] + wv[:, 1:2] * pos[1:2] + wv[:, 2:3] * pos[2:3]
        u = turns - jnp.floor(turns + 0.5)
        q = u * u
        s = u * poly(q, SIN_C)
        c = poly(q, COS_C)
        basis_ref[0, w0 : w0 + chunk] = (1.0 - 2.0 * s * s).astype(jnp.bfloat16)
        basis_ref[0, waves + w0 : waves + w0 + chunk] = (2.0 * s * c).astype(jnp.bfloat16)
    part = jnp.dot(basis_ref[0], feat_ref[0], preferred_element_type=jnp.float32)

    @pl.when(cell == 0)
    def _():
        struct_ref[...] = part

    @pl.when(cell > 0)
    def _():
        struct_ref[...] += part


def final_kernel(basis_ref, grid_ref, msg_ref, feat_ref, home_ref, wm_ref, wo_ref, out_ref):
    far = lax.dot_general(
        basis_ref[0], grid_ref[...], (((0,), (0,)), ((), ())), preferred_element_type=jnp.float32
    )
    joined = far + jnp.dot(msg_ref[0], wm_ref[...], preferred_element_type=jnp.float32)
    hidden = (joined / (1.0 + jnp.exp(-joined))).astype(jnp.bfloat16)
    result = feat_ref[0].astype(jnp.float32) + jnp.dot(hidden, wo_ref[...], preferred_element_type=jnp.float32)
    out_ref[0] = (result * home_ref[0, :, 3:4]).astype(jnp.bfloat16)


def coords(index, counts):
    return (index // (counts[1] * counts[2]), (index // counts[2]) % counts[1], index % counts[2])


def layer_kernel(
    counts,
    levels,
    feat_in,
    frac_in,
    occ_in,
    index_in,
    radial_in,
    mix_in,
    we_in,
    wm_in,
    wo_in,
    out_ref,
    feat_ref,
    frac_ref,
    occ_ref,
    index_ref,
    radial_ref,
    mix_ref,
    we_ref,
    wm_ref,
    wo_ref,
    in_sem,
    wide,
    geom,
    rows_sc,
    pos_sc,
    out_mask,
    turn_cols,
    wb,
    hb,
    phi,
    msg,
    basis,
    basis_t,
    joined,
    struct,
    pair,
    chip_sum,
    parts,
    lines,
    field,
    token,
    halo_send,
    halo_recv,
    side_send,
    side_recv,
    pair_send,
    pair_recv,
    part_send,
    part_recv,
    line_send,
    line_recv,
    share_send,
    share_recv,
):
    cx, cy, slots, feat = feat_ref.shape
    cells = cx * cy
    waves = index_ref.shape[1]
    heads = radial_ref.shape[0]
    devices = counts[0] * counts[1] * counts[2]
    grid = (counts[0] * cx, counts[1] * cy, counts[2])
    rows = waves // devices
    at = (lax.axis_index("gx"), lax.axis_index("gy"), lax.axis_index("gz"))
    core = at[2]
    nx, ny = counts[0], counts[1]
    mesh_id = pl.DeviceIdType.MESH
    pad = geom.shape[3]
    reach = 2.0 * sharpness / (levels - 1) * math.log2(math.e)
    partner = (at[0], at[1], 1 - core)
    line_near = (at[0] + nx - 1) // nx + (2 * nx - 2 - at[0]) // nx
    bits = [1 << n for n in range(ny.bit_length() - 1)]

    def over_x(k):
        return ((at[0] + k + nx) % nx, at[1], core)

    def over_y(k):
        return (at[0], (at[1] + k + ny) % ny, core)

    def to_partner(src, dst, send, recv):
        return pltpu.make_async_remote_copy(
            src_ref=src, dst_ref=dst, send_sem=send, recv_sem=recv, device_id=partner, device_id_type=mesh_id
        )

    sources = [frac_in, occ_in, index_in, radial_in, feat_in, mix_in, we_in, wm_in, wo_in]
    places = [frac_ref, occ_ref, index_ref, radial_ref, feat_ref, mix_ref, we_ref, wm_ref, wo_ref]
    loads = [pltpu.make_async_copy(src, dst, in_sem.at[n]) for n, (src, dst) in enumerate(zip(sources, places))]
    for load in loads:
        load.start()

    barrier = pltpu.get_barrier_semaphore()

    def greet_line(sem):
        @pl.when(at[0] > 0)
        def _():
            pl.semaphore_signal(sem, inc=1, device_id=over_x(-1), device_id_type=mesh_id)

        @pl.when(at[0] < nx - 1)
        def _():
            pl.semaphore_signal(sem, inc=1, device_id=over_x(1), device_id_type=mesh_id)

    def greet_near(sem):
        greet_line(sem)
        for bit in bits:
            step = bit * (1 - 2 * (at[1] // bit % 2))
            pl.semaphore_signal(sem, inc=1, device_id=over_y(step), device_id_type=mesh_id)

    pl.semaphore_signal(barrier, inc=1, device_id=partner, device_id_type=mesh_id)
    greet_near(barrier)

    loads[0].wait()
    loads[1].wait()
    rows_sc[...] = jnp.zeros_like(rows_sc)
    for x in range(cx):
        for a in range(3):
            k = (x * 3 + a) * cy
            rows_sc[k : k + cy] = frac_ref[x, a].astype(jnp.float32)
    rows_sc[3 * cells : 4 * cells] = occ_ref[...].astype(jnp.float32)
    turned = rows_sc[...].T
    for x in range(cx):
        for y in range(cy):
            k = 3 * cells + x * cy + y
            out_mask[x * cy + y] = jnp.broadcast_to(turned[:, k : k + 1], (slots, feat))
    loads[4].wait()
    for x in range(cx):
        for y in range(cy):
            cell = x * cy + y
            ks = [(x * 3 + a) * cy + y for a in range(3)]
            wide[1 + x, 1 + y, 0] = feat_ref[x, y] * out_mask[cell].astype(jnp.bfloat16)
            own = jnp.concatenate([rows_sc[k : k + 1] for k in ks] + [jnp.zeros((pad - 3, slots), jnp.float32)])
            geom[1 + x, 1 + y, 0] = own.astype(jnp.bfloat16)

    class Both:
        def __init__(self, copies):
            self.copies = copies

        def start(self):
            for copy in self.copies:
                copy.start()

        def wait(self):
            for copy in self.copies:
                copy.wait()

        def wait_send(self):
            for copy in self.copies:
                copy.wait_send()

        def wait_recv(self):
            for copy in self.copies:
                copy.wait_recv()

    halo, side = {}, {}

    def link(key, device, source, target):
        n = len(side)
        refs = list(enumerate((geom, wide)))
        side[key] = Both(
            [to_partner(r.at[(*target, 0)], r.at[(*target, 1)], side_send.at[n, i], side_recv.at[n, i]) for i, r in refs]
        )
        if device is not None:
            halo[key] = Both(
                [
                    pltpu.make_async_remote_copy(
                        src_ref=r.at[(*source, 0)],
                        dst_ref=r.at[(*target, 0)],
                        send_sem=halo_send.at[n, i],
                        recv_sem=halo_recv.at[n, i],
                        device_id=device,
                        device_id_type=mesh_id,
                    )
                    for i, r in refs
                ]
            )

    one = lambda start: pl.ds(start, 1)
    for dy in (1, -1):
        xs = pl.ds(1, cx)
        link((0, dy), over_y(dy), (xs, one(cy if dy == 1 else 1)), (xs, one(0 if dy == 1 else cy + 1)))
    for dx in (1, -1):
        sx, tx = one(cx if dx == 1 else 1), one(0 if dx == 1 else cx + 1)
        for name, ys in (("low", one(1)), ("high", one(cy)), ("middle", pl.ds(2, cy - 2))):
            link((dx, name), over_x(dx), (sx, ys), (tx, ys))
        for dy in (1, -1):
            link((dx, dy), over_y(dy), (tx, one(cy if dy == 1 else 1)), (tx, one(0 if dy == 1 else cy + 1)))
    link((0, 0), None, None, (pl.ds(1, cx), pl.ds(1, cy)))

    def send_face(step):
        for name in ("low", "high", "middle"):
            halo[step, name].start()

    def send_faces(direct):
        for step, inside in ((1, at[0] < nx - 1), (-1, at[0] > 0)):
            pl.when(inside if direct else jnp.logical_not(inside))(functools.partial(send_face, step))

    def send_rows(direct):
        for step, near in ((1, at[1] % 2 == 0), (-1, at[1] % 2 == 1)):
            pl.when(near if direct else jnp.logical_not(near))(halo[0, step].start)

    def pass_token():
        pl.semaphore_wait(token.at[0], line_near + len(bits))
        greet_line(token.at[1])
        send_rows(False)

    def open_wrap():
        pl.semaphore_wait(token.at[1], line_near)
        send_faces(False)

    pl.semaphore_wait(barrier, 1 + line_near + len(bits))
    greet_near(token.at[0])
    send_rows(True)
    send_faces(True)
    side[0, 0].start()

    loads[2].wait()
    for w0 in range(0, waves, 128):
        part = [index_ref[a : a + 1, w0 : w0 + 128].astype(jnp.float32) * (1.0 / grid[a]) for a in range(3)]
        part = jnp.concatenate(part + [jnp.zeros((5, 128), jnp.float32)])
        turn_cols[w0 : w0 + 128] = part.T
    for x in range(cx):
        for y in range(cy):
            start = [at[0] * cx + x, at[1] * cy + y, core]
            cell = x * cy + y
            for a in range(3):
                k = (x * 3 + a) * cy + y
                pos_sc[a : a + 1, cell * slots : (cell + 1) * slots] = rows_sc[k : k + 1] + start[a].astype(jnp.float32)

    @pl.loop(0, cells // 2)
    def _(two):
        pl.when(two == cells // 8)(pass_token)
        pl.when(two == cells // 4 + 1)(open_wrap)
        lanes = pl.ds(pl.multiple_of(two * 2 * slots, 2 * slots), 2 * slots)
        pos = pos_sc[:, lanes]
        chunk = 32
        for w0 in range(0, waves, chunk):
            wv = turn_cols[w0 : w0 + chunk]
            turns = wv[:, 0:1] * pos[0:1] + wv[:, 1:2] * pos[1:2] + wv[:, 2:3] * pos[2:3]
            u = turns - jnp.round(turns)
            q = u * u
            s = u * poly(q, [v * math.sqrt(2.0) for v in SIN_P])
            c = poly(q, [v * math.sqrt(2.0) for v in COS_P])
            basis[w0 : w0 + chunk, lanes] = (1.0 - s * s).astype(jnp.bfloat16)
            basis[waves + w0 : waves + w0 + chunk, lanes] = (s * c).astype(jnp.bfloat16)

    atoms = wide[1 : 1 + cx, 1 : 1 + cy, 0].reshape(cells * slots, feat)
    struct[...] = (
        jnp.dot(basis[...], atoms, preferred_element_type=jnp.float32)
        .astype(jnp.bfloat16)
        .reshape(struct.shape)
    )
    swap = to_partner(struct.at[:, 1 - core], pair, pair_send.at[0], pair_recv.at[0])
    swap.start()

    loads[3].wait()
    for x in range(cx):
        for y in range(cy):
            for a in range(3):
                k = (x * 3 + a) * cy + y
                hb[x * cy + y, a] = jnp.broadcast_to(turned[:, k : k + 1] * reach, (slots, slots))
    owner = lax.broadcasted_iota(jnp.int32, (heads, feat), 1) // (feat // heads)
    mine = owner == lax.broadcasted_iota(jnp.int32, (heads, feat), 0)
    for b in range(levels):
        level = b / (levels - 1)
        scale = math.exp(-sharpness * level * level) / math.sqrt(4.0 * slots) / reach**4
        column = jnp.broadcast_to(radial_ref[:, b : b + 1], (heads, feat)) * scale
        wb[b : b + 1] = jnp.sum(jnp.where(mine, column, 0.0), axis=0, keepdims=True)

    for load in loads[5:]:
        load.wait()
    msg[...] = jnp.zeros_like(msg)

    def part_copy(k):
        return pltpu.make_async_remote_copy(
            src_ref=chip_sum.at[:, :, (at[1] + k) % ny],
            dst_ref=parts.at[k],
            send_sem=part_send.at[k],
            recv_sem=part_recv.at[k],
            device_id=over_y(k),
            device_id_type=mesh_id,
        )

    def line_copy(k, slot):
        return pltpu.make_async_remote_copy(
            src_ref=lines.at[at[0]],
            dst_ref=lines.at[slot],
            send_sem=line_send.at[k],
            recv_sem=line_recv.at[k],
            device_id=over_x(k),
            device_id_type=mesh_id,
        )

    def share_copy(k, slot):
        return pltpu.make_async_remote_copy(
            src_ref=field.at[:, core, :, at[1]],
            dst_ref=field.at[:, core, :, slot],
            send_sem=share_send.at[k],
            recv_sem=share_recv.at[k],
            device_id=over_y(k),
            device_id_type=mesh_id,
        )

    def field_copy(half):
        mine = field.at[:, half]
        return to_partner(mine, mine, pair_send.at[1], pair_recv.at[1])

    def sum_pair():
        swap.wait()
        both = struct[:, core].astype(jnp.float32) + pair[...].astype(jnp.float32)
        chip_sum[...] = both.astype(jnp.bfloat16)
        for k in range(1, ny):
            part_copy(k).start()

    def sum_parts():
        for k in range(1, ny):
            part_copy(k).wait()
        parts[0] = chip_sum[:, :, at[1]]
        lines[at[0]] = jnp.sum(parts[...].astype(jnp.float32), axis=0).astype(jnp.bfloat16)
        for k in range(1, nx):
            line_copy(k, at[0]).start()

    def filter_share():
        for k in range(1, nx):
            line_copy(k, (at[0] - k + nx) % nx).wait()
        total = jnp.sum(lines[...].astype(jnp.float32), axis=0).reshape(2 * nx * rows, feat)
        mixed = jnp.dot(total, mix_ref[...], precision=lax.Precision.HIGHEST, preferred_element_type=jnp.float32)
        vec = [turn_cols[pl.ds(((core * nx + x) * ny + at[1]) * rows, rows)] for x in range(nx)]
        vec = jnp.concatenate(vec) * (2.0 * math.pi)
        square = jnp.sum(vec * vec, axis=1, keepdims=True)
        damp = strength * jnp.exp(-0.5 * smearing * square) / (square + screening)
        damp = damp * (1.0 / math.sqrt(cells * slots * devices * waves))
        filtered = (mixed * jnp.concatenate([damp, damp])).astype(jnp.bfloat16)
        projected = jnp.dot(filtered, we_ref[...], preferred_element_type=jnp.float32)
        field[:, core, :, at[1]] = projected.astype(jnp.bfloat16).reshape(2, nx, rows, feat)
        for k in range(1, ny):
            share_copy(k, at[1]).start()

    def join_field():
        for k in range(1, ny):
            share_copy(k, (at[1] - k + ny) % ny).wait()
        field_copy(core).start()

    first_x = 1 - (at[0] + nx - 1) // nx

    def place(slot, j):
        late = j // (2 * cy)
        i = j % (2 * cy)
        turn = i // (cy // 2)
        x = (1 - late) * slot + late * (turn + (1 - 2 * turn) * first_x)
        y = ((1 - late) * (i // 2) + late * (2 * (i % (cy // 2)) + slot) + 1) % cy
        xi = (1 - late) * (1 + i % 2) + late * x * (cx + 1)
        return x, y, xi

    def weigh(slot, j):
        x, y, xi = place(slot, j)
        cell = x * cy + y
        step = xi - (x + 1)
        chunk = 16
        done = []
        for oy in range(3):
            near = [
                geom[xi, y + oy, oz].astype(jnp.float32) * reach for oz in range(2)
            ]
            near = jnp.concatenate(near, axis=1)
            nx = near[0:1] + step.astype(jnp.float32) * reach
            ny = near[1:2] + (oy - 1.0) * reach
            nz = near[2:3]
            for p0 in range(0, slots, chunk):
                row = nx
                if len(done) >= 2:
                    o, p = done[-2]
                    row = jnp.concatenate([nx[:, :slots] + jnp.minimum(phi[slot, o, p + 7 * slots : p + 7 * slots + 8, :slots].astype(jnp.float32)[0:1], 0.0), nx[:, slots:]], axis=1)
                done.append((oy, p0))
                gx, gy, gz = (
                    n - jnp.concatenate([hb[cell, a, p0 : p0 + chunk]] * 2, axis=1) for a, n in enumerate((row, ny, nz))
                )
                gz = jnp.concatenate([gz[:, :slots], reach - jnp.abs(gz[:, slots:])], axis=1)
                diagonal = p0 + step * slots if oy == 1 else None
                radial_chain(gx, gy, gz, levels, reach, diagonal, p0, phi.at[slot, oy], slots)

    def gather(slot, j):
        x, y, xi = place(slot, j)
        near = wide[xi, pl.ds(y, 3)].reshape(6 * slots, feat)
        left = jnp.concatenate([phi[slot, oy] for oy in range(3)], axis=1)
        part = jnp.dot(left, near, preferred_element_type=jnp.float32)
        total = msg[x * cy + y]
        for b in range(levels):
            total = total + part[b * slots : (b + 1) * slots] * wb[b : b + 1]
        msg[x * cy + y] = total

    def halo_in(*keys):
        for key in keys:
            halo[key].wait_recv()
            side[key].start()

    def side_in(*keys):
        for key in keys:
            side[key].wait()

    def face_in(step):
        halo_in((step, "low"))
        halo[step, -1].start()
        halo_in((step, "high"))
        halo[step, 1].start()

    def rest_in(step):
        halo_in((step, "middle"))

    def face_done(step):
        side_in((step, "low"), (step, "high"), (step, "middle"))

    def corners_in(step):
        halo_in((step, -1), (step, 1))

    def corners_done(step):
        side_in((step, -1), (step, 1))

    def on_side(first, what):
        def run():
            for step, then in ((1, first_x == 0), (-1, first_x == 1)):
                pl.when(then if first else jnp.logical_not(then))(functools.partial(what, step))

        return run

    side_in((0, 0))
    weigh(0, jnp.int32(0))

    ends = 2 * cy - 4
    last = 3 * cy
    events = [
        (1, sum_pair),
        (ends - 3, lambda: halo_in((0, -1), (0, 1))),
        (ends - 2, on_side(True, face_in)),
        (ends - 1, lambda: side_in((0, -1))),
        (ends - 1, on_side(True, rest_in)),
        (ends, sum_parts),
        (ends + 1, lambda: side_in((0, 1))),
        (ends + 1, on_side(True, corners_in)),
        (ends + 2, on_side(False, face_in)),
        (ends + 3, on_side(True, face_done)),
        (last - 4, on_side(True, corners_done)),
        (last - 4, on_side(False, rest_in)),
        (last - 3, on_side(False, corners_in)),
        (last - 3, on_side(False, face_done)),
        (last - 3, filter_share),
        (last - 2, on_side(False, corners_done)),
    ]

    @pl.loop(0, 3 * cy)
    def _(j):
        for when, what in events:
            pl.when(j == when)(what)
        cell = j % cells
        basis_t[cell] = basis[:, pl.ds(pl.multiple_of(cell * slots, slots), slots)].T
        weigh(1, j)
        gather(0, j)
        weigh(0, (j + 1) % last)
        gather(1, j)

    for copy in halo.values():
        copy.wait_send()

    half = waves // 2
    two = 2 * slots

    def far_of(pair_of_cells, half_of):
        c0 = pair_of_cells * 2
        first = pl.multiple_of(half_of * half, half)
        left = jnp.concatenate([basis_t[pl.ds(c0, 2), :, pl.ds(k * waves + first, half)] for k in range(2)], axis=2)
        right = field[:, half_of].reshape(waves, feat)
        return jnp.dot(left.reshape(two, waves), right, preferred_element_type=jnp.float32)

    @pl.loop(0, cells // 2)
    def _(n):
        near = msg[pl.ds(2 * n, 2)].reshape(two, feat).astype(jnp.bfloat16)
        joined[n] = jnp.dot(near, wm_ref[...], preferred_element_type=jnp.float32)

    join_field()

    @pl.loop(0, cells // 2)
    def _(n):
        joined[n] += far_of(n, core)

    field_copy(core).wait_send()
    field_copy(1 - core).wait_recv()

    @pl.loop(0, cells // 2)
    def _(n):
        total = joined[n] + far_of(n, 1 - core)
        hidden = (total / (1.0 + jnp.exp(-total))).astype(jnp.bfloat16)
        result = jnp.dot(hidden, wo_ref[...], preferred_element_type=jnp.float32).reshape(2, slots, feat)
        c0 = 2 * n
        atom = wide[1 + c0 // cy, pl.ds(1 + c0 % cy, 2), 0].astype(jnp.float32)
        out_ref[pl.ds(c0, 2)] = (atom + result * out_mask[pl.ds(c0, 2)]).astype(jnp.bfloat16)


def radial_chain(gx, gy, gz, levels, reach, diagonal, p0, phi, slots):
    rows = gx.shape[0]
    sq = jnp.minimum(gx * gx + gy * gy + gz * gz, reach * reach)
    ratio = jnp.exp2(sq * lax.rsqrt(jnp.maximum(sq, 1e-30)))
    edge = reach * reach - sq
    val = edge * edge * jnp.exp2(sq * (-sharpness * math.log2(math.e) / reach**2))
    if diagonal is not None:
        row = lax.broadcasted_iota(jnp.int32, (rows, slots), 0) + diagonal
        lane = lax.broadcasted_iota(jnp.int32, (rows, slots), 1)
        val = jnp.concatenate([jnp.where(row == lane, 0.0, val[:, :slots]), val[:, slots:]], axis=1)
    second = ratio * ratio
    steps = [val.astype(jnp.bfloat16), (val * ratio).astype(jnp.bfloat16)]
    fourth = (second * second).astype(jnp.bfloat16)
    second = second.astype(jnp.bfloat16)
    for b in range(2, levels):
        steps.append(steps[b - 2] * second if b < 4 else steps[b - 4] * fourth)
    for b in range(levels):
        phi[b * slots + p0 : b * slots + p0 + rows] = steps[b]


def radial_terms(gx, gy, gz, levels, center, p0, phi, col, slots):
    rows = gx.shape[0]
    sq = jnp.minimum(gx * gx + gy * gy + gz * gz, 1.0)
    dist = sq * lax.rsqrt(jnp.maximum(sq, 1e-30))
    ratio = jnp.exp2(dist * (2.0 * sharpness / (levels - 1) * math.log2(math.e)))
    edge = 1.0 - sq
    val = edge * edge * jnp.exp2(sq * (-sharpness * math.log2(math.e)))
    if center:
        row = lax.broadcasted_iota(jnp.int32, val.shape, 0) + p0
        lane = lax.broadcasted_iota(jnp.int32, val.shape, 1)
        val = jnp.where(row == lane, 0.0, val)
    for b in range(levels):
        phi[b * slots + p0 : b * slots + p0 + rows, col : col + slots] = val.astype(jnp.bfloat16)
        if b + 1 < levels:
            val = val * ratio


def body(
    features,
    fractions,
    occupied,
    wave_index,
    radial_weight,
    ewald_mix,
    msg_weight,
    ewald_weight,
    out_weight,
):
    cx, cy, cz, slots, feat = features.shape
    levels, heads = radial_weight.shape
    cells = cx * cy * cz
    grid = [lax.axis_size("gx") * cx, lax.axis_size("gy") * cy, lax.axis_size("gz") * cz]
    devices = lax.axis_size("gx") * lax.axis_size("gy") * lax.axis_size("gz")
    waves = wave_index.shape[1]
    axes = ("gx", "gy", "gz")
    full = lambda shape: pl.BlockSpec(shape, lambda i: (0,) * len(shape))
    params = pltpu.CompilerParams(dimension_semantics=("arbitrary",), vmem_limit_bytes=56 * 2**20)

    fold_z = grid[2] == 2 and cz == 1
    counts = tuple(lax.axis_size(n) for n in axes)
    rows = waves // devices
    nx, ny = counts[:2]
    known = 2 < nx < 5 and ny == 4 and waves % 512 == 0 and cy % 2 == 0
    if fold_z and known and rows % 16 == 0 and ny > 2 and cx == 2 and cy > 2 and 4 * cells <= slots == 128:
        vmem = pl.BlockSpec(memory_space=pltpu.VMEM)
        dma = pltpu.SemaphoreType.DMA
        out = pl.pallas_call(
            functools.partial(layer_kernel, counts, levels),
            in_specs=[pl.BlockSpec(memory_space=pl.ANY)] * 9,
            out_specs=vmem,
            out_shape=pltpu.VMEM((cells, slots, feat), jnp.bfloat16),
            scratch_shapes=[
                pltpu.VMEM((cx, cy, slots, feat), jnp.bfloat16),
                pltpu.VMEM((cx, 3, cy, slots), jnp.bfloat16),
                pltpu.VMEM((cells, slots), jnp.int32),
                pltpu.VMEM(wave_index.shape, jnp.int32),
                pltpu.VMEM((heads, levels), jnp.float32),
                pltpu.VMEM(ewald_mix.shape, jnp.float32),
                pltpu.VMEM(ewald_weight.shape, jnp.bfloat16),
                pltpu.VMEM(msg_weight.shape, jnp.bfloat16),
                pltpu.VMEM(out_weight.shape, jnp.bfloat16),
                dma((9,)),
                pltpu.VMEM((cx + 2, cy + 2, 2, slots, feat), jnp.bfloat16),
                pltpu.VMEM((cx + 2, cy + 2, 2, 8, slots), jnp.bfloat16),
                pltpu.VMEM((slots, slots), jnp.float32),
                pltpu.VMEM((3, cells * slots), jnp.float32),
                pltpu.VMEM((cells, slots, feat), jnp.float32),
                pltpu.VMEM((waves, 8), jnp.float32),
                pltpu.VMEM((levels, feat), jnp.float32),
                pltpu.VMEM((cells, 3, slots, slots), jnp.float32),
                pltpu.VMEM((2, 3, levels * slots, 2 * slots), jnp.bfloat16),
                pltpu.VMEM((cells, slots, feat), jnp.float32),
                pltpu.VMEM((2 * waves, cells * slots), jnp.bfloat16),
                pltpu.VMEM((cells, slots, 2 * waves), jnp.bfloat16),
                pltpu.VMEM((cells // 2, 2 * slots, feat), jnp.float32),
                pltpu.VMEM((2, 2, nx, ny, rows, feat), jnp.bfloat16),
                pltpu.VMEM((2, nx, ny, rows, feat), jnp.bfloat16),
                pltpu.VMEM((2, nx, ny, rows, feat), jnp.bfloat16),
                pltpu.VMEM((ny, 2, nx, rows, feat), jnp.bfloat16),
                pltpu.VMEM((nx, 2, nx, rows, feat), jnp.bfloat16),
                pltpu.VMEM((2, 2, nx, ny, rows, feat), jnp.bfloat16),
                pltpu.SemaphoreType.REGULAR((2,)),
                dma((13, 2)),
                dma((13, 2)),
                dma((13, 2)),
                dma((13, 2)),
                dma((2,)),
                dma((2,)),
                dma((ny,)),
                dma((ny,)),
                dma((nx,)),
                dma((nx,)),
                dma((ny,)),
                dma((ny,)),
            ],
            compiler_params=pltpu.CompilerParams(
                collective_id=0, has_side_effects=True, vmem_limit_bytes=56 * 2**20
            ),
            name="layer",
        )(
            features.reshape(cx, cy, slots, feat),
            fractions.transpose(0, 2, 3, 1, 4).reshape(cx, 3, cy, slots),
            occupied.reshape(cells, slots),
            wave_index,
            radial_weight.T,
            ewald_mix,
            ewald_weight,
            msg_weight,
            out_weight,
        )
        return out.reshape(features.shape)

    masked = features * occupied[..., None].astype(jnp.bfloat16)
    frac = fractions.astype(jnp.float32)
    cell_feat = masked.reshape(cells, slots, feat)
    home = jnp.concatenate([frac, occupied[:, :, :, None, :].astype(jnp.float32)], axis=3)
    home = jnp.swapaxes(home.reshape(cells, 4, slots), 1, 2)

    start = [
        (lax.axis_index(n) * c + jnp.arange(c, dtype=jnp.int32)).astype(jnp.float32)
        for n, c in zip(axes, (cx, cy, cz))
    ]
    origin = jnp.stack(jnp.meshgrid(*start, indexing="ij"), axis=-1)[..., None]
    pos = (origin + frac).reshape(cells, 3, slots)
    lengths = jnp.array(grid, jnp.float32)
    index = wave_index.astype(jnp.float32)
    wave_vec = 2.0 * math.pi * index / lengths[:, None]
    wave_sq = jnp.sum(wave_vec * wave_vec, axis=0)
    damping = (
        strength
        * jnp.exp(-0.5 * smearing * wave_sq)
        / (wave_sq + screening)
        * (1.0 / math.sqrt(cells * slots * devices * waves))
    )
    wave_turn = (index / lengths[:, None]).T

    level = jnp.arange(levels, dtype=jnp.float32) / (levels - 1)
    wb = radial_weight * (jnp.exp(-sharpness * level * level) / math.sqrt(4.0 * slots))[:, None]
    wb = jnp.repeat(wb, feat // heads, axis=1)
    basis, struct = pl.pallas_call(
        basis_kernel,
        grid=(cells,),
        in_specs=[
            pl.BlockSpec((1, 3, slots), lambda i: (i, 0, 0)),
            full((waves, 3)),
            pl.BlockSpec((1, slots, feat), lambda i: (i, 0, 0)),
        ],
        out_specs=[pl.BlockSpec((1, 2 * waves, slots), lambda i: (i, 0, 0)), full((2 * waves, feat))],
        out_shape=[
            jax.ShapeDtypeStruct((cells, 2 * waves, slots), jnp.bfloat16),
            jax.ShapeDtypeStruct((2 * waves, feat), jnp.float32),
        ],
        compiler_params=params,
        name="basis",
    )(pos, wave_turn, cell_feat)

    wave_share = lax.psum_scatter(struct.reshape(2, waves, feat), axes, scatter_dimension=1, tiled=True)
    share_rows = wave_share.shape[1]
    share_damp = lax.dynamic_slice_in_dim(damping, lax.axis_index(axes) * share_rows, share_rows, 0)
    mixed = jnp.dot(wave_share.reshape(2 * share_rows, feat), ewald_mix, precision=lax.Precision.HIGHEST)
    filtered = (mixed.reshape(2, share_rows, feat) * share_damp[None, :, None]).astype(jnp.bfloat16)
    projected = jnp.dot(filtered, ewald_weight, preferred_element_type=jnp.float32).astype(jnp.bfloat16)
    field = lax.all_gather(projected, axes, axis=1, tiled=True).reshape(2 * waves, feat)

    wide_feat = widen(widen(masked, "gx", 0), "gy", 1)
    wide_geom = widen(widen(fractions, "gx", 0), "gy", 1)
    if fold_z:
        swap = [(0, 1), (1, 0)]
        wide_feat = jnp.concatenate([wide_feat, lax.ppermute(wide_feat, "gz", swap)], axis=2)
        wide_geom = jnp.concatenate([wide_geom, lax.ppermute(wide_geom, "gz", swap)], axis=2)
        near_z = 2
    else:
        wide_feat = widen(wide_feat, "gz", 2)
        wide_geom = widen(wide_geom, "gz", 2)
        near_z = 3
    wide_feat = jnp.stack([wide_feat[:, :, z : z + near_z] for z in range(cz)], axis=1)
    wide_geom = jnp.stack([wide_geom[:, :, z : z + near_z] for z in range(cz)], axis=1).astype(jnp.float32)
    messages = pl.pallas_call(
        functools.partial(message_kernel, cy, cz, fold_z, levels),
        grid=(cells,),
        in_specs=[
            pl.BlockSpec((1, slots, 4), lambda i: (i, 0, 0)),
            full(wide_feat.shape),
            full(wide_geom.shape),
            full(wb.shape),
        ],
        out_specs=pl.BlockSpec((1, slots, feat), lambda i: (i, 0, 0)),
        out_shape=jax.ShapeDtypeStruct((cells, slots, feat), jnp.bfloat16),
        scratch_shapes=[
            pltpu.VMEM((3, slots, slots), jnp.float32),
            pltpu.VMEM((3, levels * slots, 3 * near_z * slots), jnp.bfloat16),
            pltpu.VMEM((levels * slots, feat), jnp.float32),
        ],
        compiler_params=params,
        cost_estimate=pl.CostEstimate(
            flops=2 * cells * levels * slots * 9 * near_z * slots * feat, bytes_accessed=2**22, transcendentals=0
        ),
        name="messages",
    )(home, wide_feat, wide_geom, wb)

    out = pl.pallas_call(
        final_kernel,
        grid=(cells,),
        in_specs=[
            pl.BlockSpec((1, 2 * waves, slots), lambda i: (i, 0, 0)),
            full((2 * waves, feat)),
            pl.BlockSpec((1, slots, feat), lambda i: (i, 0, 0)),
            pl.BlockSpec((1, slots, feat), lambda i: (i, 0, 0)),
            pl.BlockSpec((1, slots, 4), lambda i: (i, 0, 0)),
            full((feat, feat)),
            full((feat, feat)),
        ],
        out_specs=pl.BlockSpec((1, slots, feat), lambda i: (i, 0, 0)),
        out_shape=jax.ShapeDtypeStruct((cells, slots, feat), jnp.bfloat16),
        compiler_params=params,
        name="final",
    )(basis, field, messages, cell_feat, home, msg_weight, out_weight)
    return out.reshape(features.shape)


def solution(mesh):
    cell = P("gx", "gy", "gz", None, None)
    in_specs = (cell, cell, P("gx", "gy", "gz", None), P(), P(), P(), P(), P(), P())
    return jax.shard_map(body, mesh=mesh, in_specs=in_specs, out_specs=cell, check_vma=False)
```

```python
import functools
import math

import jax
import jax.numpy as jnp
from jax import lax
from jax.experimental import pallas as pl
from jax.experimental.pallas import tpu as pltpu
from jax.sharding import PartitionSpec as P

sharpness = 16.0
smearing = 0.04
screening = 4.0
strength = 24.0

SIN_C = [(-1.0) ** k * math.pi ** (2 * k + 1) / math.factorial(2 * k + 1) for k in range(7)]
COS_C = [(-1.0) ** k * math.pi ** (2 * k) / math.factorial(2 * k) for k in range(7)]

SIN_P = [3.1415926401839953, -5.167710090331888, 2.550077659731212, -0.5982921594834444, 0.07765940825518475]
COS_P = [0.9999999534666585, -4.934792858674198, 4.058411914145813, -1.3318801611126891, 0.21969679833109643]


def poly(z, coefs):
    acc = jnp.full_like(z, coefs[-1])
    for c in coefs[-2::-1]:
        acc = acc * z + c
    return acc


def shifted(x, axis, dim, width):
    count, length = lax.axis_size(axis), x.shape[dim]
    up = [(i, (i + 1) % count) for i in range(count)]
    down = [(j, i) for i, j in up]
    last = lax.slice_in_dim(x, length - width, length, axis=dim)
    first = lax.slice_in_dim(x, 0, width, axis=dim)
    return lax.ppermute(last, axis, up), lax.ppermute(first, axis, down)


def widen(x, axis, dim):
    before, after = shifted(x, axis, dim, 1)
    return jnp.concatenate([before, x, after], axis=dim)


def message_kernel(cells_y, cells_z, fold_z, levels, home_ref, feat_ref, geom_ref, wb_ref, out_ref, hb, phi, acc):
    cell = pl.program_id(0)
    x = cell // (cells_y * cells_z)
    y = (cell // cells_z) % cells_y
    z = cell % cells_z
    slots = out_ref.shape[1]
    feat = out_ref.shape[2]
    near_z = feat_ref.shape[3]
    chunk = 32
    for a in range(3):
        hb[a] = jnp.broadcast_to(home_ref[0, :, a : a + 1], (slots, slots))
    for ox in range(3):
        for oy in range(3):
            for oz in range(near_z):
                g = geom_ref[x + ox, z, y + oy, oz]
                nx = g[0:1] + (ox - 1.0)
                ny = g[1:2] + (oy - 1.0)
                if fold_z:
                    nz = g[2:3]
                else:
                    nz = g[2:3] + (oz - 1.0)
                col = (oy * near_z + oz) * slots
                center = ox == 1 and oy == 1 and oz == (0 if fold_z else 1)
                for p0 in range(0, slots, chunk):
                    dx = nx - hb[0, p0 : p0 + chunk]
                    dy = ny - hb[1, p0 : p0 + chunk]
                    dz = nz - hb[2, p0 : p0 + chunk]
                    if fold_z and oz == 1:
                        dz = 1.0 - jnp.abs(dz)
                    radial_terms(dx, dy, dz, levels, center, p0, phi.at[ox], col, slots)
        rows = feat_ref[x + ox, z, pl.ds(y, 3)].reshape(3 * near_z * slots, feat)
        part = jnp.dot(phi[ox], rows, preferred_element_type=jnp.float32)
        if ox == 0:
            acc[...] = part
        elif ox == 1:
            acc[...] += part
    total = jnp.zeros((slots, feat), jnp.float32)
    for b in range(levels):
        both = acc[b * slots : (b + 1) * slots] + part[b * slots : (b + 1) * slots]
        total = total + both * wb_ref[b : b + 1]
    out_ref[0] = total.astype(jnp.bfloat16)


def basis_kernel(pos_ref, wave_ref, feat_ref, basis_ref, struct_ref):
    cell = pl.program_id(0)
    waves = wave_ref.shape[0]
    pos = pos_ref[0]
    chunk = 64
    for w0 in range(0, waves, chunk):
        wv = wave_ref[w0 : w0 + chunk]
        turns = wv[:, 0:1] * pos[0:1] + wv[:, 1:2] * pos[1:2] + wv[:, 2:3] * pos[2:3]
        u = turns - jnp.floor(turns + 0.5)
        q = u * u
        s = u * poly(q, SIN_C)
        c = poly(q, COS_C)
        basis_ref[0, w0 : w0 + chunk] = (1.0 - 2.0 * s * s).astype(jnp.bfloat16)
        basis_ref[0, waves + w0 : waves + w0 + chunk] = (2.0 * s * c).astype(jnp.bfloat16)
    part = jnp.dot(basis_ref[0], feat_ref[0], preferred_element_type=jnp.float32)

    @pl.when(cell == 0)
    def _():
        struct_ref[...] = part

    @pl.when(cell > 0)
    def _():
        struct_ref[...] += part


def final_kernel(basis_ref, grid_ref, msg_ref, feat_ref, home_ref, wm_ref, wo_ref, out_ref):
    far = lax.dot_general(
        basis_ref[0], grid_ref[...], (((0,), (0,)), ((), ())), preferred_element_type=jnp.float32
    )
    joined = far + jnp.dot(msg_ref[0], wm_ref[...], preferred_element_type=jnp.float32)
    hidden = (joined / (1.0 + jnp.exp(-joined))).astype(jnp.bfloat16)
    result = feat_ref[0].astype(jnp.float32) + jnp.dot(hidden, wo_ref[...], preferred_element_type=jnp.float32)
    out_ref[0] = (result * home_ref[0, :, 3:4]).astype(jnp.bfloat16)


def coords(index, counts):
    return (index // (counts[1] * counts[2]), (index // counts[2]) % counts[1], index % counts[2])


def layer_kernel(
    counts,
    levels,
    feat_in,
    frac_in,
    occ_in,
    index_in,
    radial_in,
    mix_in,
    we_in,
    wm_in,
    wo_in,
    out_ref,
    feat_ref,
    frac_ref,
    occ_ref,
    index_ref,
    radial_ref,
    mix_ref,
    we_ref,
    wm_ref,
    wo_ref,
    in_sem,
    wide,
    geom,
    rows_sc,
    pos_sc,
    out_mask,
    turn_cols,
    wb,
    hb,
    phi,
    msg,
    basis,
    basis_t,
    joined,
    struct,
    pair,
    chip_sum,
    parts,
    lines,
    field,
    token,
    halo_send,
    halo_recv,
    side_send,
    side_recv,
    pair_send,
    pair_recv,
    part_send,
    part_recv,
    line_send,
    line_recv,
    share_send,
    share_recv,
):
    cx, cy, slots, feat = feat_ref.shape
    cells = cx * cy
    waves = index_ref.shape[1]
    heads = radial_ref.shape[0]
    devices = counts[0] * counts[1] * counts[2]
    grid = (counts[0] * cx, counts[1] * cy, counts[2])
    rows = waves // devices
    at = (lax.axis_index("gx"), lax.axis_index("gy"), lax.axis_index("gz"))
    core = at[2]
    nx, ny = counts[0], counts[1]
    mesh_id = pl.DeviceIdType.MESH
    pad = geom.shape[3]
    reach = 2.0 * sharpness / (levels - 1) * math.log2(math.e)
    partner = (at[0], at[1], 1 - core)
    line_near = (at[0] + nx - 1) // nx + (2 * nx - 2 - at[0]) // nx
    bits = [1 << n for n in range(ny.bit_length() - 1)]

    def over_x(k):
        return ((at[0] + k + nx) % nx, at[1], core)

    def over_y(k):
        return (at[0], (at[1] + k + ny) % ny, core)

    def to_partner(src, dst, send, recv):
        return pltpu.make_async_remote_copy(
            src_ref=src, dst_ref=dst, send_sem=send, recv_sem=recv, device_id=partner, device_id_type=mesh_id
        )

    sources = [frac_in, occ_in, index_in, radial_in, feat_in, mix_in, we_in, wm_in, wo_in]
    places = [frac_ref, occ_ref, index_ref, radial_ref, feat_ref, mix_ref, we_ref, wm_ref, wo_ref]
    loads = [pltpu.make_async_copy(src, dst, in_sem.at[n]) for n, (src, dst) in enumerate(zip(sources, places))]
    for load in loads:
        load.start()

    barrier = pltpu.get_barrier_semaphore()

    def greet_line(sem):
        @pl.when(at[0] > 0)
        def _():
            pl.semaphore_signal(sem, inc=1, device_id=over_x(-1), device_id_type=mesh_id)

        @pl.when(at[0] < nx - 1)
        def _():
            pl.semaphore_signal(sem, inc=1, device_id=over_x(1), device_id_type=mesh_id)

    def greet_near(sem):
        greet_line(sem)
        for bit in bits:
            step = bit * (1 - 2 * (at[1] // bit % 2))
            pl.semaphore_signal(sem, inc=1, device_id=over_y(step), device_id_type=mesh_id)

    pl.semaphore_signal(barrier, inc=1, device_id=partner, device_id_type=mesh_id)
    greet_near(barrier)

    loads[0].wait()
    loads[1].wait()
    rows_sc[...] = jnp.zeros_like(rows_sc)
    for x in range(cx):
        for a in range(3):
            k = (x * 3 + a) * cy
            rows_sc[k : k + cy] = frac_ref[x, a].astype(jnp.float32)
    rows_sc[3 * cells : 4 * cells] = occ_ref[...].astype(jnp.float32)
    turned = rows_sc[...].T
    for x in range(cx):
        for y in range(cy):
            k = 3 * cells + x * cy + y
            out_mask[x * cy + y] = jnp.broadcast_to(turned[:, k : k + 1], (slots, feat))
    loads[4].wait()
    for x in range(cx):
        for y in range(cy):
            cell = x * cy + y
            ks = [(x * 3 + a) * cy + y for a in range(3)]
            wide[1 + x, 1 + y, 0] = feat_ref[x, y] * out_mask[cell].astype(jnp.bfloat16)
            own = jnp.concatenate([rows_sc[k : k + 1] for k in ks] + [jnp.zeros((pad - 3, slots), jnp.float32)])
            geom[1 + x, 1 + y, 0] = own.astype(jnp.bfloat16)

    class Both:
        def __init__(self, copies):
            self.copies = copies

        def start(self):
            for copy in self.copies:
                copy.start()

        def wait(self):
            for copy in self.copies:
                copy.wait()

        def wait_send(self):
            for copy in self.copies:
                copy.wait_send()

        def wait_recv(self):
            for copy in self.copies:
                copy.wait_recv()

    halo, side = {}, {}

    def link(key, device, source, target):
        n = len(side)
        refs = list(enumerate((geom, wide)))
        side[key] = Both(
            [to_partner(r.at[(*target, 0)], r.at[(*target, 1)], side_send.at[n, i], side_recv.at[n, i]) for i, r in refs]
        )
        if device is not None:
            halo[key] = Both(
                [
                    pltpu.make_async_remote_copy(
                        src_ref=r.at[(*source, 0)],
                        dst_ref=r.at[(*target, 0)],
                        send_sem=halo_send.at[n, i],
                        recv_sem=halo_recv.at[n, i],
                        device_id=device,
                        device_id_type=mesh_id,
                    )
                    for i, r in refs
                ]
            )

    one = lambda start: pl.ds(start, 1)
    for dy in (1, -1):
        xs = pl.ds(1, cx)
        link((0, dy), over_y(dy), (xs, one(cy if dy == 1 else 1)), (xs, one(0 if dy == 1 else cy + 1)))
    for dx in (1, -1):
        sx, tx = one(cx if dx == 1 else 1), one(0 if dx == 1 else cx + 1)
        for name, ys in (("low", one(1)), ("high", one(cy)), ("middle", pl.ds(2, cy - 2))):
            link((dx, name), over_x(dx), (sx, ys), (tx, ys))
        for dy in (1, -1):
            link((dx, dy), over_y(dy), (tx, one(cy if dy == 1 else 1)), (tx, one(0 if dy == 1 else cy + 1)))
    link((0, 0), None, None, (pl.ds(1, cx), pl.ds(1, cy)))

    def send_face(step):
        for name in ("low", "high", "middle"):
            halo[step, name].start()

    def send_faces(direct):
        for step, inside in ((1, at[0] < nx - 1), (-1, at[0] > 0)):
            pl.when(inside if direct else jnp.logical_not(inside))(functools.partial(send_face, step))

    def send_rows(direct):
        for step, near in ((1, at[1] % 2 == 0), (-1, at[1] % 2 == 1)):
            pl.when(near if direct else jnp.logical_not(near))(halo[0, step].start)

    def pass_token():
        pl.semaphore_wait(token.at[0], line_near + len(bits))
        greet_line(token.at[1])
        send_rows(False)

    def open_wrap():
        pl.semaphore_wait(token.at[1], line_near)
        send_faces(False)

    loads[2].wait()
    for w0 in range(0, waves, 128):
        part = [index_ref[a : a + 1, w0 : w0 + 128].astype(jnp.float32) * (1.0 / grid[a]) for a in range(3)]
        part = jnp.concatenate(part + [jnp.zeros((5, 128), jnp.float32)])
        turn_cols[w0 : w0 + 128] = part.T
    for x in range(cx):
        for y in range(cy):
            start = [at[0] * cx + x, at[1] * cy + y, core]
            cell = x * cy + y
            for a in range(3):
                k = (x * 3 + a) * cy + y
                pos_sc[a : a + 1, cell * slots : (cell + 1) * slots] = rows_sc[k : k + 1] + start[a].astype(jnp.float32)

    loads[3].wait()
    for x in range(cx):
        for y in range(cy):
            for a in range(3):
                k = (x * 3 + a) * cy + y
                hb[x * cy + y, a] = jnp.broadcast_to(turned[:, k : k + 1] * reach, (slots, slots))
    owner = lax.broadcasted_iota(jnp.int32, (heads, feat), 1) // (feat // heads)
    mine = owner == lax.broadcasted_iota(jnp.int32, (heads, feat), 0)
    for b in range(levels):
        level = b / (levels - 1)
        scale = math.exp(-sharpness * level * level) / math.sqrt(4.0 * slots) / reach**4
        column = jnp.broadcast_to(radial_ref[:, b : b + 1], (heads, feat)) * scale
        wb[b : b + 1] = jnp.sum(jnp.where(mine, column, 0.0), axis=0, keepdims=True)

    pl.semaphore_wait(barrier, 1 + line_near + len(bits))
    greet_near(token.at[0])
    send_rows(True)
    send_faces(True)
    side[0, 0].start()

    @pl.loop(0, cells // 2)
    def _(two):
        pl.when(two == cells // 8)(pass_token)
        pl.when(two == cells // 4 + 1)(open_wrap)
        lanes = pl.ds(pl.multiple_of(two * 2 * slots, 2 * slots), 2 * slots)
        pos = pos_sc[:, lanes]
        chunk = 32
        for w0 in range(0, waves, chunk):
            wv = turn_cols[w0 : w0 + chunk]
            turns = wv[:, 0:1] * pos[0:1] + wv[:, 1:2] * pos[1:2] + wv[:, 2:3] * pos[2:3]
            u = turns - jnp.round(turns)
            q = u * u
            s = u * poly(q, [v * math.sqrt(2.0) for v in SIN_P])
            c = poly(q, [v * math.sqrt(2.0) for v in COS_P])
            basis[w0 : w0 + chunk, lanes] = (1.0 - s * s).astype(jnp.bfloat16)
            basis[waves + w0 : waves + w0 + chunk, lanes] = (s * c).astype(jnp.bfloat16)

    atoms = wide[1 : 1 + cx, 1 : 1 + cy, 0].reshape(cells * slots, feat)
    struct[...] = (
        jnp.dot(basis[...], atoms, preferred_element_type=jnp.float32)
        .astype(jnp.bfloat16)
        .reshape(struct.shape)
    )
    swap = to_partner(struct.at[:, 1 - core], pair, pair_send.at[0], pair_recv.at[0])
    swap.start()

    for load in loads[5:]:
        load.wait()
    msg[...] = jnp.zeros_like(msg)

    def part_copy(k):
        return pltpu.make_async_remote_copy(
            src_ref=chip_sum.at[:, :, (at[1] + k) % ny],
            dst_ref=parts.at[k],
            send_sem=part_send.at[k],
            recv_sem=part_recv.at[k],
            device_id=over_y(k),
            device_id_type=mesh_id,
        )

    def line_copy(k, slot):
        return pltpu.make_async_remote_copy(
            src_ref=lines.at[at[0]],
            dst_ref=lines.at[slot],
            send_sem=line_send.at[k],
            recv_sem=line_recv.at[k],
            device_id=over_x(k),
            device_id_type=mesh_id,
        )

    def share_copy(k, slot):
        return pltpu.make_async_remote_copy(
            src_ref=field.at[:, core, :, at[1]],
            dst_ref=field.at[:, core, :, slot],
            send_sem=share_send.at[k],
            recv_sem=share_recv.at[k],
            device_id=over_y(k),
            device_id_type=mesh_id,
        )

    def field_copy(half):
        mine = field.at[:, half]
        return to_partner(mine, mine, pair_send.at[1], pair_recv.at[1])

    def sum_pair():
        swap.wait()
        both = struct[:, core].astype(jnp.float32) + pair[...].astype(jnp.float32)
        chip_sum[...] = both.astype(jnp.bfloat16)
        for k in range(1, ny):
            part_copy(k).start()

    def sum_parts():
        for k in range(1, ny):
            part_copy(k).wait()
        parts[0] = chip_sum[:, :, at[1]]
        lines[at[0]] = jnp.sum(parts[...].astype(jnp.float32), axis=0).astype(jnp.bfloat16)
        for k in range(1, nx):
            line_copy(k, at[0]).start()

    def filter_share():
        for k in range(1, nx):
            line_copy(k, (at[0] - k + nx) % nx).wait()
        total = jnp.sum(lines[...].astype(jnp.float32), axis=0).reshape(2 * nx * rows, feat)
        mixed = jnp.dot(total, mix_ref[...], precision=lax.Precision.HIGHEST, preferred_element_type=jnp.float32)
        vec = [turn_cols[pl.ds(((core * nx + x) * ny + at[1]) * rows, rows)] for x in range(nx)]
        vec = jnp.concatenate(vec) * (2.0 * math.pi)
        square = jnp.sum(vec * vec, axis=1, keepdims=True)
        damp = strength * jnp.exp(-0.5 * smearing * square) / (square + screening)
        damp = damp * (1.0 / math.sqrt(cells * slots * devices * waves))
        filtered = (mixed * jnp.concatenate([damp, damp])).astype(jnp.bfloat16)
        projected = jnp.dot(filtered, we_ref[...], preferred_element_type=jnp.float32)
        field[:, core, :, at[1]] = projected.astype(jnp.bfloat16).reshape(2, nx, rows, feat)
        for k in range(1, ny):
            share_copy(k, at[1]).start()

    def join_field():
        for k in range(1, ny):
            share_copy(k, (at[1] - k + ny) % ny).wait()
        field_copy(core).start()

    first_x = 1 - (at[0] + nx - 1) // nx

    def place(slot, j):
        late = j // (2 * cy)
        i = j % (2 * cy)
        turn = i // (cy // 2)
        x = (1 - late) * slot + late * (turn + (1 - 2 * turn) * first_x)
        y = ((1 - late) * (i // 2) + late * (2 * (i % (cy // 2)) + slot) + 1) % cy
        xi = (1 - late) * (1 + i % 2) + late * x * (cx + 1)
        return x, y, xi

    def weigh(slot, j):
        x, y, xi = place(slot, j)
        cell = x * cy + y
        step = xi - (x + 1)
        chunk = 16
        done = []
        for oy in range(3):
            near = [
                geom[xi, y + oy, oz].astype(jnp.float32) * reach for oz in range(2)
            ]
            near = jnp.concatenate(near, axis=1)
            nx = near[0:1] + step.astype(jnp.float32) * reach
            ny = near[1:2] + (oy - 1.0) * reach
            nz = near[2:3]
            for p0 in range(0, slots, chunk):
                row = nx
                if len(done) >= 2:
                    o, p = done[-2]
                    row = jnp.concatenate([nx[:, :slots] + jnp.minimum(phi[slot, o, p + 7 * slots : p + 7 * slots + 8, :slots].astype(jnp.float32)[0:1], 0.0), nx[:, slots:]], axis=1)
                done.append((oy, p0))
                gx, gy, gz = (
                    n - jnp.concatenate([hb[cell, a, p0 : p0 + chunk]] * 2, axis=1) for a, n in enumerate((row, ny, nz))
                )
                gz = jnp.concatenate([gz[:, :slots], reach - jnp.abs(gz[:, slots:])], axis=1)
                diagonal = p0 + step * slots if oy == 1 else None
                radial_chain(gx, gy, gz, levels, reach, diagonal, p0, phi.at[slot, oy], slots)

    def gather(slot, j):
        x, y, xi = place(slot, j)
        near = wide[xi, pl.ds(y, 3)].reshape(6 * slots, feat)
        left = jnp.concatenate([phi[slot, oy] for oy in range(3)], axis=1)
        part = jnp.dot(left, near, preferred_element_type=jnp.float32)
        total = msg[x * cy + y]
        for b in range(levels):
            total = total + part[b * slots : (b + 1) * slots] * wb[b : b + 1]
        msg[x * cy + y] = total

    def halo_in(*keys):
        for key in keys:
            halo[key].wait_recv()
            side[key].start()

    def side_in(*keys):
        for key in keys:
            side[key].wait()

    def face_in(step):
        halo_in((step, "low"))
        halo[step, -1].start()
        halo_in((step, "high"))
        halo[step, 1].start()

    def rest_in(step):
        halo_in((step, "middle"))

    def face_done(step):
        side_in((step, "low"), (step, "high"), (step, "middle"))

    def corners_in(step):
        halo_in((step, -1), (step, 1))

    def corners_done(step):
        side_in((step, -1), (step, 1))

    def on_side(first, what):
        def run():
            for step, then in ((1, first_x == 0), (-1, first_x == 1)):
                pl.when(then if first else jnp.logical_not(then))(functools.partial(what, step))

        return run

    side_in((0, 0))
    weigh(0, jnp.int32(0))

    ends = 2 * cy - 4
    last = 3 * cy
    events = [
        (1, sum_pair),
        (ends - 3, lambda: halo_in((0, -1), (0, 1))),
        (ends - 2, on_side(True, face_in)),
        (ends - 1, lambda: side_in((0, -1))),
        (ends - 1, on_side(True, rest_in)),
        (ends, sum_parts),
        (ends + 1, lambda: side_in((0, 1))),
        (ends + 1, on_side(True, corners_in)),
        (ends + 2, on_side(False, face_in)),
        (ends + 3, on_side(True, face_done)),
        (last - 4, on_side(True, corners_done)),
        (last - 4, on_side(False, rest_in)),
        (last - 3, on_side(False, corners_in)),
        (last - 3, on_side(False, face_done)),
        (last - 3, filter_share),
        (last - 2, on_side(False, corners_done)),
    ]

    @pl.loop(0, 3 * cy)
    def _(j):
        for when, what in events:
            pl.when(j == when)(what)
        cell = j % cells
        basis_t[cell] = basis[:, pl.ds(pl.multiple_of(cell * slots, slots), slots)].T
        weigh(1, j)
        gather(0, j)
        weigh(0, (j + 1) % last)
        gather(1, j)

    for copy in halo.values():
        copy.wait_send()

    half = waves // 2
    two = 2 * slots

    def far_of(pair_of_cells, half_of):
        c0 = pair_of_cells * 2
        first = pl.multiple_of(half_of * half, half)
        left = jnp.concatenate([basis_t[pl.ds(c0, 2), :, pl.ds(k * waves + first, half)] for k in range(2)], axis=2)
        right = field[:, half_of].reshape(waves, feat)
        return jnp.dot(left.reshape(two, waves), right, preferred_element_type=jnp.float32)

    @pl.loop(0, cells // 2, unroll=True)
    def _(n):
        near = msg[pl.ds(2 * n, 2)].reshape(two, feat).astype(jnp.bfloat16)
        joined[n] = jnp.dot(near, wm_ref[...], preferred_element_type=jnp.float32)

    join_field()

    @pl.loop(0, cells // 2, unroll=True)
    def _(n):
        joined[n] += far_of(n, core)

    field_copy(core).wait_send()
    field_copy(1 - core).wait_recv()

    @pl.loop(0, cells // 2, unroll=True)
    def _(n):
        total = joined[n] + far_of(n, 1 - core)
        hidden = (total / (1.0 + jnp.exp(-total))).astype(jnp.bfloat16)
        result = jnp.dot(hidden, wo_ref[...], preferred_element_type=jnp.float32).reshape(2, slots, feat)
        c0 = 2 * n
        atom = wide[1 + c0 // cy, pl.ds(1 + c0 % cy, 2), 0].astype(jnp.float32)
        out_ref[pl.ds(c0, 2)] = (atom + result * out_mask[pl.ds(c0, 2)]).astype(jnp.bfloat16)


def radial_chain(gx, gy, gz, levels, reach, diagonal, p0, phi, slots):
    rows = gx.shape[0]
    sq = jnp.minimum(gx * gx + gy * gy + gz * gz, reach * reach)
    ratio = jnp.exp2(sq * lax.rsqrt(jnp.maximum(sq, 1e-30)))
    edge = reach * reach - sq
    val = edge * edge * jnp.exp2(sq * (-sharpness * math.log2(math.e) / reach**2))
    if diagonal is not None:
        row = lax.broadcasted_iota(jnp.int32, (rows, slots), 0) + diagonal
        lane = lax.broadcasted_iota(jnp.int32, (rows, slots), 1)
        val = jnp.concatenate([jnp.where(row == lane, 0.0, val[:, :slots]), val[:, slots:]], axis=1)
    second = ratio * ratio
    steps = [val.astype(jnp.bfloat16), (val * ratio).astype(jnp.bfloat16)]
    fourth = (second * second).astype(jnp.bfloat16)
    second = second.astype(jnp.bfloat16)
    for b in range(2, levels):
        steps.append(steps[b - 2] * second if b < 4 else steps[b - 4] * fourth)
    for b in range(levels):
        phi[b * slots + p0 : b * slots + p0 + rows] = steps[b]


def radial_terms(gx, gy, gz, levels, center, p0, phi, col, slots):
    rows = gx.shape[0]
    sq = jnp.minimum(gx * gx + gy * gy + gz * gz, 1.0)
    dist = sq * lax.rsqrt(jnp.maximum(sq, 1e-30))
    ratio = jnp.exp2(dist * (2.0 * sharpness / (levels - 1) * math.log2(math.e)))
    edge = 1.0 - sq
    val = edge * edge * jnp.exp2(sq * (-sharpness * math.log2(math.e)))
    if center:
        row = lax.broadcasted_iota(jnp.int32, val.shape, 0) + p0
        lane = lax.broadcasted_iota(jnp.int32, val.shape, 1)
        val = jnp.where(row == lane, 0.0, val)
    for b in range(levels):
        phi[b * slots + p0 : b * slots + p0 + rows, col : col + slots] = val.astype(jnp.bfloat16)
        if b + 1 < levels:
            val = val * ratio


def body(
    features,
    fractions,
    occupied,
    wave_index,
    radial_weight,
    ewald_mix,
    msg_weight,
    ewald_weight,
    out_weight,
):
    cx, cy, cz, slots, feat = features.shape
    levels, heads = radial_weight.shape
    cells = cx * cy * cz
    grid = [lax.axis_size("gx") * cx, lax.axis_size("gy") * cy, lax.axis_size("gz") * cz]
    devices = lax.axis_size("gx") * lax.axis_size("gy") * lax.axis_size("gz")
    waves = wave_index.shape[1]
    axes = ("gx", "gy", "gz")
    full = lambda shape: pl.BlockSpec(shape, lambda i: (0,) * len(shape))
    params = pltpu.CompilerParams(dimension_semantics=("arbitrary",), vmem_limit_bytes=56 * 2**20)

    fold_z = grid[2] == 2 and cz == 1
    counts = tuple(lax.axis_size(n) for n in axes)
    rows = waves // devices
    nx, ny = counts[:2]
    known = 2 < nx < 5 and ny == 4 and waves % 512 == 0 and cy % 2 == 0
    if fold_z and known and rows % 16 == 0 and ny > 2 and cx == 2 and cy > 2 and 4 * cells <= slots == 128:
        vmem = pl.BlockSpec(memory_space=pltpu.VMEM)
        dma = pltpu.SemaphoreType.DMA
        out = pl.pallas_call(
            functools.partial(layer_kernel, counts, levels),
            in_specs=[pl.BlockSpec(memory_space=pl.ANY)] * 9,
            out_specs=vmem,
            out_shape=pltpu.VMEM((cells, slots, feat), jnp.bfloat16),
            scratch_shapes=[
                pltpu.VMEM((cx, cy, slots, feat), jnp.bfloat16),
                pltpu.VMEM((cx, 3, cy, slots), jnp.bfloat16),
                pltpu.VMEM((cells, slots), jnp.int32),
                pltpu.VMEM(wave_index.shape, jnp.int32),
                pltpu.VMEM((heads, levels), jnp.float32),
                pltpu.VMEM(ewald_mix.shape, jnp.float32),
                pltpu.VMEM(ewald_weight.shape, jnp.bfloat16),
                pltpu.VMEM(msg_weight.shape, jnp.bfloat16),
                pltpu.VMEM(out_weight.shape, jnp.bfloat16),
                dma((9,)),
                pltpu.VMEM((cx + 2, cy + 2, 2, slots, feat), jnp.bfloat16),
                pltpu.VMEM((cx + 2, cy + 2, 2, 8, slots), jnp.bfloat16),
                pltpu.VMEM((slots, slots), jnp.float32),
                pltpu.VMEM((3, cells * slots), jnp.float32),
                pltpu.VMEM((cells, slots, feat), jnp.float32),
                pltpu.VMEM((waves, 8), jnp.float32),
                pltpu.VMEM((levels, feat), jnp.float32),
                pltpu.VMEM((cells, 3, slots, slots), jnp.float32),
                pltpu.VMEM((2, 3, levels * slots, 2 * slots), jnp.bfloat16),
                pltpu.VMEM((cells, slots, feat), jnp.float32),
                pltpu.VMEM((2 * waves, cells * slots), jnp.bfloat16),
                pltpu.VMEM((cells, slots, 2 * waves), jnp.bfloat16),
                pltpu.VMEM((cells // 2, 2 * slots, feat), jnp.float32),
                pltpu.VMEM((2, 2, nx, ny, rows, feat), jnp.bfloat16),
                pltpu.VMEM((2, nx, ny, rows, feat), jnp.bfloat16),
                pltpu.VMEM((2, nx, ny, rows, feat), jnp.bfloat16),
                pltpu.VMEM((ny, 2, nx, rows, feat), jnp.bfloat16),
                pltpu.VMEM((nx, 2, nx, rows, feat), jnp.bfloat16),
                pltpu.VMEM((2, 2, nx, ny, rows, feat), jnp.bfloat16),
                pltpu.SemaphoreType.REGULAR((2,)),
                dma((13, 2)),
                dma((13, 2)),
                dma((13, 2)),
                dma((13, 2)),
                dma((2,)),
                dma((2,)),
                dma((ny,)),
                dma((ny,)),
                dma((nx,)),
                dma((nx,)),
                dma((ny,)),
                dma((ny,)),
            ],
            compiler_params=pltpu.CompilerParams(
                collective_id=0, has_side_effects=True, vmem_limit_bytes=56 * 2**20
            ),
            name="layer",
        )(
            features.reshape(cx, cy, slots, feat),
            fractions.transpose(0, 2, 3, 1, 4).reshape(cx, 3, cy, slots),
            occupied.reshape(cells, slots),
            wave_index,
            radial_weight.T,
            ewald_mix,
            ewald_weight,
            msg_weight,
            out_weight,
        )
        return out.reshape(features.shape)

    masked = features * occupied[..., None].astype(jnp.bfloat16)
    frac = fractions.astype(jnp.float32)
    cell_feat = masked.reshape(cells, slots, feat)
    home = jnp.concatenate([frac, occupied[:, :, :, None, :].astype(jnp.float32)], axis=3)
    home = jnp.swapaxes(home.reshape(cells, 4, slots), 1, 2)

    start = [
        (lax.axis_index(n) * c + jnp.arange(c, dtype=jnp.int32)).astype(jnp.float32)
        for n, c in zip(axes, (cx, cy, cz))
    ]
    origin = jnp.stack(jnp.meshgrid(*start, indexing="ij"), axis=-1)[..., None]
    pos = (origin + frac).reshape(cells, 3, slots)
    lengths = jnp.array(grid, jnp.float32)
    index = wave_index.astype(jnp.float32)
    wave_vec = 2.0 * math.pi * index / lengths[:, None]
    wave_sq = jnp.sum(wave_vec * wave_vec, axis=0)
    damping = (
        strength
        * jnp.exp(-0.5 * smearing * wave_sq)
        / (wave_sq + screening)
        * (1.0 / math.sqrt(cells * slots * devices * waves))
    )
    wave_turn = (index / lengths[:, None]).T

    level = jnp.arange(levels, dtype=jnp.float32) / (levels - 1)
    wb = radial_weight * (jnp.exp(-sharpness * level * level) / math.sqrt(4.0 * slots))[:, None]
    wb = jnp.repeat(wb, feat // heads, axis=1)
    basis, struct = pl.pallas_call(
        basis_kernel,
        grid=(cells,),
        in_specs=[
            pl.BlockSpec((1, 3, slots), lambda i: (i, 0, 0)),
            full((waves, 3)),
            pl.BlockSpec((1, slots, feat), lambda i: (i, 0, 0)),
        ],
        out_specs=[pl.BlockSpec((1, 2 * waves, slots), lambda i: (i, 0, 0)), full((2 * waves, feat))],
        out_shape=[
            jax.ShapeDtypeStruct((cells, 2 * waves, slots), jnp.bfloat16),
            jax.ShapeDtypeStruct((2 * waves, feat), jnp.float32),
        ],
        compiler_params=params,
        name="basis",
    )(pos, wave_turn, cell_feat)

    wave_share = lax.psum_scatter(struct.reshape(2, waves, feat), axes, scatter_dimension=1, tiled=True)
    share_rows = wave_share.shape[1]
    share_damp = lax.dynamic_slice_in_dim(damping, lax.axis_index(axes) * share_rows, share_rows, 0)
    mixed = jnp.dot(wave_share.reshape(2 * share_rows, feat), ewald_mix, precision=lax.Precision.HIGHEST)
    filtered = (mixed.reshape(2, share_rows, feat) * share_damp[None, :, None]).astype(jnp.bfloat16)
    projected = jnp.dot(filtered, ewald_weight, preferred_element_type=jnp.float32).astype(jnp.bfloat16)
    field = lax.all_gather(projected, axes, axis=1, tiled=True).reshape(2 * waves, feat)

    wide_feat = widen(widen(masked, "gx", 0), "gy", 1)
    wide_geom = widen(widen(fractions, "gx", 0), "gy", 1)
    if fold_z:
        swap = [(0, 1), (1, 0)]
        wide_feat = jnp.concatenate([wide_feat, lax.ppermute(wide_feat, "gz", swap)], axis=2)
        wide_geom = jnp.concatenate([wide_geom, lax.ppermute(wide_geom, "gz", swap)], axis=2)
        near_z = 2
    else:
        wide_feat = widen(wide_feat, "gz", 2)
        wide_geom = widen(wide_geom, "gz", 2)
        near_z = 3
    wide_feat = jnp.stack([wide_feat[:, :, z : z + near_z] for z in range(cz)], axis=1)
    wide_geom = jnp.stack([wide_geom[:, :, z : z + near_z] for z in range(cz)], axis=1).astype(jnp.float32)
    messages = pl.pallas_call(
        functools.partial(message_kernel, cy, cz, fold_z, levels),
        grid=(cells,),
        in_specs=[
            pl.BlockSpec((1, slots, 4), lambda i: (i, 0, 0)),
            full(wide_feat.shape),
            full(wide_geom.shape),
            full(wb.shape),
        ],
        out_specs=pl.BlockSpec((1, slots, feat), lambda i: (i, 0, 0)),
        out_shape=jax.ShapeDtypeStruct((cells, slots, feat), jnp.bfloat16),
        scratch_shapes=[
            pltpu.VMEM((3, slots, slots), jnp.float32),
            pltpu.VMEM((3, levels * slots, 3 * near_z * slots), jnp.bfloat16),
            pltpu.VMEM((levels * slots, feat), jnp.float32),
        ],
        compiler_params=params,
        cost_estimate=pl.CostEstimate(
            flops=2 * cells * levels * slots * 9 * near_z * slots * feat, bytes_accessed=2**22, transcendentals=0
        ),
        name="messages",
    )(home, wide_feat, wide_geom, wb)

    out = pl.pallas_call(
        final_kernel,
        grid=(cells,),
        in_specs=[
            pl.BlockSpec((1, 2 * waves, slots), lambda i: (i, 0, 0)),
            full((2 * waves, feat)),
            pl.BlockSpec((1, slots, feat), lambda i: (i, 0, 0)),
            pl.BlockSpec((1, slots, feat), lambda i: (i, 0, 0)),
            pl.BlockSpec((1, slots, 4), lambda i: (i, 0, 0)),
            full((feat, feat)),
            full((feat, feat)),
        ],
        out_specs=pl.BlockSpec((1, slots, feat), lambda i: (i, 0, 0)),
        out_shape=jax.ShapeDtypeStruct((cells, slots, feat), jnp.bfloat16),
        compiler_params=params,
        name="final",
    )(basis, field, messages, cell_feat, home, msg_weight, out_weight)
    return out.reshape(features.shape)


def solution(mesh):
    cell = P("gx", "gy", "gz", None, None)
    in_specs = (cell, cell, P("gx", "gy", "gz", None), P(), P(), P(), P(), P(), P())
    return jax.shard_map(body, mesh=mesh, in_specs=in_specs, out_specs=cell, check_vma=False)
```

```python
import functools
import math

import jax
import jax.numpy as jnp
from jax import lax
from jax.experimental import pallas as pl
from jax.experimental.pallas import tpu as pltpu
from jax.sharding import PartitionSpec as P

sharpness = 16.0
smearing = 0.04
screening = 4.0
strength = 24.0

SIN_C = [(-1.0) ** k * math.pi ** (2 * k + 1) / math.factorial(2 * k + 1) for k in range(7)]
COS_C = [(-1.0) ** k * math.pi ** (2 * k) / math.factorial(2 * k) for k in range(7)]

SIN_P = [3.1415926401839953, -5.167710090331888, 2.550077659731212, -0.5982921594834444, 0.07765940825518475]
COS_P = [0.9999999534666585, -4.934792858674198, 4.058411914145813, -1.3318801611126891, 0.21969679833109643]


def poly(z, coefs):
    acc = jnp.full_like(z, coefs[-1])
    for c in coefs[-2::-1]:
        acc = acc * z + c
    return acc


def shifted(x, axis, dim, width):
    count, length = lax.axis_size(axis), x.shape[dim]
    up = [(i, (i + 1) % count) for i in range(count)]
    down = [(j, i) for i, j in up]
    last = lax.slice_in_dim(x, length - width, length, axis=dim)
    first = lax.slice_in_dim(x, 0, width, axis=dim)
    return lax.ppermute(last, axis, up), lax.ppermute(first, axis, down)


def widen(x, axis, dim):
    before, after = shifted(x, axis, dim, 1)
    return jnp.concatenate([before, x, after], axis=dim)


def message_kernel(cells_y, cells_z, fold_z, levels, home_ref, feat_ref, geom_ref, wb_ref, out_ref, hb, phi, acc):
    cell = pl.program_id(0)
    x = cell // (cells_y * cells_z)
    y = (cell // cells_z) % cells_y
    z = cell % cells_z
    slots = out_ref.shape[1]
    feat = out_ref.shape[2]
    near_z = feat_ref.shape[3]
    chunk = 32
    for a in range(3):
        hb[a] = jnp.broadcast_to(home_ref[0, :, a : a + 1], (slots, slots))
    for ox in range(3):
        for oy in range(3):
            for oz in range(near_z):
                g = geom_ref[x + ox, z, y + oy, oz]
                nx = g[0:1] + (ox - 1.0)
                ny = g[1:2] + (oy - 1.0)
                if fold_z:
                    nz = g[2:3]
                else:
                    nz = g[2:3] + (oz - 1.0)
                col = (oy * near_z + oz) * slots
                center = ox == 1 and oy == 1 and oz == (0 if fold_z else 1)
                for p0 in range(0, slots, chunk):
                    dx = nx - hb[0, p0 : p0 + chunk]
                    dy = ny - hb[1, p0 : p0 + chunk]
                    dz = nz - hb[2, p0 : p0 + chunk]
                    if fold_z and oz == 1:
                        dz = 1.0 - jnp.abs(dz)
                    radial_terms(dx, dy, dz, levels, center, p0, phi.at[ox], col, slots)
        rows = feat_ref[x + ox, z, pl.ds(y, 3)].reshape(3 * near_z * slots, feat)
        part = jnp.dot(phi[ox], rows, preferred_element_type=jnp.float32)
        if ox == 0:
            acc[...] = part
        elif ox == 1:
            acc[...] += part
    total = jnp.zeros((slots, feat), jnp.float32)
    for b in range(levels):
        both = acc[b * slots : (b + 1) * slots] + part[b * slots : (b + 1) * slots]
        total = total + both * wb_ref[b : b + 1]
    out_ref[0] = total.astype(jnp.bfloat16)


def basis_kernel(pos_ref, wave_ref, feat_ref, basis_ref, struct_ref):
    cell = pl.program_id(0)
    waves = wave_ref.shape[0]
    pos = pos_ref[0]
    chunk = 64
    for w0 in range(0, waves, chunk):
        wv = wave_ref[w0 : w0 + chunk]
        turns = wv[:, 0:1] * pos[0:1] + wv[:, 1:2] * pos[1:2] + wv[:, 2:3] * pos[2:3]
        u = turns - jnp.floor(turns + 0.5)
        q = u * u
        s = u * poly(q, SIN_C)
        c = poly(q, COS_C)
        basis_ref[0, w0 : w0 + chunk] = (1.0 - 2.0 * s * s).astype(jnp.bfloat16)
        basis_ref[0, waves + w0 : waves + w0 + chunk] = (2.0 * s * c).astype(jnp.bfloat16)
    part = jnp.dot(basis_ref[0], feat_ref[0], preferred_element_type=jnp.float32)

    @pl.when(cell == 0)
    def _():
        struct_ref[...] = part

    @pl.when(cell > 0)
    def _():
        struct_ref[...] += part


def final_kernel(basis_ref, grid_ref, msg_ref, feat_ref, home_ref, wm_ref, wo_ref, out_ref):
    far = lax.dot_general(
        basis_ref[0], grid_ref[...], (((0,), (0,)), ((), ())), preferred_element_type=jnp.float32
    )
    joined = far + jnp.dot(msg_ref[0], wm_ref[...], preferred_element_type=jnp.float32)
    hidden = (joined / (1.0 + jnp.exp(-joined))).astype(jnp.bfloat16)
    result = feat_ref[0].astype(jnp.float32) + jnp.dot(hidden, wo_ref[...], preferred_element_type=jnp.float32)
    out_ref[0] = (result * home_ref[0, :, 3:4]).astype(jnp.bfloat16)


def coords(index, counts):
    return (index // (counts[1] * counts[2]), (index // counts[2]) % counts[1], index % counts[2])


def layer_kernel(
    counts,
    levels,
    feat_in,
    frac_in,
    occ_in,
    index_in,
    radial_in,
    mix_in,
    we_in,
    wm_in,
    wo_in,
    out_ref,
    feat_ref,
    frac_ref,
    occ_ref,
    index_ref,
    radial_ref,
    mix_ref,
    we_ref,
    wm_ref,
    wo_ref,
    in_sem,
    wide,
    geom,
    rows_sc,
    pos_sc,
    out_mask,
    turn_cols,
    wb,
    hb,
    phi,
    msg,
    basis,
    basis_t,
    joined,
    struct,
    pair,
    chip_sum,
    parts,
    lines,
    field,
    token,
    halo_send,
    halo_recv,
    side_send,
    side_recv,
    pair_send,
    pair_recv,
    part_send,
    part_recv,
    line_send,
    line_recv,
    share_send,
    share_recv,
):
    cx, cy, slots, feat = feat_ref.shape
    cells = cx * cy
    waves = index_ref.shape[1]
    heads = radial_ref.shape[0]
    devices = counts[0] * counts[1] * counts[2]
    grid = (counts[0] * cx, counts[1] * cy, counts[2])
    rows = waves // devices
    at = (lax.axis_index("gx"), lax.axis_index("gy"), lax.axis_index("gz"))
    core = at[2]
    nx, ny = counts[0], counts[1]
    mesh_id = pl.DeviceIdType.MESH
    pad = geom.shape[3]
    reach = 2.0 * sharpness / (levels - 1) * math.log2(math.e)
    partner = (at[0], at[1], 1 - core)
    line_near = (at[0] + nx - 1) // nx + (2 * nx - 2 - at[0]) // nx
    bits = [1 << n for n in range(ny.bit_length() - 1)]

    def over_x(k):
        return ((at[0] + k + nx) % nx, at[1], core)

    def over_y(k):
        return (at[0], (at[1] + k + ny) % ny, core)

    def to_partner(src, dst, send, recv):
        return pltpu.make_async_remote_copy(
            src_ref=src, dst_ref=dst, send_sem=send, recv_sem=recv, device_id=partner, device_id_type=mesh_id
        )

    sources = [frac_in, occ_in, index_in, radial_in, feat_in, mix_in, we_in, wm_in, wo_in]
    places = [frac_ref, occ_ref, index_ref, radial_ref, feat_ref, mix_ref, we_ref, wm_ref, wo_ref]
    loads = [pltpu.make_async_copy(src, dst, in_sem.at[n]) for n, (src, dst) in enumerate(zip(sources, places))]
    for load in loads:
        load.start()

    barrier = pltpu.get_barrier_semaphore()

    def greet_line(sem):
        @pl.when(at[0] > 0)
        def _():
            pl.semaphore_signal(sem, inc=1, device_id=over_x(-1), device_id_type=mesh_id)

        @pl.when(at[0] < nx - 1)
        def _():
            pl.semaphore_signal(sem, inc=1, device_id=over_x(1), device_id_type=mesh_id)

    def greet_near(sem):
        greet_line(sem)
        for bit in bits:
            step = bit * (1 - 2 * (at[1] // bit % 2))
            pl.semaphore_signal(sem, inc=1, device_id=over_y(step), device_id_type=mesh_id)

    pl.semaphore_signal(barrier, inc=1, device_id=partner, device_id_type=mesh_id)
    greet_near(barrier)

    loads[0].wait()
    loads[1].wait()
    rows_sc[...] = jnp.zeros_like(rows_sc)
    for x in range(cx):
        for a in range(3):
            k = (x * 3 + a) * cy
            rows_sc[k : k + cy] = frac_ref[x, a].astype(jnp.float32)
    rows_sc[3 * cells : 4 * cells] = occ_ref[...].astype(jnp.float32)
    turned = rows_sc[...].T
    for x in range(cx):
        for y in range(cy):
            k = 3 * cells + x * cy + y
            out_mask[x * cy + y] = jnp.broadcast_to(turned[:, k : k + 1], (slots, feat))
    loads[4].wait()
    for x in range(cx):
        for y in range(cy):
            cell = x * cy + y
            ks = [(x * 3 + a) * cy + y for a in range(3)]
            wide[1 + x, 1 + y, 0] = feat_ref[x, y] * out_mask[cell].astype(jnp.bfloat16)
            own = jnp.concatenate([rows_sc[k : k + 1] for k in ks] + [jnp.zeros((pad - 3, slots), jnp.float32)])
            geom[1 + x, 1 + y, 0] = own.astype(jnp.bfloat16)

    class Both:
        def __init__(self, copies):
            self.copies = copies

        def start(self):
            for copy in self.copies:
                copy.start()

        def wait(self):
            for copy in self.copies:
                copy.wait()

        def wait_send(self):
            for copy in self.copies:
                copy.wait_send()

        def wait_recv(self):
            for copy in self.copies:
                copy.wait_recv()

    halo, side = {}, {}

    def link(key, device, source, target):
        n = len(side)
        refs = list(enumerate((geom, wide)))
        side[key] = Both(
            [to_partner(r.at[(*target, 0)], r.at[(*target, 1)], side_send.at[n, i], side_recv.at[n, i]) for i, r in refs]
        )
        if device is not None:
            halo[key] = Both(
                [
                    pltpu.make_async_remote_copy(
                        src_ref=r.at[(*source, 0)],
                        dst_ref=r.at[(*target, 0)],
                        send_sem=halo_send.at[n, i],
                        recv_sem=halo_recv.at[n, i],
                        device_id=device,
                        device_id_type=mesh_id,
                    )
                    for i, r in refs
                ]
            )

    one = lambda start: pl.ds(start, 1)
    for dy in (1, -1):
        xs = pl.ds(1, cx)
        link((0, dy), over_y(dy), (xs, one(cy if dy == 1 else 1)), (xs, one(0 if dy == 1 else cy + 1)))
    for dx in (1, -1):
        sx, tx = one(cx if dx == 1 else 1), one(0 if dx == 1 else cx + 1)
        for name, ys in (("low", one(1)), ("high", one(cy)), ("middle", pl.ds(2, cy - 2))):
            link((dx, name), over_x(dx), (sx, ys), (tx, ys))
        for dy in (1, -1):
            link((dx, dy), over_y(dy), (tx, one(cy if dy == 1 else 1)), (tx, one(0 if dy == 1 else cy + 1)))
    link((0, 0), None, None, (pl.ds(1, cx), pl.ds(1, cy)))

    def send_face(step):
        for name in ("low", "high", "middle"):
            halo[step, name].start()

    def send_faces(direct):
        for step, inside in ((1, at[0] < nx - 1), (-1, at[0] > 0)):
            pl.when(inside if direct else jnp.logical_not(inside))(functools.partial(send_face, step))

    def send_rows(direct):
        for step, near in ((1, at[1] % 2 == 0), (-1, at[1] % 2 == 1)):
            pl.when(near if direct else jnp.logical_not(near))(halo[0, step].start)

    def pass_token():
        pl.semaphore_wait(token.at[0], line_near + len(bits))
        greet_line(token.at[1])
        send_rows(False)

    def open_wrap():
        pl.semaphore_wait(token.at[1], line_near)
        send_faces(False)

    loads[2].wait()
    for w0 in range(0, waves, 128):
        part = [index_ref[a : a + 1, w0 : w0 + 128].astype(jnp.float32) * (1.0 / grid[a]) for a in range(3)]
        part = jnp.concatenate(part + [jnp.zeros((5, 128), jnp.float32)])
        turn_cols[w0 : w0 + 128] = part.T
    for x in range(cx):
        for y in range(cy):
            start = [at[0] * cx + x, at[1] * cy + y, core]
            cell = x * cy + y
            for a in range(3):
                k = (x * 3 + a) * cy + y
                pos_sc[a : a + 1, cell * slots : (cell + 1) * slots] = rows_sc[k : k + 1] + start[a].astype(jnp.float32)

    loads[3].wait()
    for x in range(cx):
        for y in range(cy):
            for a in range(3):
                k = (x * 3 + a) * cy + y
                hb[x * cy + y, a] = jnp.broadcast_to(turned[:, k : k + 1] * reach, (slots, slots))
    owner = lax.broadcasted_iota(jnp.int32, (heads, feat), 1) // (feat // heads)
    mine = owner == lax.broadcasted_iota(jnp.int32, (heads, feat), 0)
    for b in range(levels):
        level = b / (levels - 1)
        scale = math.exp(-sharpness * level * level) / math.sqrt(4.0 * slots) / reach**4
        column = jnp.broadcast_to(radial_ref[:, b : b + 1], (heads, feat)) * scale
        wb[b : b + 1] = jnp.sum(jnp.where(mine, column, 0.0), axis=0, keepdims=True)

    pl.semaphore_wait(barrier, 1 + line_near + len(bits))
    greet_near(token.at[0])
    side[0, 0].start()
    send_rows(True)
    send_faces(True)

    @pl.loop(0, cells // 2)
    def _(two):
        pl.when(two == cells // 8)(pass_token)
        pl.when(two == cells // 4 + 1)(open_wrap)
        lanes = pl.ds(pl.multiple_of(two * 2 * slots, 2 * slots), 2 * slots)
        pos = pos_sc[:, lanes]
        chunk = 32
        for w0 in range(0, waves, chunk):
            wv = turn_cols[w0 : w0 + chunk]
            turns = wv[:, 0:1] * pos[0:1] + wv[:, 1:2] * pos[1:2] + wv[:, 2:3] * pos[2:3]
            u = turns - jnp.round(turns)
            q = u * u
            s = u * poly(q, [v * math.sqrt(2.0) for v in SIN_P])
            c = poly(q, [v * math.sqrt(2.0) for v in COS_P])
            basis[w0 : w0 + chunk, lanes] = (1.0 - s * s).astype(jnp.bfloat16)
            basis[waves + w0 : waves + w0 + chunk, lanes] = (s * c).astype(jnp.bfloat16)

    atoms = wide[1 : 1 + cx, 1 : 1 + cy, 0].reshape(cells * slots, feat)
    struct[...] = (
        jnp.dot(basis[...], atoms, preferred_element_type=jnp.float32)
        .astype(jnp.bfloat16)
        .reshape(struct.shape)
    )
    swap = to_partner(struct.at[:, 1 - core], pair, pair_send.at[0], pair_recv.at[0])
    swap.start()

    for load in loads[5:]:
        load.wait()
    msg[...] = jnp.zeros_like(msg)

    def part_copy(k):
        return pltpu.make_async_remote_copy(
            src_ref=chip_sum.at[:, :, (at[1] + k) % ny],
            dst_ref=parts.at[k],
            send_sem=part_send.at[k],
            recv_sem=part_recv.at[k],
            device_id=over_y(k),
            device_id_type=mesh_id,
        )

    def line_copy(k, slot):
        return pltpu.make_async_remote_copy(
            src_ref=lines.at[at[0]],
            dst_ref=lines.at[slot],
            send_sem=line_send.at[k],
            recv_sem=line_recv.at[k],
            device_id=over_x(k),
            device_id_type=mesh_id,
        )

    def share_copy(k, slot):
        return pltpu.make_async_remote_copy(
            src_ref=field.at[:, core, :, at[1]],
            dst_ref=field.at[:, core, :, slot],
            send_sem=share_send.at[k],
            recv_sem=share_recv.at[k],
            device_id=over_y(k),
            device_id_type=mesh_id,
        )

    def field_copy(half):
        mine = field.at[:, half]
        return to_partner(mine, mine, pair_send.at[1], pair_recv.at[1])

    def sum_pair():
        swap.wait()
        both = struct[:, core].astype(jnp.float32) + pair[...].astype(jnp.float32)
        chip_sum[...] = both.astype(jnp.bfloat16)
        for k in range(1, ny):
            part_copy(k).start()

    def sum_parts():
        for k in range(1, ny):
            part_copy(k).wait()
        parts[0] = chip_sum[:, :, at[1]]
        lines[at[0]] = jnp.sum(parts[...].astype(jnp.float32), axis=0).astype(jnp.bfloat16)
        for k in range(1, nx):
            line_copy(k, at[0]).start()

    def filter_share():
        for k in range(1, nx):
            line_copy(k, (at[0] - k + nx) % nx).wait()
        total = jnp.sum(lines[...].astype(jnp.float32), axis=0).reshape(2 * nx * rows, feat)
        mixed = jnp.dot(total, mix_ref[...], precision=lax.Precision.HIGHEST, preferred_element_type=jnp.float32)
        vec = [turn_cols[pl.ds(((core * nx + x) * ny + at[1]) * rows, rows)] for x in range(nx)]
        vec = jnp.concatenate(vec) * (2.0 * math.pi)
        square = jnp.sum(vec * vec, axis=1, keepdims=True)
        damp = strength * jnp.exp(-0.5 * smearing * square) / (square + screening)
        damp = damp * (1.0 / math.sqrt(cells * slots * devices * waves))
        filtered = (mixed * jnp.concatenate([damp, damp])).astype(jnp.bfloat16)
        projected = jnp.dot(filtered, we_ref[...], preferred_element_type=jnp.float32)
        field[:, core, :, at[1]] = projected.astype(jnp.bfloat16).reshape(2, nx, rows, feat)
        for k in range(1, ny):
            share_copy(k, at[1]).start()

    def join_field():
        for k in range(1, ny):
            share_copy(k, (at[1] - k + ny) % ny).wait()
        field_copy(core).start()

    first_x = 1 - (at[0] + nx - 1) // nx

    def place(slot, j):
        late = j // (2 * cy)
        i = j % (2 * cy)
        turn = i // (cy // 2)
        x = (1 - late) * slot + late * (turn + (1 - 2 * turn) * first_x)
        y = ((1 - late) * (i // 2) + late * (2 * (i % (cy // 2)) + slot) + 1) % cy
        xi = (1 - late) * (1 + i % 2) + late * x * (cx + 1)
        return x, y, xi

    def weigh(slot, j):
        x, y, xi = place(slot, j)
        cell = x * cy + y
        step = xi - (x + 1)
        chunk = 32
        done = []
        for oy in range(3):
            near = [
                geom[xi, y + oy, oz].astype(jnp.float32) * reach for oz in range(2)
            ]
            near = jnp.concatenate(near, axis=1)
            nx = near[0:1] + step.astype(jnp.float32) * reach
            ny = near[1:2] + (oy - 1.0) * reach
            nz = near[2:3]
            for p0 in range(0, slots, chunk):
                row = nx
                if len(done) >= 1:
                    o, p = done[-1]
                    row = jnp.concatenate([nx[:, :slots] + jnp.minimum(phi[slot, o, p + 7 * slots : p + 7 * slots + 8, :slots].astype(jnp.float32)[0:1], 0.0), nx[:, slots:]], axis=1)
                done.append((oy, p0))
                gx, gy, gz = (
                    n - jnp.concatenate([hb[cell, a, p0 : p0 + chunk]] * 2, axis=1) for a, n in enumerate((row, ny, nz))
                )
                gz = jnp.concatenate([gz[:, :slots], reach - jnp.abs(gz[:, slots:])], axis=1)
                diagonal = p0 + step * slots if oy == 1 else None
                radial_chain(gx, gy, gz, levels, reach, diagonal, p0, phi.at[slot, oy], slots)

    def gather(slot, j):
        x, y, xi = place(slot, j)
        near = wide[xi, pl.ds(y, 3)].reshape(6 * slots, feat)
        left = jnp.concatenate([phi[slot, oy] for oy in range(3)], axis=1)
        part = jnp.dot(left, near, preferred_element_type=jnp.float32)
        total = msg[x * cy + y]
        for b in range(levels):
            total = total + part[b * slots : (b + 1) * slots] * wb[b : b + 1]
        msg[x * cy + y] = total

    def halo_in(*keys):
        for key in keys:
            halo[key].wait_recv()
            side[key].start()

    def side_in(*keys):
        for key in keys:
            side[key].wait()

    def face_in(step):
        halo_in((step, "low"))
        halo[step, -1].start()
        halo_in((step, "high"))
        halo[step, 1].start()

    def rest_in(step):
        halo_in((step, "middle"))

    def face_done(step):
        side_in((step, "low"), (step, "high"), (step, "middle"))

    def corners_in(step):
        halo_in((step, -1), (step, 1))

    def corners_done(step):
        side_in((step, -1), (step, 1))

    def on_side(first, what):
        def run():
            for step, then in ((1, first_x == 0), (-1, first_x == 1)):
                pl.when(then if first else jnp.logical_not(then))(functools.partial(what, step))

        return run

    side_in((0, 0))
    weigh(0, jnp.int32(0))

    ends = 2 * cy - 4
    last = 3 * cy
    events = [
        (1, sum_pair),
        (ends - 3, lambda: halo_in((0, -1), (0, 1))),
        (ends - 2, on_side(True, face_in)),
        (ends - 1, lambda: side_in((0, -1))),
        (ends - 1, on_side(True, rest_in)),
        (ends, sum_parts),
        (ends + 1, lambda: side_in((0, 1))),
        (ends + 1, on_side(True, corners_in)),
        (ends + 2, on_side(False, face_in)),
        (ends + 3, on_side(True, face_done)),
        (last - 4, on_side(True, corners_done)),
        (last - 4, on_side(False, rest_in)),
        (last - 3, on_side(False, corners_in)),
        (last - 3, on_side(False, face_done)),
        (last - 3, filter_share),
        (last - 2, on_side(False, corners_done)),
    ]

    def run_all(due):
        for what in due:
            what()

    @pl.loop(0, 3 * cy)
    def _(j):
        for third in range(3):

            @pl.when(j // cy == third)
            def _():
                for k in range(third * cy, (third + 1) * cy):
                    due = [what for when, what in events if when == k]
                    if due:
                        pl.when(j == k)(functools.partial(run_all, due))

        cell = j % cells
        basis_t[cell] = basis[:, pl.ds(pl.multiple_of(cell * slots, slots), slots)].T
        weigh(1, j)
        gather(0, j)
        weigh(0, (j + 1) % last)
        gather(1, j)

    for copy in halo.values():
        copy.wait_send()

    half = waves // 2
    two = 2 * slots

    def far_of(pair_of_cells, half_of):
        c0 = pair_of_cells * 2
        first = pl.multiple_of(half_of * half, half)
        left = jnp.concatenate([basis_t[pl.ds(c0, 2), :, pl.ds(k * waves + first, half)] for k in range(2)], axis=2)
        right = field[:, half_of].reshape(waves, feat)
        return jnp.dot(left.reshape(two, waves), right, preferred_element_type=jnp.float32)

    @pl.loop(0, cells // 2, unroll=True)
    def _(n):
        near = msg[pl.ds(2 * n, 2)].reshape(two, feat).astype(jnp.bfloat16)
        joined[n] = jnp.dot(near, wm_ref[...], preferred_element_type=jnp.float32)

    join_field()

    @pl.loop(0, cells // 2, unroll=True)
    def _(n):
        joined[n] += far_of(n, core)

    field_copy(core).wait_send()
    field_copy(1 - core).wait_recv()

    @pl.loop(0, cells // 2, unroll=True)
    def _(n):
        total = joined[n] + far_of(n, 1 - core)
        hidden = (total / (1.0 + jnp.exp(-total))).astype(jnp.bfloat16)
        result = jnp.dot(hidden, wo_ref[...], preferred_element_type=jnp.float32).reshape(2, slots, feat)
        c0 = 2 * n
        atom = wide[1 + c0 // cy, pl.ds(1 + c0 % cy, 2), 0].astype(jnp.float32)
        out_ref[pl.ds(c0, 2)] = (atom + result * out_mask[pl.ds(c0, 2)]).astype(jnp.bfloat16)


def radial_chain(gx, gy, gz, levels, reach, diagonal, p0, phi, slots):
    rows = gx.shape[0]
    sq = jnp.minimum(gx * gx + gy * gy + gz * gz, reach * reach)
    ratio = jnp.exp2(sq * lax.rsqrt(jnp.maximum(sq, 1e-30)))
    edge = reach * reach - sq
    val = edge * edge * jnp.exp2(sq * (-sharpness * math.log2(math.e) / reach**2))
    if diagonal is not None:
        row = lax.broadcasted_iota(jnp.int32, (rows, slots), 0) + diagonal
        lane = lax.broadcasted_iota(jnp.int32, (rows, slots), 1)
        val = jnp.concatenate([jnp.where(row == lane, 0.0, val[:, :slots]), val[:, slots:]], axis=1)
    second = ratio * ratio
    steps = [val.astype(jnp.bfloat16), (val * ratio).astype(jnp.bfloat16)]
    fourth = (second * second).astype(jnp.bfloat16)
    second = second.astype(jnp.bfloat16)
    for b in range(2, levels):
        steps.append(steps[b - 2] * second if b < 4 else steps[b - 4] * fourth)
    for b in range(levels):
        phi[b * slots + p0 : b * slots + p0 + rows] = steps[b]


def radial_terms(gx, gy, gz, levels, center, p0, phi, col, slots):
    rows = gx.shape[0]
    sq = jnp.minimum(gx * gx + gy * gy + gz * gz, 1.0)
    dist = sq * lax.rsqrt(jnp.maximum(sq, 1e-30))
    ratio = jnp.exp2(dist * (2.0 * sharpness / (levels - 1) * math.log2(math.e)))
    edge = 1.0 - sq
    val = edge * edge * jnp.exp2(sq * (-sharpness * math.log2(math.e)))
    if center:
        row = lax.broadcasted_iota(jnp.int32, val.shape, 0) + p0
        lane = lax.broadcasted_iota(jnp.int32, val.shape, 1)
        val = jnp.where(row == lane, 0.0, val)
    for b in range(levels):
        phi[b * slots + p0 : b * slots + p0 + rows, col : col + slots] = val.astype(jnp.bfloat16)
        if b + 1 < levels:
            val = val * ratio


def body(
    features,
    fractions,
    occupied,
    wave_index,
    radial_weight,
    ewald_mix,
    msg_weight,
    ewald_weight,
    out_weight,
):
    cx, cy, cz, slots, feat = features.shape
    levels, heads = radial_weight.shape
    cells = cx * cy * cz
    grid = [lax.axis_size("gx") * cx, lax.axis_size("gy") * cy, lax.axis_size("gz") * cz]
    devices = lax.axis_size("gx") * lax.axis_size("gy") * lax.axis_size("gz")
    waves = wave_index.shape[1]
    axes = ("gx", "gy", "gz")
    full = lambda shape: pl.BlockSpec(shape, lambda i: (0,) * len(shape))
    params = pltpu.CompilerParams(dimension_semantics=("arbitrary",), vmem_limit_bytes=56 * 2**20)

    fold_z = grid[2] == 2 and cz == 1
    counts = tuple(lax.axis_size(n) for n in axes)
    rows = waves // devices
    nx, ny = counts[:2]
    known = 2 < nx < 5 and ny == 4 and waves % 512 == 0 and cy % 2 == 0
    if fold_z and known and rows % 16 == 0 and ny > 2 and cx == 2 and cy > 2 and 4 * cells <= slots == 128:
        vmem = pl.BlockSpec(memory_space=pltpu.VMEM)
        dma = pltpu.SemaphoreType.DMA
        out = pl.pallas_call(
            functools.partial(layer_kernel, counts, levels),
            in_specs=[pl.BlockSpec(memory_space=pl.ANY)] * 9,
            out_specs=vmem,
            out_shape=pltpu.VMEM((cells, slots, feat), jnp.bfloat16),
            scratch_shapes=[
                pltpu.VMEM((cx, cy, slots, feat), jnp.bfloat16),
                pltpu.VMEM((cx, 3, cy, slots), jnp.bfloat16),
                pltpu.VMEM((cells, slots), jnp.int32),
                pltpu.VMEM(wave_index.shape, jnp.int32),
                pltpu.VMEM((heads, levels), jnp.float32),
                pltpu.VMEM(ewald_mix.shape, jnp.float32),
                pltpu.VMEM(ewald_weight.shape, jnp.bfloat16),
                pltpu.VMEM(msg_weight.shape, jnp.bfloat16),
                pltpu.VMEM(out_weight.shape, jnp.bfloat16),
                dma((9,)),
                pltpu.VMEM((cx + 2, cy + 2, 2, slots, feat), jnp.bfloat16),
                pltpu.VMEM((cx + 2, cy + 2, 2, 8, slots), jnp.bfloat16),
                pltpu.VMEM((slots, slots), jnp.float32),
                pltpu.VMEM((3, cells * slots), jnp.float32),
                pltpu.VMEM((cells, slots, feat), jnp.float32),
                pltpu.VMEM((waves, 8), jnp.float32),
                pltpu.VMEM((levels, feat), jnp.float32),
                pltpu.VMEM((cells, 3, slots, slots), jnp.float32),
                pltpu.VMEM((2, 3, levels * slots, 2 * slots), jnp.bfloat16),
                pltpu.VMEM((cells, slots, feat), jnp.float32),
                pltpu.VMEM((2 * waves, cells * slots), jnp.bfloat16),
                pltpu.VMEM((cells, slots, 2 * waves), jnp.bfloat16),
                pltpu.VMEM((cells // 2, 2 * slots, feat), jnp.float32),
                pltpu.VMEM((2, 2, nx, ny, rows, feat), jnp.bfloat16),
                pltpu.VMEM((2, nx, ny, rows, feat), jnp.bfloat16),
                pltpu.VMEM((2, nx, ny, rows, feat), jnp.bfloat16),
                pltpu.VMEM((ny, 2, nx, rows, feat), jnp.bfloat16),
                pltpu.VMEM((nx, 2, nx, rows, feat), jnp.bfloat16),
                pltpu.VMEM((2, 2, nx, ny, rows, feat), jnp.bfloat16),
                pltpu.SemaphoreType.REGULAR((2,)),
                dma((13, 2)),
                dma((13, 2)),
                dma((13, 2)),
                dma((13, 2)),
                dma((2,)),
                dma((2,)),
                dma((ny,)),
                dma((ny,)),
                dma((nx,)),
                dma((nx,)),
                dma((ny,)),
                dma((ny,)),
            ],
            compiler_params=pltpu.CompilerParams(
                collective_id=0, has_side_effects=True, vmem_limit_bytes=56 * 2**20
            ),
            name="layer",
        )(
            features.reshape(cx, cy, slots, feat),
            fractions.transpose(0, 2, 3, 1, 4).reshape(cx, 3, cy, slots),
            occupied.reshape(cells, slots),
            wave_index,
            radial_weight.T,
            ewald_mix,
            ewald_weight,
            msg_weight,
            out_weight,
        )
        return out.reshape(features.shape)

    masked = features * occupied[..., None].astype(jnp.bfloat16)
    frac = fractions.astype(jnp.float32)
    cell_feat = masked.reshape(cells, slots, feat)
    home = jnp.concatenate([frac, occupied[:, :, :, None, :].astype(jnp.float32)], axis=3)
    home = jnp.swapaxes(home.reshape(cells, 4, slots), 1, 2)

    start = [
        (lax.axis_index(n) * c + jnp.arange(c, dtype=jnp.int32)).astype(jnp.float32)
        for n, c in zip(axes, (cx, cy, cz))
    ]
    origin = jnp.stack(jnp.meshgrid(*start, indexing="ij"), axis=-1)[..., None]
    pos = (origin + frac).reshape(cells, 3, slots)
    lengths = jnp.array(grid, jnp.float32)
    index = wave_index.astype(jnp.float32)
    wave_vec = 2.0 * math.pi * index / lengths[:, None]
    wave_sq = jnp.sum(wave_vec * wave_vec, axis=0)
    damping = (
        strength
        * jnp.exp(-0.5 * smearing * wave_sq)
        / (wave_sq + screening)
        * (1.0 / math.sqrt(cells * slots * devices * waves))
    )
    wave_turn = (index / lengths[:, None]).T

    level = jnp.arange(levels, dtype=jnp.float32) / (levels - 1)
    wb = radial_weight * (jnp.exp(-sharpness * level * level) / math.sqrt(4.0 * slots))[:, None]
    wb = jnp.repeat(wb, feat // heads, axis=1)
    basis, struct = pl.pallas_call(
        basis_kernel,
        grid=(cells,),
        in_specs=[
            pl.BlockSpec((1, 3, slots), lambda i: (i, 0, 0)),
            full((waves, 3)),
            pl.BlockSpec((1, slots, feat), lambda i: (i, 0, 0)),
        ],
        out_specs=[pl.BlockSpec((1, 2 * waves, slots), lambda i: (i, 0, 0)), full((2 * waves, feat))],
        out_shape=[
            jax.ShapeDtypeStruct((cells, 2 * waves, slots), jnp.bfloat16),
            jax.ShapeDtypeStruct((2 * waves, feat), jnp.float32),
        ],
        compiler_params=params,
        name="basis",
    )(pos, wave_turn, cell_feat)

    wave_share = lax.psum_scatter(struct.reshape(2, waves, feat), axes, scatter_dimension=1, tiled=True)
    share_rows = wave_share.shape[1]
    share_damp = lax.dynamic_slice_in_dim(damping, lax.axis_index(axes) * share_rows, share_rows, 0)
    mixed = jnp.dot(wave_share.reshape(2 * share_rows, feat), ewald_mix, precision=lax.Precision.HIGHEST)
    filtered = (mixed.reshape(2, share_rows, feat) * share_damp[None, :, None]).astype(jnp.bfloat16)
    projected = jnp.dot(filtered, ewald_weight, preferred_element_type=jnp.float32).astype(jnp.bfloat16)
    field = lax.all_gather(projected, axes, axis=1, tiled=True).reshape(2 * waves, feat)

    wide_feat = widen(widen(masked, "gx", 0), "gy", 1)
    wide_geom = widen(widen(fractions, "gx", 0), "gy", 1)
    if fold_z:
        swap = [(0, 1), (1, 0)]
        wide_feat = jnp.concatenate([wide_feat, lax.ppermute(wide_feat, "gz", swap)], axis=2)
        wide_geom = jnp.concatenate([wide_geom, lax.ppermute(wide_geom, "gz", swap)], axis=2)
        near_z = 2
    else:
        wide_feat = widen(wide_feat, "gz", 2)
        wide_geom = widen(wide_geom, "gz", 2)
        near_z = 3
    wide_feat = jnp.stack([wide_feat[:, :, z : z + near_z] for z in range(cz)], axis=1)
    wide_geom = jnp.stack([wide_geom[:, :, z : z + near_z] for z in range(cz)], axis=1).astype(jnp.float32)
    messages = pl.pallas_call(
        functools.partial(message_kernel, cy, cz, fold_z, levels),
        grid=(cells,),
        in_specs=[
            pl.BlockSpec((1, slots, 4), lambda i: (i, 0, 0)),
            full(wide_feat.shape),
            full(wide_geom.shape),
            full(wb.shape),
        ],
        out_specs=pl.BlockSpec((1, slots, feat), lambda i: (i, 0, 0)),
        out_shape=jax.ShapeDtypeStruct((cells, slots, feat), jnp.bfloat16),
        scratch_shapes=[
            pltpu.VMEM((3, slots, slots), jnp.float32),
            pltpu.VMEM((3, levels * slots, 3 * near_z * slots), jnp.bfloat16),
            pltpu.VMEM((levels * slots, feat), jnp.float32),
        ],
        compiler_params=params,
        cost_estimate=pl.CostEstimate(
            flops=2 * cells * levels * slots * 9 * near_z * slots * feat, bytes_accessed=2**22, transcendentals=0
        ),
        name="messages",
    )(home, wide_feat, wide_geom, wb)

    out = pl.pallas_call(
        final_kernel,
        grid=(cells,),
        in_specs=[
            pl.BlockSpec((1, 2 * waves, slots), lambda i: (i, 0, 0)),
            full((2 * waves, feat)),
            pl.BlockSpec((1, slots, feat), lambda i: (i, 0, 0)),
            pl.BlockSpec((1, slots, feat), lambda i: (i, 0, 0)),
            pl.BlockSpec((1, slots, 4), lambda i: (i, 0, 0)),
            full((feat, feat)),
            full((feat, feat)),
        ],
        out_specs=pl.BlockSpec((1, slots, feat), lambda i: (i, 0, 0)),
        out_shape=jax.ShapeDtypeStruct((cells, slots, feat), jnp.bfloat16),
        compiler_params=params,
        name="final",
    )(basis, field, messages, cell_feat, home, msg_weight, out_weight)
    return out.reshape(features.shape)


def solution(mesh):
    cell = P("gx", "gy", "gz", None, None)
    in_specs = (cell, cell, P("gx", "gy", "gz", None), P(), P(), P(), P(), P(), P())
    return jax.shard_map(body, mesh=mesh, in_specs=in_specs, out_specs=cell, check_vma=False)
```

```python
import functools
import math

import jax
import jax.numpy as jnp
from jax import lax
from jax.experimental import pallas as pl
from jax.experimental.pallas import tpu as pltpu
from jax.sharding import PartitionSpec as P

sharpness = 16.0
smearing = 0.04
screening = 4.0
strength = 24.0

SIN_C = [(-1.0) ** k * math.pi ** (2 * k + 1) / math.factorial(2 * k + 1) for k in range(7)]
COS_C = [(-1.0) ** k * math.pi ** (2 * k) / math.factorial(2 * k) for k in range(7)]

SIN_P = [3.1415926401839953, -5.167710090331888, 2.550077659731212, -0.5982921594834444, 0.07765940825518475]
COS_P = [0.9999999534666585, -4.934792858674198, 4.058411914145813, -1.3318801611126891, 0.21969679833109643]


def poly(z, coefs):
    acc = jnp.full_like(z, coefs[-1])
    for c in coefs[-2::-1]:
        acc = acc * z + c
    return acc


def shifted(x, axis, dim, width):
    count, length = lax.axis_size(axis), x.shape[dim]
    up = [(i, (i + 1) % count) for i in range(count)]
    down = [(j, i) for i, j in up]
    last = lax.slice_in_dim(x, length - width, length, axis=dim)
    first = lax.slice_in_dim(x, 0, width, axis=dim)
    return lax.ppermute(last, axis, up), lax.ppermute(first, axis, down)


def widen(x, axis, dim):
    before, after = shifted(x, axis, dim, 1)
    return jnp.concatenate([before, x, after], axis=dim)


def message_kernel(cells_y, cells_z, fold_z, levels, home_ref, feat_ref, geom_ref, wb_ref, out_ref, hb, phi, acc):
    cell = pl.program_id(0)
    x = cell // (cells_y * cells_z)
    y = (cell // cells_z) % cells_y
    z = cell % cells_z
    slots = out_ref.shape[1]
    feat = out_ref.shape[2]
    near_z = feat_ref.shape[3]
    chunk = 32
    for a in range(3):
        hb[a] = jnp.broadcast_to(home_ref[0, :, a : a + 1], (slots, slots))
    for ox in range(3):
        for oy in range(3):
            for oz in range(near_z):
                g = geom_ref[x + ox, z, y + oy, oz]
                nx = g[0:1] + (ox - 1.0)
                ny = g[1:2] + (oy - 1.0)
                if fold_z:
                    nz = g[2:3]
                else:
                    nz = g[2:3] + (oz - 1.0)
                col = (oy * near_z + oz) * slots
                center = ox == 1 and oy == 1 and oz == (0 if fold_z else 1)
                for p0 in range(0, slots, chunk):
                    dx = nx - hb[0, p0 : p0 + chunk]
                    dy = ny - hb[1, p0 : p0 + chunk]
                    dz = nz - hb[2, p0 : p0 + chunk]
                    if fold_z and oz == 1:
                        dz = 1.0 - jnp.abs(dz)
                    radial_terms(dx, dy, dz, levels, center, p0, phi.at[ox], col, slots)
        rows = feat_ref[x + ox, z, pl.ds(y, 3)].reshape(3 * near_z * slots, feat)
        part = jnp.dot(phi[ox], rows, preferred_element_type=jnp.float32)
        if ox == 0:
            acc[...] = part
        elif ox == 1:
            acc[...] += part
    total = jnp.zeros((slots, feat), jnp.float32)
    for b in range(levels):
        both = acc[b * slots : (b + 1) * slots] + part[b * slots : (b + 1) * slots]
        total = total + both * wb_ref[b : b + 1]
    out_ref[0] = total.astype(jnp.bfloat16)


def basis_kernel(pos_ref, wave_ref, feat_ref, basis_ref, struct_ref):
    cell = pl.program_id(0)
    waves = wave_ref.shape[0]
    pos = pos_ref[0]
    chunk = 64
    for w0 in range(0, waves, chunk):
        wv = wave_ref[w0 : w0 + chunk]
        turns = wv[:, 0:1] * pos[0:1] + wv[:, 1:2] * pos[1:2] + wv[:, 2:3] * pos[2:3]
        u = turns - jnp.floor(turns + 0.5)
        q = u * u
        s = u * poly(q, SIN_C)
        c = poly(q, COS_C)
        basis_ref[0, w0 : w0 + chunk] = (1.0 - 2.0 * s * s).astype(jnp.bfloat16)
        basis_ref[0, waves + w0 : waves + w0 + chunk] = (2.0 * s * c).astype(jnp.bfloat16)
    part = jnp.dot(basis_ref[0], feat_ref[0], preferred_element_type=jnp.float32)

    @pl.when(cell == 0)
    def _():
        struct_ref[...] = part

    @pl.when(cell > 0)
    def _():
        struct_ref[...] += part


def final_kernel(basis_ref, grid_ref, msg_ref, feat_ref, home_ref, wm_ref, wo_ref, out_ref):
    far = lax.dot_general(
        basis_ref[0], grid_ref[...], (((0,), (0,)), ((), ())), preferred_element_type=jnp.float32
    )
    joined = far + jnp.dot(msg_ref[0], wm_ref[...], preferred_element_type=jnp.float32)
    hidden = (joined / (1.0 + jnp.exp(-joined))).astype(jnp.bfloat16)
    result = feat_ref[0].astype(jnp.float32) + jnp.dot(hidden, wo_ref[...], preferred_element_type=jnp.float32)
    out_ref[0] = (result * home_ref[0, :, 3:4]).astype(jnp.bfloat16)


def coords(index, counts):
    return (index // (counts[1] * counts[2]), (index // counts[2]) % counts[1], index % counts[2])


def layer_kernel(
    counts,
    levels,
    feat_in,
    frac_in,
    occ_in,
    index_in,
    radial_in,
    mix_in,
    we_in,
    wm_in,
    wo_in,
    out_ref,
    feat_ref,
    frac_ref,
    occ_ref,
    index_ref,
    radial_ref,
    mix_ref,
    we_ref,
    wm_ref,
    wo_ref,
    in_sem,
    wide,
    geom,
    rows_sc,
    pos_sc,
    out_mask,
    turn_cols,
    wb,
    hb,
    phi,
    msg,
    basis,
    basis_t,
    joined,
    struct,
    pair,
    chip_sum,
    parts,
    lines,
    field,
    token,
    halo_send,
    halo_recv,
    side_send,
    side_recv,
    pair_send,
    pair_recv,
    part_send,
    part_recv,
    line_send,
    line_recv,
    share_send,
    share_recv,
):
    cx, cy, slots, feat = feat_ref.shape
    cells = cx * cy
    waves = index_ref.shape[1]
    heads = radial_ref.shape[0]
    devices = counts[0] * counts[1] * counts[2]
    grid = (counts[0] * cx, counts[1] * cy, counts[2])
    rows = waves // devices
    at = (lax.axis_index("gx"), lax.axis_index("gy"), lax.axis_index("gz"))
    core = at[2]
    nx, ny = counts[0], counts[1]
    mesh_id = pl.DeviceIdType.MESH
    pad = geom.shape[3]
    reach = 2.0 * sharpness / (levels - 1) * math.log2(math.e)
    partner = (at[0], at[1], 1 - core)
    line_near = (at[0] + nx - 1) // nx + (2 * nx - 2 - at[0]) // nx
    bits = [1 << n for n in range(ny.bit_length() - 1)]

    def over_x(k):
        return ((at[0] + k + nx) % nx, at[1], core)

    def over_y(k):
        return (at[0], (at[1] + k + ny) % ny, core)

    def to_partner(src, dst, send, recv):
        return pltpu.make_async_remote_copy(
            src_ref=src, dst_ref=dst, send_sem=send, recv_sem=recv, device_id=partner, device_id_type=mesh_id
        )

    sources = [frac_in, occ_in, index_in, radial_in, feat_in, mix_in, we_in, wm_in, wo_in]
    places = [frac_ref, occ_ref, index_ref, radial_ref, feat_ref, mix_ref, we_ref, wm_ref, wo_ref]
    loads = [pltpu.make_async_copy(src, dst, in_sem.at[n]) for n, (src, dst) in enumerate(zip(sources, places))]
    for load in loads:
        load.start()

    barrier = pltpu.get_barrier_semaphore()

    def greet_line(sem):
        @pl.when(at[0] > 0)
        def _():
            pl.semaphore_signal(sem, inc=1, device_id=over_x(-1), device_id_type=mesh_id)

        @pl.when(at[0] < nx - 1)
        def _():
            pl.semaphore_signal(sem, inc=1, device_id=over_x(1), device_id_type=mesh_id)

    def greet_near(sem):
        greet_line(sem)
        for bit in bits:
            step = bit * (1 - 2 * (at[1] // bit % 2))
            pl.semaphore_signal(sem, inc=1, device_id=over_y(step), device_id_type=mesh_id)

    pl.semaphore_signal(barrier, inc=1, device_id=partner, device_id_type=mesh_id)
    greet_near(barrier)

    loads[0].wait()
    loads[1].wait()
    rows_sc[...] = jnp.zeros_like(rows_sc)
    for x in range(cx):
        for a in range(3):
            k = (x * 3 + a) * cy
            rows_sc[k : k + cy] = frac_ref[x, a].astype(jnp.float32)
    rows_sc[3 * cells : 4 * cells] = occ_ref[...].astype(jnp.float32)
    turned = rows_sc[...].T
    for x in range(cx):
        for y in range(cy):
            k = 3 * cells + x * cy + y
            out_mask[x * cy + y] = jnp.broadcast_to(turned[:, k : k + 1], (slots, feat))
    loads[4].wait()
    for x in range(cx):
        for y in range(cy):
            cell = x * cy + y
            ks = [(x * 3 + a) * cy + y for a in range(3)]
            wide[1 + x, 1 + y, 0] = feat_ref[x, y] * out_mask[cell].astype(jnp.bfloat16)
            own = jnp.concatenate([rows_sc[k : k + 1] for k in ks] + [jnp.zeros((pad - 3, slots), jnp.float32)])
            geom[1 + x, 1 + y, 0] = own.astype(jnp.bfloat16)

    class Both:
        def __init__(self, copies):
            self.copies = copies

        def start(self):
            for copy in self.copies:
                copy.start()

        def wait(self):
            for copy in self.copies:
                copy.wait()

        def wait_send(self):
            for copy in self.copies:
                copy.wait_send()

        def wait_recv(self):
            for copy in self.copies:
                copy.wait_recv()

    halo, side = {}, {}

    def link(key, device, source, target):
        n = len(side)
        refs = list(enumerate((geom, wide)))
        side[key] = Both(
            [to_partner(r.at[(*target, 0)], r.at[(*target, 1)], side_send.at[n, i], side_recv.at[n, i]) for i, r in refs]
        )
        if device is not None:
            halo[key] = Both(
                [
                    pltpu.make_async_remote_copy(
                        src_ref=r.at[(*source, 0)],
                        dst_ref=r.at[(*target, 0)],
                        send_sem=halo_send.at[n, i],
                        recv_sem=halo_recv.at[n, i],
                        device_id=device,
                        device_id_type=mesh_id,
                    )
                    for i, r in refs
                ]
            )

    one = lambda start: pl.ds(start, 1)
    for dy in (1, -1):
        xs = pl.ds(1, cx)
        link((0, dy), over_y(dy), (xs, one(cy if dy == 1 else 1)), (xs, one(0 if dy == 1 else cy + 1)))
    for dx in (1, -1):
        sx, tx = one(cx if dx == 1 else 1), one(0 if dx == 1 else cx + 1)
        for name, ys in (("low", one(1)), ("high", one(cy)), ("middle", pl.ds(2, cy - 2))):
            link((dx, name), over_x(dx), (sx, ys), (tx, ys))
        for dy in (1, -1):
            link((dx, dy), over_y(dy), (tx, one(cy if dy == 1 else 1)), (tx, one(0 if dy == 1 else cy + 1)))
    link((0, 0), None, None, (pl.ds(1, cx), pl.ds(1, cy)))

    def send_face(step):
        for name in ("low", "high", "middle"):
            halo[step, name].start()

    def send_faces(direct):
        for step, inside in ((1, at[0] < nx - 1), (-1, at[0] > 0)):
            pl.when(inside if direct else jnp.logical_not(inside))(functools.partial(send_face, step))

    def send_rows(direct):
        for step, near in ((1, at[1] % 2 == 0), (-1, at[1] % 2 == 1)):
            pl.when(near if direct else jnp.logical_not(near))(halo[0, step].start)

    def pass_token():
        pl.semaphore_wait(token.at[0], line_near + len(bits))
        greet_line(token.at[1])
        send_rows(False)

    def open_wrap():
        pl.semaphore_wait(token.at[1], line_near)
        send_faces(False)

    loads[2].wait()
    for w0 in range(0, waves, 128):
        part = [index_ref[a : a + 1, w0 : w0 + 128].astype(jnp.float32) * (1.0 / grid[a]) for a in range(3)]
        part = jnp.concatenate(part + [jnp.zeros((5, 128), jnp.float32)])
        turn_cols[w0 : w0 + 128] = part.T
    for x in range(cx):
        for y in range(cy):
            start = [at[0] * cx + x, at[1] * cy + y, core]
            cell = x * cy + y
            for a in range(3):
                k = (x * 3 + a) * cy + y
                pos_sc[a : a + 1, cell * slots : (cell + 1) * slots] = rows_sc[k : k + 1] + start[a].astype(jnp.float32)

    loads[3].wait()
    for x in range(cx):
        for y in range(cy):
            for a in range(3):
                k = (x * 3 + a) * cy + y
                hb[x * cy + y, a] = jnp.broadcast_to(turned[:, k : k + 1] * reach, (slots, slots))
    owner = lax.broadcasted_iota(jnp.int32, (heads, feat), 1) // (feat // heads)
    mine = owner == lax.broadcasted_iota(jnp.int32, (heads, feat), 0)
    for b in range(levels):
        level = b / (levels - 1)
        scale = math.exp(-sharpness * level * level) / math.sqrt(4.0 * slots) / reach**4
        column = jnp.broadcast_to(radial_ref[:, b : b + 1], (heads, feat)) * scale
        wb[b : b + 1] = jnp.sum(jnp.where(mine, column, 0.0), axis=0, keepdims=True)

    pl.semaphore_wait(barrier, 1 + line_near + len(bits))
    greet_near(token.at[0])
    side[0, 0].start()
    send_rows(True)
    send_faces(True)

    @pl.loop(0, cells // 2)
    def _(two):
        pl.when(two == cells // 8)(pass_token)
        pl.when(two == cells // 4 + 1)(open_wrap)
        lanes = pl.ds(pl.multiple_of(two * 2 * slots, 2 * slots), 2 * slots)
        pos = pos_sc[:, lanes]
        chunk = 32
        for w0 in range(0, waves, chunk):
            wv = turn_cols[w0 : w0 + chunk]
            turns = wv[:, 0:1] * pos[0:1] + wv[:, 1:2] * pos[1:2] + wv[:, 2:3] * pos[2:3]
            u = turns - jnp.round(turns)
            q = u * u
            s = u * poly(q, [v * math.sqrt(2.0) for v in SIN_P])
            c = poly(q, [v * math.sqrt(2.0) for v in COS_P])
            basis[w0 : w0 + chunk, lanes] = (1.0 - s * s).astype(jnp.bfloat16)
            basis[waves + w0 : waves + w0 + chunk, lanes] = (s * c).astype(jnp.bfloat16)

    atoms = wide[1 : 1 + cx, 1 : 1 + cy, 0].reshape(cells * slots, feat)
    struct[...] = (
        jnp.dot(basis[...], atoms, preferred_element_type=jnp.float32)
        .astype(jnp.bfloat16)
        .reshape(struct.shape)
    )
    swap = to_partner(struct.at[:, 1 - core], pair, pair_send.at[0], pair_recv.at[0])
    swap.start()

    for load in loads[5:]:
        load.wait()
    msg[...] = jnp.zeros_like(msg)

    def part_copy(k):
        return pltpu.make_async_remote_copy(
            src_ref=chip_sum.at[:, :, (at[1] + k) % ny],
            dst_ref=parts.at[k],
            send_sem=part_send.at[k],
            recv_sem=part_recv.at[k],
            device_id=over_y(k),
            device_id_type=mesh_id,
        )

    def line_copy(k, slot):
        return pltpu.make_async_remote_copy(
            src_ref=lines.at[at[0]],
            dst_ref=lines.at[slot],
            send_sem=line_send.at[k],
            recv_sem=line_recv.at[k],
            device_id=over_x(k),
            device_id_type=mesh_id,
        )

    def share_copy(k, slot):
        return pltpu.make_async_remote_copy(
            src_ref=field.at[:, core, :, at[1]],
            dst_ref=field.at[:, core, :, slot],
            send_sem=share_send.at[k],
            recv_sem=share_recv.at[k],
            device_id=over_y(k),
            device_id_type=mesh_id,
        )

    def field_copy(half, k):
        mine = field.at[:, half, :, (at[1] - k + ny) % ny]
        return to_partner(mine, mine, pair_send.at[1 + k], pair_recv.at[1 + k])

    def sum_pair():
        swap.wait()
        both = struct[:, core].astype(jnp.float32) + pair[...].astype(jnp.float32)
        chip_sum[...] = both.astype(jnp.bfloat16)
        for k in range(1, ny):
            part_copy(k).start()

    def sum_parts():
        for k in range(1, ny):
            part_copy(k).wait()
        parts[0] = chip_sum[:, :, at[1]]
        lines[at[0]] = jnp.sum(parts[...].astype(jnp.float32), axis=0).astype(jnp.bfloat16)
        for k in range(1, nx):
            line_copy(k, at[0]).start()

    def filter_share():
        for k in range(1, nx):
            line_copy(k, (at[0] - k + nx) % nx).wait()
        total = jnp.sum(lines[...].astype(jnp.float32), axis=0).reshape(2 * nx * rows, feat)
        mixed = jnp.dot(total, mix_ref[...], precision=lax.Precision.HIGHEST, preferred_element_type=jnp.float32)
        vec = [turn_cols[pl.ds(((core * nx + x) * ny + at[1]) * rows, rows)] for x in range(nx)]
        vec = jnp.concatenate(vec) * (2.0 * math.pi)
        square = jnp.sum(vec * vec, axis=1, keepdims=True)
        damp = strength * jnp.exp(-0.5 * smearing * square) / (square + screening)
        damp = damp * (1.0 / math.sqrt(cells * slots * devices * waves))
        filtered = (mixed * jnp.concatenate([damp, damp])).astype(jnp.bfloat16)
        projected = jnp.dot(filtered, we_ref[...], preferred_element_type=jnp.float32)
        field[:, core, :, at[1]] = projected.astype(jnp.bfloat16).reshape(2, nx, rows, feat)
        for k in range(1, ny):
            share_copy(k, at[1]).start()
        field_copy(core, 0).start()

    def join_field():
        for k in range(1, ny):
            share_copy(k, (at[1] - k + ny) % ny).wait()
            field_copy(core, k).start()

    first_x = 1 - (at[0] + nx - 1) // nx

    def place(slot, j):
        late = j // (2 * cy)
        i = j % (2 * cy)
        turn = i // (cy // 2)
        x = (1 - late) * slot + late * (turn + (1 - 2 * turn) * first_x)
        y = ((1 - late) * (i // 2) + late * (2 * (i % (cy // 2)) + slot) + 1) % cy
        xi = (1 - late) * (1 + i % 2) + late * x * (cx + 1)
        return x, y, xi

    def weigh(slot, j):
        x, y, xi = place(slot, j)
        cell = x * cy + y
        step = xi - (x + 1)
        chunk = 32
        done = []
        for oy in range(3):
            near = [
                geom[xi, y + oy, oz].astype(jnp.float32) * reach for oz in range(2)
            ]
            near = jnp.concatenate(near, axis=1)
            nx = near[0:1] + step.astype(jnp.float32) * reach
            ny = near[1:2] + (oy - 1.0) * reach
            nz = near[2:3]
            for p0 in range(0, slots, chunk):
                row = nx
                if len(done) >= 1:
                    o, p = done[-1]
                    row = jnp.concatenate([nx[:, :slots] + jnp.minimum(phi[slot, o, p + 7 * slots : p + 7 * slots + 8, :slots].astype(jnp.float32)[0:1], 0.0), nx[:, slots:]], axis=1)
                done.append((oy, p0))
                gx, gy, gz = (
                    n - jnp.concatenate([hb[cell, a, p0 : p0 + chunk]] * 2, axis=1) for a, n in enumerate((row, ny, nz))
                )
                gz = jnp.concatenate([gz[:, :slots], reach - jnp.abs(gz[:, slots:])], axis=1)
                diagonal = p0 + step * slots if oy == 1 else None
                radial_chain(gx, gy, gz, levels, reach, diagonal, p0, phi.at[slot, oy], slots)

    def gather(slot, j):
        x, y, xi = place(slot, j)
        near = wide[xi, pl.ds(y, 3)].reshape(6 * slots, feat)
        left = jnp.concatenate([phi[slot, oy] for oy in range(3)], axis=1)
        part = jnp.dot(left, near, preferred_element_type=jnp.float32)
        total = msg[x * cy + y]
        for b in range(levels):
            total = total + part[b * slots : (b + 1) * slots] * wb[b : b + 1]
        msg[x * cy + y] = total

    def halo_in(*keys):
        for key in keys:
            halo[key].wait_recv()
            side[key].start()

    def side_in(*keys):
        for key in keys:
            side[key].wait()

    def face_in(step):
        halo_in((step, "low"))
        halo[step, -1].start()
        halo_in((step, "high"))
        halo[step, 1].start()

    def rest_in(step):
        halo_in((step, "middle"))

    def face_done(step):
        side_in((step, "low"), (step, "high"), (step, "middle"))

    def corners_in(step):
        halo_in((step, -1), (step, 1))

    def corners_done(step):
        side_in((step, -1), (step, 1))

    def on_side(first, what):
        def run():
            for step, then in ((1, first_x == 0), (-1, first_x == 1)):
                pl.when(then if first else jnp.logical_not(then))(functools.partial(what, step))

        return run

    side_in((0, 0))
    weigh(0, jnp.int32(0))

    ends = 2 * cy - 4
    last = 3 * cy
    events = [
        (1, sum_pair),
        (ends - 3, lambda: halo_in((0, -1), (0, 1))),
        (ends - 2, on_side(True, face_in)),
        (ends - 1, lambda: side_in((0, -1))),
        (ends - 1, on_side(True, rest_in)),
        (ends, sum_parts),
        (ends + 1, lambda: side_in((0, 1))),
        (ends + 1, on_side(True, corners_in)),
        (ends + 2, on_side(False, face_in)),
        (ends + 3, on_side(True, face_done)),
        (last - 4, on_side(True, corners_done)),
        (last - 4, on_side(False, rest_in)),
        (last - 3, on_side(False, corners_in)),
        (last - 3, on_side(False, face_done)),
        (last - 3, filter_share),
        (last - 2, on_side(False, corners_done)),
    ]

    def run_all(due):
        for what in due:
            what()

    @pl.loop(0, 3 * cy)
    def _(j):
        for third in range(3):

            @pl.when(j // cy == third)
            def _():
                for k in range(third * cy, (third + 1) * cy):
                    due = [what for when, what in events if when == k]
                    if due:
                        pl.when(j == k)(functools.partial(run_all, due))

        cell = j % cells
        basis_t[cell] = basis[:, pl.ds(pl.multiple_of(cell * slots, slots), slots)].T
        weigh(1, j)
        gather(0, j)
        weigh(0, (j + 1) % last)
        gather(1, j)

    for copy in halo.values():
        copy.wait_send()

    half = waves // 2
    two = 2 * slots

    def far_of(pair_of_cells, half_of):
        c0 = pair_of_cells * 2
        first = pl.multiple_of(half_of * half, half)
        left = jnp.concatenate([basis_t[pl.ds(c0, 2), :, pl.ds(k * waves + first, half)] for k in range(2)], axis=2)
        right = field[:, half_of].reshape(waves, feat)
        return jnp.dot(left.reshape(two, waves), right, preferred_element_type=jnp.float32)

    @pl.loop(0, cells // 2, unroll=True)
    def _(n):
        near = msg[pl.ds(2 * n, 2)].reshape(two, feat).astype(jnp.bfloat16)
        joined[n] = jnp.dot(near, wm_ref[...], preferred_element_type=jnp.float32)

    join_field()

    @pl.loop(0, cells // 2, unroll=True)
    def _(n):
        joined[n] += far_of(n, core)

    for k in range(ny):
        field_copy(core, k).wait_send()
        field_copy(1 - core, k).wait_recv()

    @pl.loop(0, cells // 2, unroll=True)
    def _(n):
        total = joined[n] + far_of(n, 1 - core)
        hidden = (total / (1.0 + jnp.exp(-total))).astype(jnp.bfloat16)
        result = jnp.dot(hidden, wo_ref[...], preferred_element_type=jnp.float32).reshape(2, slots, feat)
        c0 = 2 * n
        atom = wide[1 + c0 // cy, pl.ds(1 + c0 % cy, 2), 0].astype(jnp.float32)
        out_ref[pl.ds(c0, 2)] = (atom + result * out_mask[pl.ds(c0, 2)]).astype(jnp.bfloat16)


def radial_chain(gx, gy, gz, levels, reach, diagonal, p0, phi, slots):
    rows = gx.shape[0]
    sq = jnp.minimum(gx * gx + gy * gy + gz * gz, reach * reach)
    ratio = jnp.exp2(sq * lax.rsqrt(jnp.maximum(sq, 1e-30)))
    edge = reach * reach - sq
    val = edge * edge * jnp.exp2(sq * (-sharpness * math.log2(math.e) / reach**2))
    if diagonal is not None:
        row = lax.broadcasted_iota(jnp.int32, (rows, slots), 0) + diagonal
        lane = lax.broadcasted_iota(jnp.int32, (rows, slots), 1)
        val = jnp.concatenate([jnp.where(row == lane, 0.0, val[:, :slots]), val[:, slots:]], axis=1)
    second = ratio * ratio
    steps = [val.astype(jnp.bfloat16), (val * ratio).astype(jnp.bfloat16)]
    fourth = (second * second).astype(jnp.bfloat16)
    second = second.astype(jnp.bfloat16)
    for b in range(2, levels):
        steps.append(steps[b - 2] * second if b < 4 else steps[b - 4] * fourth)
    for b in range(levels):
        phi[b * slots + p0 : b * slots + p0 + rows] = steps[b]


def radial_terms(gx, gy, gz, levels, center, p0, phi, col, slots):
    rows = gx.shape[0]
    sq = jnp.minimum(gx * gx + gy * gy + gz * gz, 1.0)
    dist = sq * lax.rsqrt(jnp.maximum(sq, 1e-30))
    ratio = jnp.exp2(dist * (2.0 * sharpness / (levels - 1) * math.log2(math.e)))
    edge = 1.0 - sq
    val = edge * edge * jnp.exp2(sq * (-sharpness * math.log2(math.e)))
    if center:
        row = lax.broadcasted_iota(jnp.int32, val.shape, 0) + p0
        lane = lax.broadcasted_iota(jnp.int32, val.shape, 1)
        val = jnp.where(row == lane, 0.0, val)
    for b in range(levels):
        phi[b * slots + p0 : b * slots + p0 + rows, col : col + slots] = val.astype(jnp.bfloat16)
        if b + 1 < levels:
            val = val * ratio


def body(
    features,
    fractions,
    occupied,
    wave_index,
    radial_weight,
    ewald_mix,
    msg_weight,
    ewald_weight,
    out_weight,
):
    cx, cy, cz, slots, feat = features.shape
    levels, heads = radial_weight.shape
    cells = cx * cy * cz
    grid = [lax.axis_size("gx") * cx, lax.axis_size("gy") * cy, lax.axis_size("gz") * cz]
    devices = lax.axis_size("gx") * lax.axis_size("gy") * lax.axis_size("gz")
    waves = wave_index.shape[1]
    axes = ("gx", "gy", "gz")
    full = lambda shape: pl.BlockSpec(shape, lambda i: (0,) * len(shape))
    params = pltpu.CompilerParams(dimension_semantics=("arbitrary",), vmem_limit_bytes=56 * 2**20)

    fold_z = grid[2] == 2 and cz == 1
    counts = tuple(lax.axis_size(n) for n in axes)
    rows = waves // devices
    nx, ny = counts[:2]
    known = 2 < nx < 5 and ny == 4 and waves % 512 == 0 and cy % 2 == 0
    if fold_z and known and rows % 16 == 0 and ny > 2 and cx == 2 and cy > 2 and 4 * cells <= slots == 128:
        vmem = pl.BlockSpec(memory_space=pltpu.VMEM)
        dma = pltpu.SemaphoreType.DMA
        out = pl.pallas_call(
            functools.partial(layer_kernel, counts, levels),
            in_specs=[pl.BlockSpec(memory_space=pl.ANY)] * 9,
            out_specs=vmem,
            out_shape=pltpu.VMEM((cells, slots, feat), jnp.bfloat16),
            scratch_shapes=[
                pltpu.VMEM((cx, cy, slots, feat), jnp.bfloat16),
                pltpu.VMEM((cx, 3, cy, slots), jnp.bfloat16),
                pltpu.VMEM((cells, slots), jnp.int32),
                pltpu.VMEM(wave_index.shape, jnp.int32),
                pltpu.VMEM((heads, levels), jnp.float32),
                pltpu.VMEM(ewald_mix.shape, jnp.float32),
                pltpu.VMEM(ewald_weight.shape, jnp.bfloat16),
                pltpu.VMEM(msg_weight.shape, jnp.bfloat16),
                pltpu.VMEM(out_weight.shape, jnp.bfloat16),
                dma((9,)),
                pltpu.VMEM((cx + 2, cy + 2, 2, slots, feat), jnp.bfloat16),
                pltpu.VMEM((cx + 2, cy + 2, 2, 8, slots), jnp.bfloat16),
                pltpu.VMEM((slots, slots), jnp.float32),
                pltpu.VMEM((3, cells * slots), jnp.float32),
                pltpu.VMEM((cells, slots, feat), jnp.float32),
                pltpu.VMEM((waves, 8), jnp.float32),
                pltpu.VMEM((levels, feat), jnp.float32),
                pltpu.VMEM((cells, 3, slots, slots), jnp.float32),
                pltpu.VMEM((2, 3, levels * slots, 2 * slots), jnp.bfloat16),
                pltpu.VMEM((cells, slots, feat), jnp.float32),
                pltpu.VMEM((2 * waves, cells * slots), jnp.bfloat16),
                pltpu.VMEM((cells, slots, 2 * waves), jnp.bfloat16),
                pltpu.VMEM((cells // 2, 2 * slots, feat), jnp.float32),
                pltpu.VMEM((2, 2, nx, ny, rows, feat), jnp.bfloat16),
                pltpu.VMEM((2, nx, ny, rows, feat), jnp.bfloat16),
                pltpu.VMEM((2, nx, ny, rows, feat), jnp.bfloat16),
                pltpu.VMEM((ny, 2, nx, rows, feat), jnp.bfloat16),
                pltpu.VMEM((nx, 2, nx, rows, feat), jnp.bfloat16),
                pltpu.VMEM((2, 2, nx, ny, rows, feat), jnp.bfloat16),
                pltpu.SemaphoreType.REGULAR((2,)),
                dma((13, 2)),
                dma((13, 2)),
                dma((13, 2)),
                dma((13, 2)),
                dma((1 + ny,)),
                dma((1 + ny,)),
                dma((ny,)),
                dma((ny,)),
                dma((nx,)),
                dma((nx,)),
                dma((ny,)),
                dma((ny,)),
            ],
            compiler_params=pltpu.CompilerParams(
                collective_id=0, has_side_effects=True, vmem_limit_bytes=56 * 2**20
            ),
            name="layer",
        )(
            features.reshape(cx, cy, slots, feat),
            fractions.transpose(0, 2, 3, 1, 4).reshape(cx, 3, cy, slots),
            occupied.reshape(cells, slots),
            wave_index,
            radial_weight.T,
            ewald_mix,
            ewald_weight,
            msg_weight,
            out_weight,
        )
        return out.reshape(features.shape)

    masked = features * occupied[..., None].astype(jnp.bfloat16)
    frac = fractions.astype(jnp.float32)
    cell_feat = masked.reshape(cells, slots, feat)
    home = jnp.concatenate([frac, occupied[:, :, :, None, :].astype(jnp.float32)], axis=3)
    home = jnp.swapaxes(home.reshape(cells, 4, slots), 1, 2)

    start = [
        (lax.axis_index(n) * c + jnp.arange(c, dtype=jnp.int32)).astype(jnp.float32)
        for n, c in zip(axes, (cx, cy, cz))
    ]
    origin = jnp.stack(jnp.meshgrid(*start, indexing="ij"), axis=-1)[..., None]
    pos = (origin + frac).reshape(cells, 3, slots)
    lengths = jnp.array(grid, jnp.float32)
    index = wave_index.astype(jnp.float32)
    wave_vec = 2.0 * math.pi * index / lengths[:, None]
    wave_sq = jnp.sum(wave_vec * wave_vec, axis=0)
    damping = (
        strength
        * jnp.exp(-0.5 * smearing * wave_sq)
        / (wave_sq + screening)
        * (1.0 / math.sqrt(cells * slots * devices * waves))
    )
    wave_turn = (index / lengths[:, None]).T

    level = jnp.arange(levels, dtype=jnp.float32) / (levels - 1)
    wb = radial_weight * (jnp.exp(-sharpness * level * level) / math.sqrt(4.0 * slots))[:, None]
    wb = jnp.repeat(wb, feat // heads, axis=1)
    basis, struct = pl.pallas_call(
        basis_kernel,
        grid=(cells,),
        in_specs=[
            pl.BlockSpec((1, 3, slots), lambda i: (i, 0, 0)),
            full((waves, 3)),
            pl.BlockSpec((1, slots, feat), lambda i: (i, 0, 0)),
        ],
        out_specs=[pl.BlockSpec((1, 2 * waves, slots), lambda i: (i, 0, 0)), full((2 * waves, feat))],
        out_shape=[
            jax.ShapeDtypeStruct((cells, 2 * waves, slots), jnp.bfloat16),
            jax.ShapeDtypeStruct((2 * waves, feat), jnp.float32),
        ],
        compiler_params=params,
        name="basis",
    )(pos, wave_turn, cell_feat)

    wave_share = lax.psum_scatter(struct.reshape(2, waves, feat), axes, scatter_dimension=1, tiled=True)
    share_rows = wave_share.shape[1]
    share_damp = lax.dynamic_slice_in_dim(damping, lax.axis_index(axes) * share_rows, share_rows, 0)
    mixed = jnp.dot(wave_share.reshape(2 * share_rows, feat), ewald_mix, precision=lax.Precision.HIGHEST)
    filtered = (mixed.reshape(2, share_rows, feat) * share_damp[None, :, None]).astype(jnp.bfloat16)
    projected = jnp.dot(filtered, ewald_weight, preferred_element_type=jnp.float32).astype(jnp.bfloat16)
    field = lax.all_gather(projected, axes, axis=1, tiled=True).reshape(2 * waves, feat)

    wide_feat = widen(widen(masked, "gx", 0), "gy", 1)
    wide_geom = widen(widen(fractions, "gx", 0), "gy", 1)
    if fold_z:
        swap = [(0, 1), (1, 0)]
        wide_feat = jnp.concatenate([wide_feat, lax.ppermute(wide_feat, "gz", swap)], axis=2)
        wide_geom = jnp.concatenate([wide_geom, lax.ppermute(wide_geom, "gz", swap)], axis=2)
        near_z = 2
    else:
        wide_feat = widen(wide_feat, "gz", 2)
        wide_geom = widen(wide_geom, "gz", 2)
        near_z = 3
    wide_feat = jnp.stack([wide_feat[:, :, z : z + near_z] for z in range(cz)], axis=1)
    wide_geom = jnp.stack([wide_geom[:, :, z : z + near_z] for z in range(cz)], axis=1).astype(jnp.float32)
    messages = pl.pallas_call(
        functools.partial(message_kernel, cy, cz, fold_z, levels),
        grid=(cells,),
        in_specs=[
            pl.BlockSpec((1, slots, 4), lambda i: (i, 0, 0)),
            full(wide_feat.shape),
            full(wide_geom.shape),
            full(wb.shape),
        ],
        out_specs=pl.BlockSpec((1, slots, feat), lambda i: (i, 0, 0)),
        out_shape=jax.ShapeDtypeStruct((cells, slots, feat), jnp.bfloat16),
        scratch_shapes=[
            pltpu.VMEM((3, slots, slots), jnp.float32),
            pltpu.VMEM((3, levels * slots, 3 * near_z * slots), jnp.bfloat16),
            pltpu.VMEM((levels * slots, feat), jnp.float32),
        ],
        compiler_params=params,
        cost_estimate=pl.CostEstimate(
            flops=2 * cells * levels * slots * 9 * near_z * slots * feat, bytes_accessed=2**22, transcendentals=0
        ),
        name="messages",
    )(home, wide_feat, wide_geom, wb)

    out = pl.pallas_call(
        final_kernel,
        grid=(cells,),
        in_specs=[
            pl.BlockSpec((1, 2 * waves, slots), lambda i: (i, 0, 0)),
            full((2 * waves, feat)),
            pl.BlockSpec((1, slots, feat), lambda i: (i, 0, 0)),
            pl.BlockSpec((1, slots, feat), lambda i: (i, 0, 0)),
            pl.BlockSpec((1, slots, 4), lambda i: (i, 0, 0)),
            full((feat, feat)),
            full((feat, feat)),
        ],
        out_specs=pl.BlockSpec((1, slots, feat), lambda i: (i, 0, 0)),
        out_shape=jax.ShapeDtypeStruct((cells, slots, feat), jnp.bfloat16),
        compiler_params=params,
        name="final",
    )(basis, field, messages, cell_feat, home, msg_weight, out_weight)
    return out.reshape(features.shape)


def solution(mesh):
    cell = P("gx", "gy", "gz", None, None)
    in_specs = (cell, cell, P("gx", "gy", "gz", None), P(), P(), P(), P(), P(), P())
    return jax.shard_map(body, mesh=mesh, in_specs=in_specs, out_specs=cell, check_vma=False)
```

```python
import functools
import math

import jax
import jax.numpy as jnp
from jax import lax
from jax.experimental import pallas as pl
from jax.experimental.pallas import tpu as pltpu
from jax.sharding import PartitionSpec as P

sharpness = 16.0
smearing = 0.04
screening = 4.0
strength = 24.0

SIN_C = [(-1.0) ** k * math.pi ** (2 * k + 1) / math.factorial(2 * k + 1) for k in range(7)]
COS_C = [(-1.0) ** k * math.pi ** (2 * k) / math.factorial(2 * k) for k in range(7)]

SIN_P = [3.1415926401839953, -5.167710090331888, 2.550077659731212, -0.5982921594834444, 0.07765940825518475]
COS_P = [0.9999999534666585, -4.934792858674198, 4.058411914145813, -1.3318801611126891, 0.21969679833109643]


def poly(z, coefs):
    acc = jnp.full_like(z, coefs[-1])
    for c in coefs[-2::-1]:
        acc = acc * z + c
    return acc


def shifted(x, axis, dim, width):
    count, length = lax.axis_size(axis), x.shape[dim]
    up = [(i, (i + 1) % count) for i in range(count)]
    down = [(j, i) for i, j in up]
    last = lax.slice_in_dim(x, length - width, length, axis=dim)
    first = lax.slice_in_dim(x, 0, width, axis=dim)
    return lax.ppermute(last, axis, up), lax.ppermute(first, axis, down)


def widen(x, axis, dim):
    before, after = shifted(x, axis, dim, 1)
    return jnp.concatenate([before, x, after], axis=dim)


def message_kernel(cells_y, cells_z, fold_z, levels, home_ref, feat_ref, geom_ref, wb_ref, out_ref, hb, phi, acc):
    cell = pl.program_id(0)
    x = cell // (cells_y * cells_z)
    y = (cell // cells_z) % cells_y
    z = cell % cells_z
    slots = out_ref.shape[1]
    feat = out_ref.shape[2]
    near_z = feat_ref.shape[3]
    chunk = 32
    for a in range(3):
        hb[a] = jnp.broadcast_to(home_ref[0, :, a : a + 1], (slots, slots))
    for ox in range(3):
        for oy in range(3):
            for oz in range(near_z):
                g = geom_ref[x + ox, z, y + oy, oz]
                nx = g[0:1] + (ox - 1.0)
                ny = g[1:2] + (oy - 1.0)
                if fold_z:
                    nz = g[2:3]
                else:
                    nz = g[2:3] + (oz - 1.0)
                col = (oy * near_z + oz) * slots
                center = ox == 1 and oy == 1 and oz == (0 if fold_z else 1)
                for p0 in range(0, slots, chunk):
                    dx = nx - hb[0, p0 : p0 + chunk]
                    dy = ny - hb[1, p0 : p0 + chunk]
                    dz = nz - hb[2, p0 : p0 + chunk]
                    if fold_z and oz == 1:
                        dz = 1.0 - jnp.abs(dz)
                    radial_terms(dx, dy, dz, levels, center, p0, phi.at[ox], col, slots)
        rows = feat_ref[x + ox, z, pl.ds(y, 3)].reshape(3 * near_z * slots, feat)
        part = jnp.dot(phi[ox], rows, preferred_element_type=jnp.float32)
        if ox == 0:
            acc[...] = part
        elif ox == 1:
            acc[...] += part
    total = jnp.zeros((slots, feat), jnp.float32)
    for b in range(levels):
        both = acc[b * slots : (b + 1) * slots] + part[b * slots : (b + 1) * slots]
        total = total + both * wb_ref[b : b + 1]
    out_ref[0] = total.astype(jnp.bfloat16)


def basis_kernel(pos_ref, wave_ref, feat_ref, basis_ref, struct_ref):
    cell = pl.program_id(0)
    waves = wave_ref.shape[0]
    pos = pos_ref[0]
    chunk = 64
    for w0 in range(0, waves, chunk):
        wv = wave_ref[w0 : w0 + chunk]
        turns = wv[:, 0:1] * pos[0:1] + wv[:, 1:2] * pos[1:2] + wv[:, 2:3] * pos[2:3]
        u = turns - jnp.floor(turns + 0.5)
        q = u * u
        s = u * poly(q, SIN_C)
        c = poly(q, COS_C)
        basis_ref[0, w0 : w0 + chunk] = (1.0 - 2.0 * s * s).astype(jnp.bfloat16)
        basis_ref[0, waves + w0 : waves + w0 + chunk] = (2.0 * s * c).astype(jnp.bfloat16)
    part = jnp.dot(basis_ref[0], feat_ref[0], preferred_element_type=jnp.float32)

    @pl.when(cell == 0)
    def _():
        struct_ref[...] = part

    @pl.when(cell > 0)
    def _():
        struct_ref[...] += part


def final_kernel(basis_ref, grid_ref, msg_ref, feat_ref, home_ref, wm_ref, wo_ref, out_ref):
    far = lax.dot_general(
        basis_ref[0], grid_ref[...], (((0,), (0,)), ((), ())), preferred_element_type=jnp.float32
    )
    joined = far + jnp.dot(msg_ref[0], wm_ref[...], preferred_element_type=jnp.float32)
    hidden = (joined / (1.0 + jnp.exp(-joined))).astype(jnp.bfloat16)
    result = feat_ref[0].astype(jnp.float32) + jnp.dot(hidden, wo_ref[...], preferred_element_type=jnp.float32)
    out_ref[0] = (result * home_ref[0, :, 3:4]).astype(jnp.bfloat16)


def coords(index, counts):
    return (index // (counts[1] * counts[2]), (index // counts[2]) % counts[1], index % counts[2])


def layer_kernel(
    counts,
    levels,
    feat_in,
    frac_in,
    occ_in,
    index_in,
    radial_in,
    mix_in,
    we_in,
    wm_in,
    wo_in,
    out_ref,
    feat_ref,
    frac_ref,
    occ_ref,
    index_ref,
    radial_ref,
    mix_ref,
    we_ref,
    wm_ref,
    wo_ref,
    in_sem,
    wide,
    geom,
    rows_sc,
    pos_sc,
    out_mask,
    turn_cols,
    wb,
    hb,
    phi,
    msg,
    basis,
    basis_t,
    joined,
    struct,
    pair,
    chip_sum,
    parts,
    lines,
    field,
    token,
    halo_send,
    halo_recv,
    side_send,
    side_recv,
    pair_send,
    pair_recv,
    part_send,
    part_recv,
    line_send,
    line_recv,
    share_send,
    share_recv,
):
    cx, cy, slots, feat = feat_ref.shape
    cells = cx * cy
    waves = index_ref.shape[1]
    heads = radial_ref.shape[0]
    devices = counts[0] * counts[1] * counts[2]
    grid = (counts[0] * cx, counts[1] * cy, counts[2])
    rows = waves // devices
    at = (lax.axis_index("gx"), lax.axis_index("gy"), lax.axis_index("gz"))
    core = at[2]
    nx, ny = counts[0], counts[1]
    mesh_id = pl.DeviceIdType.MESH
    pad = geom.shape[3]
    reach = 2.0 * sharpness / (levels - 1) * math.log2(math.e)
    partner = (at[0], at[1], 1 - core)
    line_near = (at[0] + nx - 1) // nx + (2 * nx - 2 - at[0]) // nx
    bits = [1 << n for n in range(ny.bit_length() - 1)]

    def over_x(k):
        return ((at[0] + k + nx) % nx, at[1], core)

    def over_y(k):
        return (at[0], (at[1] + k + ny) % ny, core)

    def to_partner(src, dst, send, recv):
        return pltpu.make_async_remote_copy(
            src_ref=src, dst_ref=dst, send_sem=send, recv_sem=recv, device_id=partner, device_id_type=mesh_id
        )

    sources = [frac_in, occ_in, index_in, radial_in, feat_in, mix_in, we_in, wm_in, wo_in]
    places = [frac_ref, occ_ref, index_ref, radial_ref, feat_ref, mix_ref, we_ref, wm_ref, wo_ref]
    loads = [pltpu.make_async_copy(src, dst, in_sem.at[n]) for n, (src, dst) in enumerate(zip(sources, places))]
    for load in loads:
        load.start()

    barrier = pltpu.get_barrier_semaphore()

    def greet_line(sem):
        @pl.when(at[0] > 0)
        def _():
            pl.semaphore_signal(sem, inc=1, device_id=over_x(-1), device_id_type=mesh_id)

        @pl.when(at[0] < nx - 1)
        def _():
            pl.semaphore_signal(sem, inc=1, device_id=over_x(1), device_id_type=mesh_id)

    def greet_near(sem):
        greet_line(sem)
        for bit in bits:
            step = bit * (1 - 2 * (at[1] // bit % 2))
            pl.semaphore_signal(sem, inc=1, device_id=over_y(step), device_id_type=mesh_id)

    pl.semaphore_signal(barrier, inc=1, device_id=partner, device_id_type=mesh_id)
    greet_near(barrier)

    loads[0].wait()
    loads[1].wait()
    rows_sc[...] = jnp.zeros_like(rows_sc)
    for x in range(cx):
        for a in range(3):
            k = (x * 3 + a) * cy
            rows_sc[k : k + cy] = frac_ref[x, a].astype(jnp.float32)
    rows_sc[3 * cells : 4 * cells] = occ_ref[...].astype(jnp.float32)
    turned = rows_sc[...].T
    for x in range(cx):
        for y in range(cy):
            k = 3 * cells + x * cy + y
            out_mask[x * cy + y] = jnp.broadcast_to(turned[:, k : k + 1], (slots, feat))
    loads[4].wait()
    for x in range(cx):
        for y in range(cy):
            cell = x * cy + y
            ks = [(x * 3 + a) * cy + y for a in range(3)]
            wide[1 + x, 1 + y, 0] = feat_ref[x, y] * out_mask[cell].astype(jnp.bfloat16)
            own = jnp.concatenate([rows_sc[k : k + 1] for k in ks] + [jnp.zeros((pad - 3, slots), jnp.float32)])
            geom[1 + x, 1 + y, 0] = own.astype(jnp.bfloat16)

    class Both:
        def __init__(self, copies):
            self.copies = copies

        def start(self):
            for copy in self.copies:
                copy.start()

        def wait(self):
            for copy in self.copies:
                copy.wait()

        def wait_send(self):
            for copy in self.copies:
                copy.wait_send()

        def wait_recv(self):
            for copy in self.copies:
                copy.wait_recv()

    halo, side = {}, {}

    def link(key, device, source, target):
        n = len(side)
        refs = list(enumerate((geom, wide)))
        side[key] = Both(
            [to_partner(r.at[(*target, 0)], r.at[(*target, 1)], side_send.at[n, i], side_recv.at[n, i]) for i, r in refs]
        )
        if device is not None:
            halo[key] = Both(
                [
                    pltpu.make_async_remote_copy(
                        src_ref=r.at[(*source, 0)],
                        dst_ref=r.at[(*target, 0)],
                        send_sem=halo_send.at[n, i],
                        recv_sem=halo_recv.at[n, i],
                        device_id=device,
                        device_id_type=mesh_id,
                    )
                    for i, r in refs
                ]
            )

    one = lambda start: pl.ds(start, 1)
    for dy in (1, -1):
        xs = pl.ds(1, cx)
        link((0, dy), over_y(dy), (xs, one(cy if dy == 1 else 1)), (xs, one(0 if dy == 1 else cy + 1)))
    for dx in (1, -1):
        sx, tx = one(cx if dx == 1 else 1), one(0 if dx == 1 else cx + 1)
        for name, ys in (("low", one(1)), ("high", one(cy)), ("middle", pl.ds(2, cy - 2))):
            link((dx, name), over_x(dx), (sx, ys), (tx, ys))
        for dy in (1, -1):
            link((dx, dy), over_y(dy), (tx, one(cy if dy == 1 else 1)), (tx, one(0 if dy == 1 else cy + 1)))
    link((0, 0), None, None, (pl.ds(1, cx), pl.ds(1, cy)))

    def send_face(step):
        for name in ("low", "high", "middle"):
            halo[step, name].start()

    def send_faces(direct):
        for step, inside in ((1, at[0] < nx - 1), (-1, at[0] > 0)):
            pl.when(inside if direct else jnp.logical_not(inside))(functools.partial(send_face, step))

    def send_rows(direct):
        for step, near in ((1, at[1] % 2 == 0), (-1, at[1] % 2 == 1)):
            pl.when(near if direct else jnp.logical_not(near))(halo[0, step].start)

    def pass_token():
        pl.semaphore_wait(token.at[0], line_near + len(bits))
        greet_line(token.at[1])
        send_rows(False)

    def open_wrap():
        pl.semaphore_wait(token.at[1], line_near)
        send_faces(False)

    loads[2].wait()
    for w0 in range(0, waves, 128):
        part = [index_ref[a : a + 1, w0 : w0 + 128].astype(jnp.float32) * (1.0 / grid[a]) for a in range(3)]
        part = jnp.concatenate(part + [jnp.zeros((5, 128), jnp.float32)])
        turn_cols[w0 : w0 + 128] = part.T
    for x in range(cx):
        for y in range(cy):
            start = [at[0] * cx + x, at[1] * cy + y, core]
            cell = x * cy + y
            for a in range(3):
                k = (x * 3 + a) * cy + y
                pos_sc[a : a + 1, cell * slots : (cell + 1) * slots] = rows_sc[k : k + 1] + start[a].astype(jnp.float32)

    loads[3].wait()
    for x in range(cx):
        for y in range(cy):
            for a in range(3):
                k = (x * 3 + a) * cy + y
                hb[x * cy + y, a] = jnp.broadcast_to(turned[:, k : k + 1] * reach, (slots, slots))
    owner = lax.broadcasted_iota(jnp.int32, (heads, feat), 1) // (feat // heads)
    mine = owner == lax.broadcasted_iota(jnp.int32, (heads, feat), 0)
    for b in range(levels):
        level = b / (levels - 1)
        scale = math.exp(-sharpness * level * level) / math.sqrt(4.0 * slots) / reach**4
        column = jnp.broadcast_to(radial_ref[:, b : b + 1], (heads, feat)) * scale
        wb[b : b + 1] = jnp.sum(jnp.where(mine, column, 0.0), axis=0, keepdims=True)

    pl.semaphore_wait(barrier, 1 + line_near + len(bits))
    greet_near(token.at[0])
    side[0, 0].start()
    send_rows(True)
    send_faces(True)

    @pl.loop(0, cells // 2)
    def _(two):
        pl.when(two == cells // 8)(pass_token)
        pl.when(two == cells // 4 + 1)(open_wrap)
        lanes = pl.ds(pl.multiple_of(two * 2 * slots, 2 * slots), 2 * slots)
        pos = pos_sc[:, lanes]
        chunk = 32
        for w0 in range(0, waves, chunk):
            wv = turn_cols[w0 : w0 + chunk]
            turns = wv[:, 0:1] * pos[0:1] + wv[:, 1:2] * pos[1:2] + wv[:, 2:3] * pos[2:3]
            u = turns - jnp.round(turns)
            q = u * u
            s = u * poly(q, [v * math.sqrt(2.0) for v in SIN_P])
            c = poly(q, [v * math.sqrt(2.0) for v in COS_P])
            basis[w0 : w0 + chunk, lanes] = (1.0 - s * s).astype(jnp.bfloat16)
            basis[waves + w0 : waves + w0 + chunk, lanes] = (s * c).astype(jnp.bfloat16)

    atoms = wide[1 : 1 + cx, 1 : 1 + cy, 0].reshape(cells * slots, feat)
    struct[...] = (
        jnp.dot(basis[...], atoms, preferred_element_type=jnp.float32)
        .astype(jnp.bfloat16)
        .reshape(struct.shape)
    )
    swap = to_partner(struct.at[:, 1 - core], pair, pair_send.at[0], pair_recv.at[0])
    swap.start()

    for load in loads[5:]:
        load.wait()
    msg[...] = jnp.zeros_like(msg)

    def part_copy(k):
        return pltpu.make_async_remote_copy(
            src_ref=chip_sum.at[:, :, (at[1] + k) % ny],
            dst_ref=parts.at[k],
            send_sem=part_send.at[k],
            recv_sem=part_recv.at[k],
            device_id=over_y(k),
            device_id_type=mesh_id,
        )

    def line_copy(k, slot):
        return pltpu.make_async_remote_copy(
            src_ref=lines.at[at[0]],
            dst_ref=lines.at[slot],
            send_sem=line_send.at[k],
            recv_sem=line_recv.at[k],
            device_id=over_x(k),
            device_id_type=mesh_id,
        )

    def share_copy(k, slot):
        return pltpu.make_async_remote_copy(
            src_ref=field.at[:, core, :, at[1]],
            dst_ref=field.at[:, core, :, slot],
            send_sem=share_send.at[k],
            recv_sem=share_recv.at[k],
            device_id=over_y(k),
            device_id_type=mesh_id,
        )

    def field_copy(half, k):
        mine = field.at[:, half, :, (at[1] - k + ny) % ny]
        return to_partner(mine, mine, pair_send.at[1 + k], pair_recv.at[1 + k])

    def sum_pair():
        swap.wait()
        both = struct[:, core].astype(jnp.float32) + pair[...].astype(jnp.float32)
        chip_sum[...] = both.astype(jnp.bfloat16)
        for k in range(1, ny):
            part_copy(k).start()

    def sum_parts():
        for k in range(1, ny):
            part_copy(k).wait()
        parts[0] = chip_sum[:, :, at[1]]
        lines[at[0]] = jnp.sum(parts[...].astype(jnp.float32), axis=0).astype(jnp.bfloat16)
        for k in range(1, nx):
            line_copy(k, at[0]).start()

    def filter_share():
        for k in range(1, nx):
            line_copy(k, (at[0] - k + nx) % nx).wait()
        total = jnp.sum(lines[...].astype(jnp.float32), axis=0).reshape(2 * nx * rows, feat)
        mixed = jnp.dot(total, mix_ref[...], precision=lax.Precision.HIGHEST, preferred_element_type=jnp.float32)
        vec = [turn_cols[pl.ds(((core * nx + x) * ny + at[1]) * rows, rows)] for x in range(nx)]
        vec = jnp.concatenate(vec) * (2.0 * math.pi)
        square = jnp.sum(vec * vec, axis=1, keepdims=True)
        damp = strength * jnp.exp(-0.5 * smearing * square) / (square + screening)
        damp = damp * (1.0 / math.sqrt(cells * slots * devices * waves))
        filtered = (mixed * jnp.concatenate([damp, damp])).astype(jnp.bfloat16)
        projected = jnp.dot(filtered, we_ref[...], preferred_element_type=jnp.float32)
        field[:, core, :, at[1]] = projected.astype(jnp.bfloat16).reshape(2, nx, rows, feat)
        for k in range(1, ny):
            share_copy(k, at[1]).start()
        field_copy(core, 0).start()

    def join_field():
        for k in range(1, ny):
            share_copy(k, (at[1] - k + ny) % ny).wait()
            field_copy(core, k).start()

    first_x = 1 - (at[0] + nx - 1) // nx

    def place(slot, j):
        late = j // (2 * cy)
        i = j % (2 * cy)
        turn = i // (cy // 2)
        x = (1 - late) * slot + late * (turn + (1 - 2 * turn) * first_x)
        y = ((1 - late) * (i // 2) + late * (2 * (i % (cy // 2)) + slot) + 1) % cy
        xi = (1 - late) * (1 + i % 2) + late * x * (cx + 1)
        return x, y, xi

    def weigh(slot, j):
        x, y, xi = place(slot, j)
        cell = x * cy + y
        step = xi - (x + 1)
        chunk = 32
        done = []
        for oy in range(3):
            near = [
                geom[xi, y + oy, oz].astype(jnp.float32) * reach for oz in range(2)
            ]
            near = jnp.concatenate(near, axis=1)
            nx = near[0:1] + step.astype(jnp.float32) * reach
            ny = near[1:2] + (oy - 1.0) * reach
            nz = near[2:3]
            for p0 in range(0, slots, chunk):
                row = nx
                if len(done) >= 1:
                    o, p = done[-1]
                    row = jnp.concatenate([nx[:, :slots] + jnp.minimum(phi[slot, o, p + 7 * slots : p + 7 * slots + 8, :slots].astype(jnp.float32)[0:1], 0.0), nx[:, slots:]], axis=1)
                done.append((oy, p0))
                gx, gy, gz = (
                    n - jnp.concatenate([hb[cell, a, p0 : p0 + chunk]] * 2, axis=1) for a, n in enumerate((row, ny, nz))
                )
                gz = jnp.concatenate([gz[:, :slots], reach - jnp.abs(gz[:, slots:])], axis=1)
                diagonal = p0 + step * slots if oy == 1 else None
                radial_chain(gx, gy, gz, levels, reach, diagonal, p0, phi.at[slot, oy], slots)

    def gather(slot, j):
        x, y, xi = place(slot, j)
        near = wide[xi, pl.ds(y, 3)].reshape(6 * slots, feat)
        left = jnp.concatenate([phi[slot, oy] for oy in range(3)], axis=1)
        part = jnp.dot(left, near, preferred_element_type=jnp.float32)
        total = msg[x * cy + y]
        for b in range(levels):
            total = total + part[b * slots : (b + 1) * slots] * wb[b : b + 1]
        msg[x * cy + y] = total

    def halo_in(*keys):
        for key in keys:
            halo[key].wait_recv()
            side[key].start()

    def side_in(*keys):
        for key in keys:
            side[key].wait()

    def face_in(step):
        halo_in((step, "low"))
        halo[step, -1].start()
        halo_in((step, "high"))
        halo[step, 1].start()

    def rest_in(step):
        halo_in((step, "middle"))

    def face_done(step):
        side_in((step, "low"), (step, "high"), (step, "middle"))

    def corners_in(step):
        halo_in((step, -1), (step, 1))

    def corners_done(step):
        side_in((step, -1), (step, 1))

    def on_side(first, what):
        def run():
            for step, then in ((1, first_x == 0), (-1, first_x == 1)):
                pl.when(then if first else jnp.logical_not(then))(functools.partial(what, step))

        return run

    side_in((0, 0))
    weigh(0, jnp.int32(0))

    ends = 2 * cy - 4
    last = 3 * cy
    events = [
        (1, sum_pair),
        (ends - 3, lambda: halo_in((0, -1), (0, 1))),
        (ends - 2, on_side(True, face_in)),
        (ends - 1, lambda: side_in((0, -1))),
        (ends - 1, on_side(True, rest_in)),
        (ends, sum_parts),
        (ends + 1, lambda: side_in((0, 1))),
        (ends + 1, on_side(True, corners_in)),
        (ends + 2, on_side(False, face_in)),
        (ends + 3, on_side(True, face_done)),
        (last - 4, on_side(True, corners_done)),
        (last - 4, on_side(False, rest_in)),
        (last - 3, filter_share),
        (last - 3, on_side(False, corners_in)),
        (last - 3, on_side(False, face_done)),
        (last - 2, on_side(False, corners_done)),
    ]

    def run_all(due):
        for what in due:
            what()

    @pl.loop(0, 3 * cy)
    def _(j):
        for third in range(3):

            @pl.when(j // cy == third)
            def _():
                for k in range(third * cy, (third + 1) * cy):
                    due = [what for when, what in events if when == k]
                    if due:
                        pl.when(j == k)(functools.partial(run_all, due))

        cell = j % cells
        basis_t[cell] = basis[:, pl.ds(pl.multiple_of(cell * slots, slots), slots)].T
        weigh(1, j)
        gather(0, j)
        weigh(0, (j + 1) % last)
        gather(1, j)

    for copy in halo.values():
        copy.wait_send()

    half = waves // 2
    two = 2 * slots

    def far_of(pair_of_cells, half_of):
        c0 = pair_of_cells * 2
        first = pl.multiple_of(half_of * half, half)
        left = jnp.concatenate([basis_t[pl.ds(c0, 2), :, pl.ds(k * waves + first, half)] for k in range(2)], axis=2)
        right = field[:, half_of].reshape(waves, feat)
        return jnp.dot(left.reshape(two, waves), right, preferred_element_type=jnp.float32)

    @pl.loop(0, cells // 2, unroll=True)
    def _(n):
        near = msg[pl.ds(2 * n, 2)].reshape(two, feat).astype(jnp.bfloat16)
        joined[n] = jnp.dot(near, wm_ref[...], preferred_element_type=jnp.float32)

    join_field()

    @pl.loop(0, cells // 2, unroll=True)
    def _(n):
        joined[n] += far_of(n, core)

    for k in range(ny):
        field_copy(core, k).wait_send()
        field_copy(1 - core, k).wait_recv()

    @pl.loop(0, cells // 2, unroll=True)
    def _(n):
        total = joined[n] + far_of(n, 1 - core)
        hidden = (total / (1.0 + jnp.exp(-total))).astype(jnp.bfloat16)
        result = jnp.dot(hidden, wo_ref[...], preferred_element_type=jnp.float32).reshape(2, slots, feat)
        c0 = 2 * n
        atom = wide[1 + c0 // cy, pl.ds(1 + c0 % cy, 2), 0].astype(jnp.float32)
        out_ref[pl.ds(c0, 2)] = (atom + result * out_mask[pl.ds(c0, 2)]).astype(jnp.bfloat16)


def radial_chain(gx, gy, gz, levels, reach, diagonal, p0, phi, slots):
    rows = gx.shape[0]
    sq = jnp.minimum(gx * gx + gy * gy + gz * gz, reach * reach)
    ratio = jnp.exp2(sq * lax.rsqrt(jnp.maximum(sq, 1e-30)))
    edge = reach * reach - sq
    val = edge * edge * jnp.exp2(sq * (-sharpness * math.log2(math.e) / reach**2))
    if diagonal is not None:
        row = lax.broadcasted_iota(jnp.int32, (rows, slots), 0) + diagonal
        lane = lax.broadcasted_iota(jnp.int32, (rows, slots), 1)
        val = jnp.concatenate([jnp.where(row == lane, 0.0, val[:, :slots]), val[:, slots:]], axis=1)
    second = ratio * ratio
    steps = [val.astype(jnp.bfloat16), (val * ratio).astype(jnp.bfloat16)]
    fourth = (second * second).astype(jnp.bfloat16)
    second = second.astype(jnp.bfloat16)
    for b in range(2, levels):
        steps.append(steps[b - 2] * second if b < 4 else steps[b - 4] * fourth)
    for b in range(levels):
        phi[b * slots + p0 : b * slots + p0 + rows] = steps[b]


def radial_terms(gx, gy, gz, levels, center, p0, phi, col, slots):
    rows = gx.shape[0]
    sq = jnp.minimum(gx * gx + gy * gy + gz * gz, 1.0)
    dist = sq * lax.rsqrt(jnp.maximum(sq, 1e-30))
    ratio = jnp.exp2(dist * (2.0 * sharpness / (levels - 1) * math.log2(math.e)))
    edge = 1.0 - sq
    val = edge * edge * jnp.exp2(sq * (-sharpness * math.log2(math.e)))
    if center:
        row = lax.broadcasted_iota(jnp.int32, val.shape, 0) + p0
        lane = lax.broadcasted_iota(jnp.int32, val.shape, 1)
        val = jnp.where(row == lane, 0.0, val)
    for b in range(levels):
        phi[b * slots + p0 : b * slots + p0 + rows, col : col + slots] = val.astype(jnp.bfloat16)
        if b + 1 < levels:
            val = val * ratio


def body(
    features,
    fractions,
    occupied,
    wave_index,
    radial_weight,
    ewald_mix,
    msg_weight,
    ewald_weight,
    out_weight,
):
    cx, cy, cz, slots, feat = features.shape
    levels, heads = radial_weight.shape
    cells = cx * cy * cz
    grid = [lax.axis_size("gx") * cx, lax.axis_size("gy") * cy, lax.axis_size("gz") * cz]
    devices = lax.axis_size("gx") * lax.axis_size("gy") * lax.axis_size("gz")
    waves = wave_index.shape[1]
    axes = ("gx", "gy", "gz")
    full = lambda shape: pl.BlockSpec(shape, lambda i: (0,) * len(shape))
    params = pltpu.CompilerParams(dimension_semantics=("arbitrary",), vmem_limit_bytes=56 * 2**20)

    fold_z = grid[2] == 2 and cz == 1
    counts = tuple(lax.axis_size(n) for n in axes)
    rows = waves // devices
    nx, ny = counts[:2]
    known = 2 < nx < 5 and ny == 4 and waves % 512 == 0 and cy % 2 == 0
    if fold_z and known and rows % 16 == 0 and ny > 2 and cx == 2 and cy > 2 and 4 * cells <= slots == 128:
        vmem = pl.BlockSpec(memory_space=pltpu.VMEM)
        dma = pltpu.SemaphoreType.DMA
        out = pl.pallas_call(
            functools.partial(layer_kernel, counts, levels),
            in_specs=[pl.BlockSpec(memory_space=pl.ANY)] * 9,
            out_specs=vmem,
            out_shape=pltpu.VMEM((cells, slots, feat), jnp.bfloat16),
            scratch_shapes=[
                pltpu.VMEM((cx, cy, slots, feat), jnp.bfloat16),
                pltpu.VMEM((cx, 3, cy, slots), jnp.bfloat16),
                pltpu.VMEM((cells, slots), jnp.int32),
                pltpu.VMEM(wave_index.shape, jnp.int32),
                pltpu.VMEM((heads, levels), jnp.float32),
                pltpu.VMEM(ewald_mix.shape, jnp.float32),
                pltpu.VMEM(ewald_weight.shape, jnp.bfloat16),
                pltpu.VMEM(msg_weight.shape, jnp.bfloat16),
                pltpu.VMEM(out_weight.shape, jnp.bfloat16),
                dma((9,)),
                pltpu.VMEM((cx + 2, cy + 2, 2, slots, feat), jnp.bfloat16),
                pltpu.VMEM((cx + 2, cy + 2, 2, 8, slots), jnp.bfloat16),
                pltpu.VMEM((slots, slots), jnp.float32),
                pltpu.VMEM((3, cells * slots), jnp.float32),
                pltpu.VMEM((cells, slots, feat), jnp.float32),
                pltpu.VMEM((waves, 8), jnp.float32),
                pltpu.VMEM((levels, feat), jnp.float32),
                pltpu.VMEM((cells, 3, slots, slots), jnp.float32),
                pltpu.VMEM((2, 3, levels * slots, 2 * slots), jnp.bfloat16),
                pltpu.VMEM((cells, slots, feat), jnp.float32),
                pltpu.VMEM((2 * waves, cells * slots), jnp.bfloat16),
                pltpu.VMEM((cells, slots, 2 * waves), jnp.bfloat16),
                pltpu.VMEM((cells // 2, 2 * slots, feat), jnp.float32),
                pltpu.VMEM((2, 2, nx, ny, rows, feat), jnp.bfloat16),
                pltpu.VMEM((2, nx, ny, rows, feat), jnp.bfloat16),
                pltpu.VMEM((2, nx, ny, rows, feat), jnp.bfloat16),
                pltpu.VMEM((ny, 2, nx, rows, feat), jnp.bfloat16),
                pltpu.VMEM((nx, 2, nx, rows, feat), jnp.bfloat16),
                pltpu.VMEM((2, 2, nx, ny, rows, feat), jnp.bfloat16),
                pltpu.SemaphoreType.REGULAR((2,)),
                dma((13, 2)),
                dma((13, 2)),
                dma((13, 2)),
                dma((13, 2)),
                dma((1 + ny,)),
                dma((1 + ny,)),
                dma((ny,)),
                dma((ny,)),
                dma((nx,)),
                dma((nx,)),
                dma((ny,)),
                dma((ny,)),
            ],
            compiler_params=pltpu.CompilerParams(
                collective_id=0, has_side_effects=True, vmem_limit_bytes=56 * 2**20
            ),
            name="layer",
        )(
            features.reshape(cx, cy, slots, feat),
            fractions.transpose(0, 2, 3, 1, 4).reshape(cx, 3, cy, slots),
            occupied.reshape(cells, slots),
            wave_index,
            radial_weight.T,
            ewald_mix,
            ewald_weight,
            msg_weight,
            out_weight,
        )
        return out.reshape(features.shape)

    masked = features * occupied[..., None].astype(jnp.bfloat16)
    frac = fractions.astype(jnp.float32)
    cell_feat = masked.reshape(cells, slots, feat)
    home = jnp.concatenate([frac, occupied[:, :, :, None, :].astype(jnp.float32)], axis=3)
    home = jnp.swapaxes(home.reshape(cells, 4, slots), 1, 2)

    start = [
        (lax.axis_index(n) * c + jnp.arange(c, dtype=jnp.int32)).astype(jnp.float32)
        for n, c in zip(axes, (cx, cy, cz))
    ]
    origin = jnp.stack(jnp.meshgrid(*start, indexing="ij"), axis=-1)[..., None]
    pos = (origin + frac).reshape(cells, 3, slots)
    lengths = jnp.array(grid, jnp.float32)
    index = wave_index.astype(jnp.float32)
    wave_vec = 2.0 * math.pi * index / lengths[:, None]
    wave_sq = jnp.sum(wave_vec * wave_vec, axis=0)
    damping = (
        strength
        * jnp.exp(-0.5 * smearing * wave_sq)
        / (wave_sq + screening)
        * (1.0 / math.sqrt(cells * slots * devices * waves))
    )
    wave_turn = (index / lengths[:, None]).T

    level = jnp.arange(levels, dtype=jnp.float32) / (levels - 1)
    wb = radial_weight * (jnp.exp(-sharpness * level * level) / math.sqrt(4.0 * slots))[:, None]
    wb = jnp.repeat(wb, feat // heads, axis=1)
    basis, struct = pl.pallas_call(
        basis_kernel,
        grid=(cells,),
        in_specs=[
            pl.BlockSpec((1, 3, slots), lambda i: (i, 0, 0)),
            full((waves, 3)),
            pl.BlockSpec((1, slots, feat), lambda i: (i, 0, 0)),
        ],
        out_specs=[pl.BlockSpec((1, 2 * waves, slots), lambda i: (i, 0, 0)), full((2 * waves, feat))],
        out_shape=[
            jax.ShapeDtypeStruct((cells, 2 * waves, slots), jnp.bfloat16),
            jax.ShapeDtypeStruct((2 * waves, feat), jnp.float32),
        ],
        compiler_params=params,
        name="basis",
    )(pos, wave_turn, cell_feat)

    wave_share = lax.psum_scatter(struct.reshape(2, waves, feat), axes, scatter_dimension=1, tiled=True)
    share_rows = wave_share.shape[1]
    share_damp = lax.dynamic_slice_in_dim(damping, lax.axis_index(axes) * share_rows, share_rows, 0)
    mixed = jnp.dot(wave_share.reshape(2 * share_rows, feat), ewald_mix, precision=lax.Precision.HIGHEST)
    filtered = (mixed.reshape(2, share_rows, feat) * share_damp[None, :, None]).astype(jnp.bfloat16)
    projected = jnp.dot(filtered, ewald_weight, preferred_element_type=jnp.float32).astype(jnp.bfloat16)
    field = lax.all_gather(projected, axes, axis=1, tiled=True).reshape(2 * waves, feat)

    wide_feat = widen(widen(masked, "gx", 0), "gy", 1)
    wide_geom = widen(widen(fractions, "gx", 0), "gy", 1)
    if fold_z:
        swap = [(0, 1), (1, 0)]
        wide_feat = jnp.concatenate([wide_feat, lax.ppermute(wide_feat, "gz", swap)], axis=2)
        wide_geom = jnp.concatenate([wide_geom, lax.ppermute(wide_geom, "gz", swap)], axis=2)
        near_z = 2
    else:
        wide_feat = widen(wide_feat, "gz", 2)
        wide_geom = widen(wide_geom, "gz", 2)
        near_z = 3
    wide_feat = jnp.stack([wide_feat[:, :, z : z + near_z] for z in range(cz)], axis=1)
    wide_geom = jnp.stack([wide_geom[:, :, z : z + near_z] for z in range(cz)], axis=1).astype(jnp.float32)
    messages = pl.pallas_call(
        functools.partial(message_kernel, cy, cz, fold_z, levels),
        grid=(cells,),
        in_specs=[
            pl.BlockSpec((1, slots, 4), lambda i: (i, 0, 0)),
            full(wide_feat.shape),
            full(wide_geom.shape),
            full(wb.shape),
        ],
        out_specs=pl.BlockSpec((1, slots, feat), lambda i: (i, 0, 0)),
        out_shape=jax.ShapeDtypeStruct((cells, slots, feat), jnp.bfloat16),
        scratch_shapes=[
            pltpu.VMEM((3, slots, slots), jnp.float32),
            pltpu.VMEM((3, levels * slots, 3 * near_z * slots), jnp.bfloat16),
            pltpu.VMEM((levels * slots, feat), jnp.float32),
        ],
        compiler_params=params,
        cost_estimate=pl.CostEstimate(
            flops=2 * cells * levels * slots * 9 * near_z * slots * feat, bytes_accessed=2**22, transcendentals=0
        ),
        name="messages",
    )(home, wide_feat, wide_geom, wb)

    out = pl.pallas_call(
        final_kernel,
        grid=(cells,),
        in_specs=[
            pl.BlockSpec((1, 2 * waves, slots), lambda i: (i, 0, 0)),
            full((2 * waves, feat)),
            pl.BlockSpec((1, slots, feat), lambda i: (i, 0, 0)),
            pl.BlockSpec((1, slots, feat), lambda i: (i, 0, 0)),
            pl.BlockSpec((1, slots, 4), lambda i: (i, 0, 0)),
            full((feat, feat)),
            full((feat, feat)),
        ],
        out_specs=pl.BlockSpec((1, slots, feat), lambda i: (i, 0, 0)),
        out_shape=jax.ShapeDtypeStruct((cells, slots, feat), jnp.bfloat16),
        compiler_params=params,
        name="final",
    )(basis, field, messages, cell_feat, home, msg_weight, out_weight)
    return out.reshape(features.shape)


def solution(mesh):
    cell = P("gx", "gy", "gz", None, None)
    in_specs = (cell, cell, P("gx", "gy", "gz", None), P(), P(), P(), P(), P(), P())
    return jax.shard_map(body, mesh=mesh, in_specs=in_specs, out_specs=cell, check_vma=False)
```
